32 devices in a mesh: grp: 2 (over y), vec: 4 (over z), walk: 2 (over x), orb: 2 (over core).
Axes of the slice: x: 2, y: 2, z: 4, core: 2. Of those that a mesh axis runs over, the one named last changes fastest.
Arguments:
- walkers: bfloat16 [32, 512, 128], P(('grp', 'walk'), 'orb'), parts along dimension 0, may hold values from -3 to 3
- inv_intersection: bfloat16 [32, 128, 128], P(('grp', 'walk')), parts along dimension 0, may hold values from -0.5 to 0.5
- trial: bfloat16 [512, 128], replicated, may hold values from -0.25 to 0.25
- vectors: bfloat16 [32, 512, 512], P('vec', 'orb')
- aux_field: float32 [32, 32], P(('grp', 'walk'), 'vec'), parts along dimension 0, may hold values from -5 to 5
- log_weight: float32 [32], P(('grp', 'walk')), parts along dimension 0, may hold values from -4 to 4
- copy_list: int32 [32], P(('grp', 'walk')), parts along dimension 0, may hold values from 0 to 15
Outputs:
- walkers_out: bfloat16 [32, 512, 128], P(('grp', 'walk'), 'orb'), parts along dimension 0
- weights_out: float32 [32], P(('grp', 'walk')), parts along dimension 0
The draws below stay inside these ranges and needn't reach their ends.
There are 2 independent parts, one for each index of `grp`. The reference program is written for one: setup_inputs(seed, part) draws one part's arguments, and reference() takes and returns one part's arrays. A program takes and returns all parts, laid end to end along the dimension named above; an argument that names none is the same for every part. Nothing has to cross between parts.
Inputs may be any that keep to these rules, and one draw needn't show every extreme that they name: `copy_list`: the walker, within the same ensemble, whose copy fills the slot.
All inputs are finite; a program needn't handle non-finite values.
Results may differ from the reference program's by a relative error of at most 0.008.
Values may be sent and summed in bfloat16 or wider, within the bound.
No kernel may reach another device: no remote copies, remote signals or barrier semaphores. Data moves between devices by JAX's collectives and lax.ppermute only.
A program may use at most 64 MiB of HBM per device.

```python
import math
import jax
import jax.numpy as jnp
import numpy as np
from jax import lax

N = 512
E = 128
ORDER = 6
CHOL = 32
WALKERS = 16


def draw_vectors(key, part):
    base = jax.random.normal(key, (CHOL, N, N), jnp.float32)
    spread = 5.0 / math.sqrt(N * CHOL)
    sym = (base + jnp.swapaxes(base, 1, 2)) * (spread / math.sqrt(2.0))
    return sym.astype(jnp.bfloat16)


def set_ends(drawn, key, smallest, top_value):
    dims = drawn.shape
    index_at = [jax.random.randint(jax.random.fold_in(key, axis), (), 0, dims[axis]) for axis in range(len(dims))]
    drawn = drawn.at[tuple(index_at)].set(smallest)
    longest = dims.index(max(dims))
    index_at[longest] = (index_at[longest] + 1) % dims[longest]
    return drawn.at[tuple(index_at)].set(top_value)


def steps_of(own_key, shape, shards, smallest, high):
    level, own = 1.0, jax.random.fold_in(own_key, 6)
    for position, parts in shards:
        heights = jnp.exp(jax.random.uniform(jax.random.fold_in(own, position), (parts,), jnp.float32, smallest / len(shards), high / len(shards)))
        level = level * jnp.repeat(heights, shape[position] // parts).reshape([-1 if axis == position else 1 for axis in range(len(shape))])
    return level


def rank_bounds(count, slope):
    loads = [(1 << 20) // math.isqrt(grade ** slope) + 1 for grade in range(1, count + 1)]
    width = 1 + sum(loads) // (1 << 30)
    return np.cumsum(np.array([max(1, weight // width) for weight in loads]))


def ranked_ids(own_key, shape, count, slope):
    table = rank_bounds(count, slope)
    pick = jax.random.randint(jax.random.fold_in(own_key, 1), shape, 0, int(table[count - 1]))
    rank = jnp.searchsorted(jnp.asarray(table, jnp.int32), pick, side="right")
    return jax.random.permutation(jax.random.fold_in(own_key, 2), count)[rank].astype(jnp.int32)


def gaussian(own_key, extent, scale, reach, pieces=(), kind=jnp.bfloat16):
    factor_of = steps_of(own_key, extent, pieces, -0.22, 0.18) if pieces else 1.0
    array = jax.random.normal(own_key, extent, jnp.float32) * scale * factor_of
    return jnp.minimum(jnp.maximum(array, -reach), reach).astype(kind)


def setup_inputs(seed: int = 0, part: int = 0) -> dict:
    streams_of = jax.random.split(jax.random.key(seed), 8)
    own_keys = jax.random.split(jax.random.fold_in(streams_of[7], part), 8)
    return {
        "walkers": gaussian(own_keys[0], (WALKERS, N, E), 0.5, 3.0, ((0, 2), (1, 2))),
        "inv_intersection": gaussian(own_keys[1], (WALKERS, E, E), E ** -0.5, 0.5, ((0, 2),)),
        "trial": gaussian(streams_of[2], (N, E), N ** -0.5, 0.25),
        "vectors": draw_vectors(jax.random.fold_in(streams_of[7], 71), part),
        "aux_field": gaussian(own_keys[4], (WALKERS, CHOL), 1.0, 5.0, ((0, 2), (1, 4)), jnp.float32),
        "log_weight": gaussian(own_keys[5], (WALKERS,), 1.0, 4.0, ((0, 2),), jnp.float32),
        "copy_list": set_ends(ranked_ids(own_keys[6], (WALKERS,), WALKERS, 2), jax.random.fold_in(own_keys[6], 3), 0, WALKERS - 1).astype(jnp.int32),
    }


step_root = math.sqrt(0.08)

def reference(walkers, inv_intersection, trial, vectors, aux_field, log_weight, copy_list):
    high = lax.Precision.HIGHEST
    green = jnp.einsum('wne,wef->wnf', walkers.astype(jnp.float32), inv_intersection.astype(jnp.float32), precision=high).astype(jnp.bfloat16)
    mixed = jnp.einsum('gnm,me->gne', vectors.astype(jnp.float32), trial.astype(jnp.float32), precision=high).astype(jnp.bfloat16)
    bias = jnp.einsum('wne,gne->wg', green.astype(jnp.float32), mixed.astype(jnp.float32), precision=high)
    shift = -step_root * bias
    field = aux_field - shift
    new_log = log_weight + lax.optimization_barrier(jnp.sum(aux_field * shift - 0.5 * shift * shift, axis=1))
    weighted = (field * step_root).astype(jnp.bfloat16)
    operator = jnp.einsum('wg,gnm->wnm', weighted.astype(jnp.float32), vectors.astype(jnp.float32), precision=high).astype(jnp.bfloat16)
    operand = operator.astype(jnp.float32)
    term = walkers
    total = walkers.astype(jnp.float32)
    for degree in range(1, ORDER + 1):
        product = jnp.einsum('wnm,wme->wne', operand, term.astype(jnp.float32), precision=high)
        term = (product / degree).astype(jnp.bfloat16)
        total = total + term.astype(jnp.float32)
    propagated = total.astype(jnp.bfloat16)
    return (propagated[copy_list], new_log[copy_list])
```

```python
from functools import partial
import math

import jax
import jax.numpy as jnp
from jax import lax
from jax.experimental import pallas as pl
from jax.experimental.pallas import tpu as pltpu
from jax.sharding import PartitionSpec as P

ORDER = 6
LANE = 128

step_root = math.sqrt(0.08)

VMEM = pltpu.VMEM
SMEM = pltpu.SMEM


def in_vmem():
    return pl.BlockSpec(memory_space=VMEM)


def in_smem():
    return pl.BlockSpec(memory_space=SMEM)


def in_any():
    return pl.BlockSpec(memory_space=pl.ANY)


def mm(a, b):
    return jnp.dot(a, b, preferred_element_type=jnp.float32)


def fold_rows(operator, carry, piece, start):
    return jnp.einsum("wnm,wme->wne", operator, piece, preferred_element_type=jnp.float32)


def general_device(walkers, inv_intersection, trial, vectors, aux_field, log_weight, copy_list):
    green = jnp.einsum(
        "wne,wef->wnf", walkers, inv_intersection, preferred_element_type=jnp.float32
    ).astype(jnp.bfloat16)
    mixed = jnp.einsum("gnm,me->gne", vectors, trial, preferred_element_type=jnp.float32).astype(
        jnp.bfloat16
    )
    partial_bias = jnp.einsum("wne,gne->wg", green, mixed, preferred_element_type=jnp.float32)
    bias = lax.psum(partial_bias, "orb")
    shift = -step_root * bias
    field = aux_field - shift
    own_factor = jnp.sum(aux_field * shift - 0.5 * shift * shift, axis=1)
    new_log = log_weight + lax.psum(own_factor, "vec")
    weighted = (field * step_root).astype(jnp.bfloat16)
    local_operator = jnp.einsum(
        "wg,gnm->wnm", weighted, vectors, preferred_element_type=jnp.float32
    )
    operator = lax.psum(local_operator, "vec").astype(jnp.bfloat16)
    running = walkers.astype(jnp.float32)
    folder = partial(fold_rows, operator)
    operand = walkers
    for degree in range(1, ORDER + 1):
        initial = jnp.zeros(running.shape, jnp.float32)
        summed = folder(initial, lax.all_gather(operand, "orb", axis=1, tiled=True), jnp.int32(0))
        new_term = (summed / degree).astype(jnp.bfloat16)
        running = running + new_term.astype(jnp.float32)
        if degree < ORDER:
            operand = new_term
    propagated = running.astype(jnp.bfloat16)
    every_walker = lax.all_gather(propagated, "walk", axis=0, tiled=True)
    every_log = lax.all_gather(new_log, "walk", axis=0, tiled=True)
    return (every_walker[copy_list], every_log[copy_list])


def bias_kernel(walkers_hbm, inv_hbm, trial_hbm, vec_hbm, out_ref,
                walkers_ref, inv_ref, trial_ref, vec_ref, green_ref, sems):
    n_walk = walkers_hbm.shape[0]
    n_vec = vec_hbm.shape[0]
    copies = [
        pltpu.make_async_copy(walkers_hbm, walkers_ref, sems.at[0]),
        pltpu.make_async_copy(inv_hbm, inv_ref, sems.at[1]),
        pltpu.make_async_copy(trial_hbm, trial_ref, sems.at[2]),
    ]
    vec_copies = [
        pltpu.make_async_copy(vec_hbm.at[g], vec_ref.at[g], sems.at[3 + g]) for g in range(n_vec)
    ]
    for copy in copies + vec_copies:
        copy.start()
    copies[0].wait()
    copies[1].wait()
    for w in range(n_walk):
        green_ref[w] = mm(walkers_ref[w], inv_ref[w]).astype(jnp.bfloat16).astype(jnp.float32)
    copies[2].wait()
    trial = trial_ref[...]
    lane = lax.broadcasted_iota(jnp.int32, (n_walk, n_vec), 1)
    total = jnp.zeros((n_walk, n_vec), jnp.float32)
    for g in range(n_vec):
        vec_copies[g].wait()
        mixed = mm(vec_ref[g], trial).astype(jnp.bfloat16).astype(jnp.float32)
        rows = [jnp.sum(green_ref[w] * mixed, axis=0, keepdims=True) for w in range(n_walk)]
        column = jnp.sum(jnp.concatenate(rows, axis=0), axis=1, keepdims=True)
        total = total + jnp.where(lane == g, column, 0.0)
    out_ref[...] = total


def partial_bias_of(walkers, inv, trial, vectors):
    n_walk, n_vec = walkers.shape[0], vectors.shape[0]
    return pl.pallas_call(
        bias_kernel,
        out_shape=jax.ShapeDtypeStruct((n_walk, n_vec), jnp.float32),
        in_specs=[in_any()] * 4,
        out_specs=in_vmem(),
        scratch_shapes=[
            VMEM(walkers.shape, walkers.dtype),
            VMEM(inv.shape, inv.dtype),
            VMEM(trial.shape, trial.dtype),
            VMEM(vectors.shape, vectors.dtype),
            VMEM(walkers.shape, jnp.float32),
            pltpu.SemaphoreType.DMA((3 + n_vec,)),
        ],
        name="bias",
    )(walkers, inv, trial, vectors)


def operator_kernel(n_line, n_orb, group, place_ref, source_ref, bias0, bias1, bias2, bias3, aux_ref,
                    vec_hbm, factor_ref, *rest):
    piece_refs = rest[:n_line]
    vec_ref, field_ref, weight_ref, sems = rest[n_line:]
    n_walk, n_vec = bias0.shape
    n_rows, n_cols = vec_hbm.shape[1:]
    half = n_rows // 2
    vec_copies = [
        pltpu.make_async_copy(
            vec_hbm.at[:, pl.ds(j * group, group)], vec_ref.at[:, pl.ds(j * group, group)], sems.at[j]
        )
        for j in range(n_rows // group)
    ]
    for copy in vec_copies:
        copy.start()
    z, o = place_ref[0], place_ref[1]
    own = bias0[...] + bias1[...]
    other = bias2[...] + bias3[...]
    shift = -step_root * jnp.concatenate([own, other], axis=0)
    aux = aux_ref[...]
    field_ref[...] = (aux - shift) * step_root
    factor_ref[...] = jnp.sum(aux * shift - 0.5 * shift * shift, axis=1, keepdims=True)
    n_z = n_line // n_orb
    for k in range(n_line):
        to_z = lax.rem(z + k // n_orb, n_z)
        to_o = lax.rem(o + k % n_orb, n_orb)
        row = source_ref[to_z * n_orb + to_o]
        weight_ref[pl.ds(k, 1), :] = field_ref[pl.ds(row, 1), :]
    weighted = weight_ref[...].astype(jnp.bfloat16)
    rows_of = lax.broadcasted_iota(jnp.int32, (n_line * group, n_line), 0) // group
    pick = (rows_of == lax.broadcasted_iota(jnp.int32, (n_line * group, n_line), 1))
    tall = mm(pick.astype(jnp.float32).astype(jnp.bfloat16), weighted).astype(jnp.bfloat16)
    cols_of = lax.broadcasted_iota(jnp.int32, (n_vec, n_vec * group), 1) // group
    spread = (cols_of == lax.broadcasted_iota(jnp.int32, (n_vec, n_vec * group), 0))
    wide = mm(tall, spread.astype(jnp.float32).astype(jnp.bfloat16))
    row_in = lax.rem(lax.broadcasted_iota(jnp.int32, wide.shape, 0), group)
    col_in = lax.rem(lax.broadcasted_iota(jnp.int32, wide.shape, 1), group)
    spreader = jnp.where(row_in == col_in, wide, 0.0).astype(jnp.bfloat16)

    def block(row, col_block):
        col = pl.multiple_of(lax.rem(col_block, n_cols // LANE) * LANE, LANE)
        stack = vec_ref[:, pl.ds(row, group), pl.ds(col, LANE)]
        return mm(spreader, stack.reshape(n_vec * group, LANE)).reshape(n_line, group, LANE)

    first = o * (n_rows // LANE)
    for copy in vec_copies:
        copy.wait()
    rest_rows = 4 * half
    for k in range(n_line):
        piece_refs[k][pl.ds(rest_rows, 16), :] = jnp.zeros((16, LANE), jnp.bfloat16)
    diag_rows = [jnp.zeros((1, LANE), jnp.float32) for _ in range(n_line)]
    for j in range(half // group):
        low = j * group
        upper = block(low, first)
        lower = block(half + low, first + 1)
        i_at = low + lax.broadcasted_iota(jnp.int32, (group, LANE), 0)
        j_at = lax.broadcasted_iota(jnp.int32, (group, LANE), 1)
        next0 = block(low, first + 1)
        next1 = block(half + low, first + 2)
        extra = block(pl.multiple_of(o * half, half) + low, first + 2 + o)
        for k in range(n_line):
            merged = jnp.where(i_at <= j_at, upper[k], lower[k])
            diag_rows[k] = diag_rows[k] + jnp.sum(
                jnp.where(i_at == j_at, lower[k], 0.0), axis=0, keepdims=True
            )
            piece_refs[k][pl.ds(low, group), :] = merged.astype(jnp.bfloat16)
            piece_refs[k][pl.ds(half + low, group), :] = next0[k].astype(jnp.bfloat16)
            piece_refs[k][pl.ds(2 * half + low, group), :] = next1[k].astype(jnp.bfloat16)
            piece_refs[k][pl.ds(3 * half + low, group), :] = extra[k].astype(jnp.bfloat16)
    for k in range(n_line):
        piece_refs[k][pl.ds(rest_rows, 16), :] = jnp.broadcast_to(
            diag_rows[k], (16, LANE)
        ).astype(jnp.bfloat16)


def partial_operators(place, source, biases, aux, vectors, n_line, n_orb):
    n_walk, n_vec = biases[0].shape
    n_rows = vectors.shape[1]
    group = 2 * LANE // n_vec
    piece = jax.ShapeDtypeStruct((2 * n_rows + 16, LANE), jnp.bfloat16)
    return pl.pallas_call(
        partial(operator_kernel, n_line, n_orb, group),
        out_shape=[jax.ShapeDtypeStruct((2 * n_walk, 1), jnp.float32)] + [piece] * n_line,
        in_specs=[in_smem(), in_smem()] + [in_vmem()] * 5 + [in_any()],
        out_specs=[in_vmem()] * (1 + n_line),
        scratch_shapes=[
            VMEM(vectors.shape, vectors.dtype),
            VMEM((2 * n_walk, n_vec), jnp.float32),
            VMEM((n_line, n_vec), jnp.float32),
            pltpu.SemaphoreType.DMA((n_rows // group,)),
        ],
        name="operators",
    )(place, source, *biases, aux, vectors)


def taylor_kernel(n_z, flags_ref, *refs):
    same, flip = refs[:n_z], refs[n_z : 2 * n_z]
    own_ref, orb_ref, walk_ref, far_ref, mine_ref, other_ref, op_ref, term_ref, sum_ref = refs[2 * n_z :]
    half = LANE

    def total(pieces):
        result = pieces[0][...].astype(jnp.float32)
        for piece in pieces[1:]:
            result = result + piece[...].astype(jnp.float32)
        return result

    i_at = lax.broadcasted_iota(jnp.int32, (LANE, LANE), 0)
    j_at = lax.broadcasted_iota(jnp.int32, (LANE, LANE), 1)

    def put(bi, bj, value):
        op_ref[pl.ds(bi * LANE, LANE), pl.ds(bj * LANE, LANE)] = value.astype(jnp.bfloat16)

    def put_pair(bi, bj, value):
        put(bi, bj, value)
        put(bj, bi, value.T)

    extras = []
    for base, pieces in ((0, same), (2, flip)):
        sums = total(pieces)
        merged = sums[:half]
        turned = merged.T
        put(base, base, jnp.where(i_at <= j_at, merged, turned))
        second = jnp.where(i_at > j_at, merged, turned)
        put(base + 1, base + 1, jnp.where(i_at == j_at, sums[4 * half : 4 * half + 1], second))
        put_pair(base, base + 1, sums[half : 2 * half])
        put_pair(base + 1, (base + 2) % 4, sums[2 * half : 3 * half])
        extras.append(sums[3 * half : 4 * half])
    lowest = flags_ref[0] == 0
    across = extras[1].T
    put_pair(0, 2, jnp.where(lowest, extras[0], across))
    put_pair(1, 3, jnp.where(lowest, across, extras[0]))

    here = flags_ref[1] == 1
    rows = own_ref.shape[0]
    term_ref[pl.ds(0, rows), :] = jnp.where(here, own_ref[...], walk_ref[...])
    term_ref[pl.ds(rows, rows), :] = jnp.where(here, orb_ref[...], far_ref[...])
    sum_ref[...] = term_ref[...].astype(jnp.float32)
    for degree in range(1, ORDER + 1):
        product = mm(op_ref[...], term_ref[...])
        term = (product / degree).astype(jnp.bfloat16)
        sum_ref[...] += term.astype(jnp.float32)
        if degree < ORDER:
            term_ref[...] = term
    mine_ref[...] = sum_ref[pl.ds(0, rows), :].astype(jnp.bfloat16)
    other_ref[...] = sum_ref[pl.ds(rows, rows), :].astype(jnp.bfloat16)


def taylor(flags, same, flip, candidates):
    rows, width = candidates[0].shape
    out = jax.ShapeDtypeStruct((rows, width), jnp.bfloat16)
    return pl.pallas_call(
        partial(taylor_kernel, len(same)),
        out_shape=[out, out],
        in_specs=[in_smem()] + [in_vmem()] * (len(same) + len(flip) + 4),
        out_specs=[in_vmem()] * 2,
        scratch_shapes=[
            VMEM((2 * rows, 2 * rows), jnp.bfloat16),
            VMEM((2 * rows, width), jnp.bfloat16),
            VMEM((2 * rows, width), jnp.float32),
        ],
        name="taylor",
    )(flags, *same, *flip, *candidates)


def place_kernel(n_line, n_orb, place_ref, *refs):
    pieces, out_ref, sems = refs[:n_line], refs[n_line], refs[n_line + 1]
    z, o = place_ref[0], place_ref[1]
    n_z = n_line // n_orb
    copies = []
    for k in range(n_line):
        from_z = lax.rem(z + n_z - k // n_orb, n_z)
        from_o = lax.rem(o + n_orb - k % n_orb, n_orb)
        copies.append(
            pltpu.make_async_copy(pieces[k], out_ref.at[from_z * n_orb + from_o], sems.at[k])
        )
    for copy in copies:
        copy.start()
    for copy in copies:
        copy.wait()


def put_in_place(place, pieces, n_orb):
    n_line = len(pieces)
    return pl.pallas_call(
        partial(place_kernel, n_line, n_orb),
        out_shape=jax.ShapeDtypeStruct((n_line,) + pieces[0].shape, pieces[0].dtype),
        in_specs=[in_smem()] + [in_any()] * n_line,
        out_specs=in_any(),
        scratch_shapes=[pltpu.SemaphoreType.DMA((n_line,))],
        name="place",
    )(place, *pieces)


def moved(value, axes, sizes, steps):
    perm = []
    for a in range(sizes[0]):
        for b in range(sizes[1]):
            to = ((a + steps[0]) % sizes[0]) * sizes[1] + (b + steps[1]) % sizes[1]
            perm.append((a * sizes[1] + b, to))
    return lax.ppermute(value, axes, perm)


def slot_device(n_z, n_x, n_o, walkers, inv_intersection, trial, vectors, aux_field, log_weight, copy_list):
    n_walk = walkers.shape[0]
    n_line = n_z * n_o
    z, x, o = lax.axis_index("vec"), lax.axis_index("walk"), lax.axis_index("orb")
    line = partial(moved, axes=("vec", "orb"), sizes=(n_z, n_o))
    near = partial(moved, axes=("walk", "orb"), sizes=(n_x, n_o))

    packed = jnp.concatenate(
        [aux_field, log_weight[None, :], copy_list.astype(jnp.float32)[None, :]], axis=0
    )
    far = near(packed, steps=(1, 0))
    far_copy = far[n_walk + 1].astype(jnp.int32)
    aux_both = jnp.concatenate([aux_field, far[:n_walk]], axis=0)
    log_both = jnp.concatenate([log_weight, far[n_walk]], axis=0)
    source = copy_list % n_walk + n_walk * (copy_list // n_walk != x).astype(jnp.int32)
    place = jnp.stack([z, o]).astype(jnp.int32)

    own_bias = partial_bias_of(walkers, inv_intersection, trial, vectors)
    biases = [own_bias] + [near(own_bias, steps=s) for s in ((0, 1), (1, 0), (1, 1))]

    def walker_at(index):
        return lax.dynamic_index_in_dim(walkers, index % n_walk, 0, keepdims=False)

    slot = z * n_o + o
    mate = z * n_o + (n_o - 1 - o)
    candidates = [
        walker_at(copy_list[slot]),
        near(walker_at(copy_list[mate]), steps=(0, 1)),
        near(walker_at(far_copy[slot]), steps=(1, 0)),
        near(walker_at(far_copy[mate]), steps=(1, 1)),
    ]

    factor, *pieces = partial_operators(place, source, biases, aux_both, vectors, n_line, n_o)
    steps = [(k // n_o, k % n_o) for k in range(n_line)]
    arrived = [pieces[0]] + [line(pieces[k], steps=steps[k]) for k in range(1, n_line)]
    same = [arrived[k] for k in range(n_line) if steps[k][1] == 0]
    flip = [arrived[k] for k in range(n_line) if steps[k][1] == 1]
    factors = [factor] + [line(factor, steps=(d, 0)) for d in range(1, n_z)]
    new_log = log_both + ((factors[0] + factors[2]) + (factors[1] + factors[3]))[:, 0]
    weights_out = new_log[source]

    flags = jnp.stack([o, (copy_list[slot] // n_walk == x).astype(jnp.int32)]).astype(jnp.int32)
    mine, other = taylor(flags, same, flip, candidates)
    landed = []
    for k in range(n_line):
        half = mine if steps[k][1] == 0 else other
        landed.append(half if k == 0 else line(half, steps=steps[k]))
    return put_in_place(place, landed, n_o), weights_out


def suits(mesh, walkers, trial, vectors):
    n_z, n_x, n_o = mesh.shape["vec"], mesh.shape["walk"], mesh.shape["orb"]
    per_device = walkers.shape[0] // (mesh.shape["grp"] * n_x)
    local_vectors = vectors.shape[0] // n_z
    return (
        n_o == 2
        and n_x == 2
        and n_z == 4
        and per_device == n_z * n_o
        and local_vectors == per_device
        and vectors.shape[1] == 4 * LANE
        and trial.shape[1] == LANE
    )


def solution(mesh):
    def step(walkers, inv_intersection, trial, vectors, aux_field, log_weight, copy_list):
        if suits(mesh, walkers, trial, vectors):
            body = partial(slot_device, mesh.shape["vec"], mesh.shape["walk"], mesh.shape["orb"])
        else:
            body = general_device
        return jax.shard_map(
            body,
            mesh=mesh,
            in_specs=(
                P(("grp", "walk"), "orb", None),
                P(("grp", "walk"), None, None),
                P(),
                P("vec", "orb", None),
                P(("grp", "walk"), "vec"),
                P(("grp", "walk")),
                P(("grp", "walk")),
            ),
            out_specs=(P(("grp", "walk"), "orb", None), P(("grp", "walk"))),
            check_vma=False,
        )(walkers, inv_intersection, trial, vectors, aux_field, log_weight, copy_list)

    return step
```

```python
from functools import partial
import math

import jax
import jax.numpy as jnp
from jax import lax
from jax.experimental import pallas as pl
from jax.experimental.pallas import tpu as pltpu
from jax.sharding import PartitionSpec as P

ORDER = 6
LANE = 128

step_root = math.sqrt(0.08)

VMEM = pltpu.VMEM
SMEM = pltpu.SMEM


def in_vmem():
    return pl.BlockSpec(memory_space=VMEM)


def in_smem():
    return pl.BlockSpec(memory_space=SMEM)


def in_any():
    return pl.BlockSpec(memory_space=pl.ANY)


def mm(a, b):
    return jnp.dot(a, b, preferred_element_type=jnp.float32)


def fold_rows(operator, carry, piece, start):
    return jnp.einsum("wnm,wme->wne", operator, piece, preferred_element_type=jnp.float32)


def general_device(walkers, inv_intersection, trial, vectors, aux_field, log_weight, copy_list):
    green = jnp.einsum(
        "wne,wef->wnf", walkers, inv_intersection, preferred_element_type=jnp.float32
    ).astype(jnp.bfloat16)
    mixed = jnp.einsum("gnm,me->gne", vectors, trial, preferred_element_type=jnp.float32).astype(
        jnp.bfloat16
    )
    partial_bias = jnp.einsum("wne,gne->wg", green, mixed, preferred_element_type=jnp.float32)
    bias = lax.psum(partial_bias, "orb")
    shift = -step_root * bias
    field = aux_field - shift
    own_factor = jnp.sum(aux_field * shift - 0.5 * shift * shift, axis=1)
    new_log = log_weight + lax.psum(own_factor, "vec")
    weighted = (field * step_root).astype(jnp.bfloat16)
    local_operator = jnp.einsum(
        "wg,gnm->wnm", weighted, vectors, preferred_element_type=jnp.float32
    )
    operator = lax.psum(local_operator, "vec").astype(jnp.bfloat16)
    running = walkers.astype(jnp.float32)
    folder = partial(fold_rows, operator)
    operand = walkers
    for degree in range(1, ORDER + 1):
        initial = jnp.zeros(running.shape, jnp.float32)
        summed = folder(initial, lax.all_gather(operand, "orb", axis=1, tiled=True), jnp.int32(0))
        new_term = (summed / degree).astype(jnp.bfloat16)
        running = running + new_term.astype(jnp.float32)
        if degree < ORDER:
            operand = new_term
    propagated = running.astype(jnp.bfloat16)
    every_walker = lax.all_gather(propagated, "walk", axis=0, tiled=True)
    every_log = lax.all_gather(new_log, "walk", axis=0, tiled=True)
    return (every_walker[copy_list], every_log[copy_list])


def bias_kernel(aux_ref, log_ref, walkers_hbm, inv_hbm, trial_hbm, vec_hbm, out_ref,
                walkers_ref, inv_ref, trial_ref, vec_ref, green_ref, sems):
    n_walk = walkers_hbm.shape[0]
    n_vec = vec_hbm.shape[0]
    copies = [
        pltpu.make_async_copy(walkers_hbm, walkers_ref, sems.at[0]),
        pltpu.make_async_copy(inv_hbm, inv_ref, sems.at[1]),
        pltpu.make_async_copy(trial_hbm, trial_ref, sems.at[2]),
    ]
    vec_copies = [
        pltpu.make_async_copy(vec_hbm.at[g], vec_ref.at[g], sems.at[3 + g]) for g in range(n_vec)
    ]
    for copy in copies + vec_copies:
        copy.start()
    out_ref[...] = jnp.zeros_like(out_ref)
    out_ref[pl.ds(n_walk, n_walk), :] = aux_ref[...]
    out_ref[pl.ds(2 * n_walk, 1), :] = log_ref[...]
    copies[0].wait()
    copies[1].wait()
    for w in range(n_walk):
        green_ref[w] = mm(walkers_ref[w], inv_ref[w]).astype(jnp.bfloat16).astype(jnp.float32)
    copies[2].wait()
    trial = trial_ref[...]
    lane = lax.broadcasted_iota(jnp.int32, (n_walk, n_vec), 1)
    total = jnp.zeros((n_walk, n_vec), jnp.float32)
    for g in range(n_vec):
        vec_copies[g].wait()
        mixed = mm(vec_ref[g], trial).astype(jnp.bfloat16).astype(jnp.float32)
        rows = [jnp.sum(green_ref[w] * mixed, axis=0, keepdims=True) for w in range(n_walk)]
        column = jnp.sum(jnp.concatenate(rows, axis=0), axis=1, keepdims=True)
        total = total + jnp.where(lane == g, column, 0.0)
    out_ref[pl.ds(0, n_walk), :] = total


def partial_bias_of(aux, log_weight, walkers, inv, trial, vectors):
    n_walk, n_vec = aux.shape
    return pl.pallas_call(
        bias_kernel,
        out_shape=jax.ShapeDtypeStruct((3 * n_walk, n_vec), jnp.float32),
        in_specs=[in_vmem()] * 2 + [in_any()] * 4,
        out_specs=in_vmem(),
        scratch_shapes=[
            VMEM(walkers.shape, walkers.dtype),
            VMEM(inv.shape, inv.dtype),
            VMEM(trial.shape, trial.dtype),
            VMEM(vectors.shape, vectors.dtype),
            VMEM(walkers.shape, jnp.float32),
            pltpu.SemaphoreType.DMA((3 + n_vec,)),
        ],
        name="bias",
    )(aux, log_weight[None, :], walkers, inv, trial, vectors)


def operator_kernel(n_z, n_o, group, copy_ref, own_ref, orb_ref, walk_ref, far_ref, here_hbm, mate_hbm,
                    factor_ref, log_ref, *rest):
    piece_refs = rest[:n_z]
    vec_ref, field_ref, weight_ref, sems = rest[n_z:]
    n_walk = own_ref.shape[0] // 3
    n_vec = own_ref.shape[1]
    size = here_hbm.shape[2]
    n_rows = here_hbm.shape[1]
    n_block = size // LANE
    z, x, o = lax.axis_index("vec"), lax.axis_index("walk"), lax.axis_index("orb")

    def block_copy(b, source):
        rows = pl.ds(b * LANE % n_rows, LANE)
        cols = pl.ds(b * LANE, size - b * LANE)
        return pltpu.make_async_copy(
            source.at[:, rows, cols], vec_ref.at[:, pl.ds(b * LANE, LANE), cols], sems.at[b]
        )

    for b in range(n_block):
        mine = o == b * LANE // n_rows

        @pl.when(mine)
        def _():
            block_copy(b, here_hbm).start()

        @pl.when(jnp.logical_not(mine))
        def _():
            block_copy(b, mate_hbm).start()

    bias = jnp.concatenate(
        [own_ref[pl.ds(0, n_walk), :] + orb_ref[pl.ds(0, n_walk), :],
         walk_ref[pl.ds(0, n_walk), :] + far_ref[pl.ds(0, n_walk), :]], axis=0
    )
    aux = jnp.concatenate([own_ref[pl.ds(n_walk, n_walk), :], walk_ref[pl.ds(n_walk, n_walk), :]], axis=0)
    shift = -step_root * bias
    field_ref[...] = (aux - shift) * step_root
    factor_ref[...] = jnp.sum(aux * shift - 0.5 * shift * shift, axis=1, keepdims=True)
    for side, ref in enumerate((own_ref, walk_ref)):
        square = (n_walk, n_walk)
        eye = lax.broadcasted_iota(jnp.int32, square, 0) == lax.broadcasted_iota(jnp.int32, square, 1)
        log_ref[pl.ds(side * n_walk, n_walk), :] = jnp.sum(
            jnp.where(eye, ref[pl.ds(2 * n_walk, 1), :], 0.0), axis=1, keepdims=True
        )
    for k in range(n_z):
        source = copy_ref[jnp.bitwise_xor(z, k) * n_o + o]
        row = lax.rem(source, n_walk) + n_walk * (lax.div(source, n_walk) != x).astype(jnp.int32)
        weight_ref[pl.ds(k, 1), :] = field_ref[pl.ds(row, 1), :]
    weighted = weight_ref[...].astype(jnp.bfloat16)
    tall_shape = (n_z * group, n_z)
    pick = lax.broadcasted_iota(jnp.int32, tall_shape, 0) // group == lax.broadcasted_iota(
        jnp.int32, tall_shape, 1
    )
    tall = mm(pick.astype(jnp.float32).astype(jnp.bfloat16), weighted).astype(jnp.bfloat16)
    wide_shape = (n_vec, n_vec * group)
    spread = lax.broadcasted_iota(jnp.int32, wide_shape, 1) // group == lax.broadcasted_iota(
        jnp.int32, wide_shape, 0
    )
    wide = mm(tall, spread.astype(jnp.float32).astype(jnp.bfloat16))
    row_in = lax.rem(lax.broadcasted_iota(jnp.int32, wide.shape, 0), group)
    col_in = lax.rem(lax.broadcasted_iota(jnp.int32, wide.shape, 1), group)
    spreader = jnp.where(row_in == col_in, wide, 0.0).astype(jnp.bfloat16)

    half = n_block // 2
    offsets, at = {}, half * LANE
    for i in range(n_block):
        for j in range(i + 1, n_block):
            offsets[(i, j)] = at
            at += LANE
    lane = lax.broadcasted_iota(jnp.int32, (group, LANE), 1)
    line = lax.broadcasted_iota(jnp.int32, (group, LANE), 0)
    kept = {}
    for i in range(n_block):
        if i < n_block:
            block_copy(i, here_hbm).wait()
        diagonal = [jnp.zeros((1, LANE), jnp.float32) for _ in range(n_z)]
        for step in range(LANE // group):
            low = i * LANE + step * group
            stack = vec_ref[:, pl.ds(low, group), pl.ds(i * LANE, size - i * LANE)]
            value = mm(spreader, stack.reshape(n_vec * group, size - i * LANE))
            value = value.reshape(n_z, group, size - i * LANE)
            row_at = line + step * group
            for k in range(n_z):
                first = value[k, :, :LANE]
                spot = pl.ds((i // 2) * LANE + step * group, group)
                if i % 2 == 0:
                    kept[(k, step)] = first
                else:
                    merged = jnp.where(row_at <= lane, kept[(k, step)], first)
                    piece_refs[k][spot, :] = merged.astype(jnp.bfloat16)
                    diagonal[k] = diagonal[k] + jnp.sum(
                        jnp.where(row_at == lane, first, 0.0), axis=0, keepdims=True
                    )
                for j in range(i + 1, n_block):
                    spot = pl.ds(offsets[(i, j)] + step * group, group)
                    part = value[k, :, (j - i) * LANE : (j - i + 1) * LANE]
                    piece_refs[k][spot, :] = part.astype(jnp.bfloat16)
        if i % 2 == 1:
            for k in range(n_z):
                piece_refs[k][pl.ds(at + (i // 2) * 16, 16), :] = jnp.broadcast_to(
                    diagonal[k], (16, LANE)
                ).astype(jnp.bfloat16)


def piece_rows(size):
    n_block = size // LANE
    return (n_block // 2 + n_block * (n_block - 1) // 2) * LANE + n_block // 2 * 16


def partial_operators(copy_list, packs, vectors, mate_vectors, n_z, n_o):
    n_walk, n_vec = packs[0].shape[0] // 3, packs[0].shape[1]
    size = vectors.shape[2]
    group = 2 * LANE // n_vec
    piece = jax.ShapeDtypeStruct((piece_rows(size), LANE), jnp.bfloat16)
    column = jax.ShapeDtypeStruct((2 * n_walk, 1), jnp.float32)
    return pl.pallas_call(
        partial(operator_kernel, n_z, n_o, group),
        out_shape=[column, column] + [piece] * n_z,
        in_specs=[in_smem()] + [in_vmem()] * 4 + [in_any()] * 2,
        out_specs=[in_vmem()] * (2 + n_z),
        scratch_shapes=[
            VMEM((n_vec, size, size), vectors.dtype),
            VMEM((2 * n_walk, n_vec), jnp.float32),
            VMEM((n_z, n_vec), jnp.float32),
            pltpu.SemaphoreType.DMA((size // LANE,)),
        ],
        name="operators",
    )(copy_list, *packs, vectors, mate_vectors)


def source_kernel(n_o, copy_ref, far_ref, walkers_hbm, own_out, orb_out, walk_out, diag_out, sems):
    n_walk = walkers_hbm.shape[0]
    z, o = lax.axis_index("vec"), lax.axis_index("orb")
    slot, mate = z * n_o + o, z * n_o + (n_o - 1 - o)
    wanted = [
        (copy_ref, slot, own_out), (copy_ref, mate, orb_out), (far_ref, slot, walk_out), (far_ref, mate, diag_out)
    ]
    copies = [
        pltpu.make_async_copy(walkers_hbm.at[lax.rem(ref[at], n_walk)], out, sems.at[i])
        for i, (ref, at, out) in enumerate(wanted)
    ]
    for copy in copies:
        copy.start()
    for copy in copies:
        copy.wait()


def source_walkers(copy_list, far_copy, walkers, n_o):
    out = jax.ShapeDtypeStruct(walkers.shape[1:], walkers.dtype)
    return pl.pallas_call(
        partial(source_kernel, n_o),
        out_shape=[out] * 4,
        in_specs=[in_smem()] * 2 + [in_any()],
        out_specs=[in_vmem()] * 4,
        scratch_shapes=[pltpu.SemaphoreType.DMA((4,))],
        name="sources",
    )(copy_list, far_copy, walkers)


def weights_kernel(copy_ref, log_ref, f0, f1, f2, f3, out_ref):
    n_both = log_ref.shape[0]
    n_walk = n_both // 2
    x = lax.axis_index("walk")
    new_log = log_ref[...] + ((f0[...] + f1[...]) + (f2[...] + f3[...]))
    source = copy_ref[...]
    row = lax.rem(source, n_walk) + n_walk * (lax.div(source, n_walk) != x).astype(jnp.int32)
    shape = (n_both, source.shape[1])
    at = lax.broadcasted_iota(jnp.int32, shape, 0)
    out_ref[...] = jnp.sum(
        jnp.where(at == jnp.broadcast_to(row, shape), jnp.broadcast_to(new_log, shape), 0.0),
        axis=0, keepdims=True,
    )


def slot_weights(copy_list, log_column, factors):
    return pl.pallas_call(
        weights_kernel,
        out_shape=jax.ShapeDtypeStruct((1,) + copy_list.shape, jnp.float32),
        in_specs=[in_vmem()] * 6,
        out_specs=in_vmem(),
        name="weights",
    )(copy_list[None, :], log_column, *factors)[0]


def taylor_kernel(n_z, n_o, copy_ref, *refs):
    pieces = refs[:n_z]
    own_ref, orb_ref, walk_ref, far_ref, mine_ref, other_ref, op_ref, term_ref, sum_ref = refs[n_z:]
    z, x, o = lax.axis_index("vec"), lax.axis_index("walk"), lax.axis_index("orb")
    n_walk = copy_ref.shape[0]
    n_block = op_ref.shape[0] // LANE
    i_at = lax.broadcasted_iota(jnp.int32, (LANE, LANE), 0)
    j_at = lax.broadcasted_iota(jnp.int32, (LANE, LANE), 1)

    def total(start, count):
        result = pieces[0][pl.ds(start, count), :].astype(jnp.float32)
        for piece in pieces[1:]:
            result = result + piece[pl.ds(start, count), :].astype(jnp.float32)
        return result

    def put(i, j, value):
        op_ref[pl.ds(i * LANE, LANE), pl.ds(j * LANE, LANE)] = value.astype(jnp.bfloat16)

    at = n_block // 2 * LANE
    for i in range(n_block):
        for j in range(i + 1, n_block):
            value = total(at, LANE)
            put(i, j, value)
            put(j, i, value.T)
            at += LANE
    for pair in range(n_block // 2):
        merged = total(pair * LANE, LANE)
        diagonal = total(at + pair * 16, 16)[:1]
        turned = merged.T
        put(2 * pair, 2 * pair, jnp.where(i_at <= j_at, merged, turned))
        second = jnp.where(i_at > j_at, merged, turned)
        put(2 * pair + 1, 2 * pair + 1, jnp.where(i_at == j_at, diagonal, second))

    here = lax.div(copy_ref[z * n_o + o], n_walk) == x
    rows = own_ref.shape[0]
    top = pl.ds(pl.multiple_of(o * rows, rows), rows)
    bottom = pl.ds(pl.multiple_of((1 - o) * rows, rows), rows)
    term_ref[top, :] = jnp.where(here, own_ref[...], walk_ref[...])
    term_ref[bottom, :] = jnp.where(here, orb_ref[...], far_ref[...])
    sum_ref[...] = term_ref[...].astype(jnp.float32)
    for degree in range(1, ORDER + 1):
        product = mm(op_ref[...], term_ref[...])
        term = (product / degree).astype(jnp.bfloat16)
        sum_ref[...] += term.astype(jnp.float32)
        if degree < ORDER:
            term_ref[...] = term
    mine_ref[...] = sum_ref[top, :].astype(jnp.bfloat16)
    other_ref[...] = sum_ref[bottom, :].astype(jnp.bfloat16)


def taylor(copy_list, pieces, candidates, n_o):
    rows, width = candidates[0].shape
    size = n_o * rows
    out = jax.ShapeDtypeStruct((rows, width), jnp.bfloat16)
    return pl.pallas_call(
        partial(taylor_kernel, len(pieces), n_o),
        out_shape=[out, out],
        in_specs=[in_smem()] + [in_vmem()] * (len(pieces) + 4),
        out_specs=[in_vmem()] * 2,
        scratch_shapes=[
            VMEM((size, size), jnp.bfloat16),
            VMEM((size, width), jnp.bfloat16),
            VMEM((size, width), jnp.float32),
        ],
        name="taylor",
    )(copy_list, *pieces, *candidates)


def place_kernel(steps, n_o, *refs):
    n_line = len(steps)
    pieces, out_ref, sems = refs[:n_line], refs[n_line], refs[n_line + 1]
    z, o = lax.axis_index("vec"), lax.axis_index("orb")
    copies = [
        pltpu.make_async_copy(
            pieces[k],
            out_ref.at[jnp.bitwise_xor(z, dz) * n_o + jnp.bitwise_xor(o, flip)],
            sems.at[k],
        )
        for k, (dz, flip) in enumerate(steps)
    ]
    for copy in copies:
        copy.start()
    for copy in copies:
        copy.wait()


def put_in_place(steps, pieces, n_o):
    n_line = len(pieces)
    return pl.pallas_call(
        partial(place_kernel, steps, n_o),
        out_shape=jax.ShapeDtypeStruct((n_line,) + pieces[0].shape, pieces[0].dtype),
        in_specs=[in_any()] * n_line,
        out_specs=in_vmem(),
        scratch_shapes=[pltpu.SemaphoreType.DMA((n_line,))],
        name="place",
    )(*pieces)


def swapped(value, axes, sizes, masks):
    perm = []
    for a in range(sizes[0]):
        for b in range(sizes[1]):
            perm.append((a * sizes[1] + b, (a ^ masks[0]) * sizes[1] + (b ^ masks[1])))
    return lax.ppermute(value, axes, perm)


def slot_device(n_z, n_x, n_o, walkers, inv_intersection, trial, vectors, aux_field, log_weight, copy_list):
    line = partial(swapped, axes=("vec", "orb"), sizes=(n_z, n_o))
    near = partial(swapped, axes=("walk", "orb"), sizes=(n_x, n_o))

    mate_vectors = near(vectors, masks=(0, 1))
    far_copy = near(copy_list, masks=(1, 0))
    own_pack = partial_bias_of(aux_field, log_weight, walkers, inv_intersection, trial, vectors)
    packs = [own_pack] + [near(own_pack, masks=m) for m in ((0, 1), (1, 0), (1, 1))]
    wanted = source_walkers(copy_list, far_copy, walkers, n_o)
    candidates = [wanted[0]] + [
        near(value, masks=m) for value, m in zip(wanted[1:], ((0, 1), (1, 0), (1, 1)))
    ]
    factor, log_column, *pieces = partial_operators(copy_list, packs, vectors, mate_vectors, n_z, n_o)
    arrived = [pieces[0]] + [line(pieces[k], masks=(k, 0)) for k in range(1, n_z)]
    factors = [factor] + [line(factor, masks=(k, 0)) for k in range(1, n_z)]
    weights_out = slot_weights(copy_list, log_column, factors)

    mine, other = taylor(copy_list, arrived, candidates, n_o)
    steps = [(k, flip) for k in range(n_z) for flip in range(n_o)]
    landed = []
    for dz, flip in steps:
        half = mine if flip == 0 else other
        landed.append(half if (dz, flip) == (0, 0) else line(half, masks=(dz, flip)))
    return put_in_place(steps, landed, n_o), weights_out


def suits(mesh, walkers, trial, vectors):
    n_z, n_x, n_o = mesh.shape["vec"], mesh.shape["walk"], mesh.shape["orb"]
    per_device = walkers.shape[0] // (mesh.shape["grp"] * n_x)
    local_vectors = vectors.shape[0] // n_z
    return (
        n_o == 2
        and n_x == 2
        and n_z == 4
        and per_device == n_z * n_o
        and local_vectors == per_device
        and vectors.shape[1] == 4 * LANE
        and trial.shape[1] == LANE
    )


def solution(mesh):
    def step(walkers, inv_intersection, trial, vectors, aux_field, log_weight, copy_list):
        if suits(mesh, walkers, trial, vectors):
            body = partial(slot_device, mesh.shape["vec"], mesh.shape["walk"], mesh.shape["orb"])
        else:
            body = general_device
        return jax.shard_map(
            body,
            mesh=mesh,
            in_specs=(
                P(("grp", "walk"), "orb", None),
                P(("grp", "walk"), None, None),
                P(),
                P("vec", "orb", None),
                P(("grp", "walk"), "vec"),
                P(("grp", "walk")),
                P(("grp", "walk")),
            ),
            out_specs=(P(("grp", "walk"), "orb", None), P(("grp", "walk"))),
            check_vma=False,
        )(walkers, inv_intersection, trial, vectors, aux_field, log_weight, copy_list)

    return step
```

```python
from functools import partial
import math

import jax
import jax.numpy as jnp
from jax import lax
from jax.experimental import pallas as pl
from jax.experimental.pallas import tpu as pltpu
from jax.sharding import PartitionSpec as P

ORDER = 6
LANE = 128

step_root = math.sqrt(0.08)

VMEM = pltpu.VMEM
SMEM = pltpu.SMEM


def in_vmem():
    return pl.BlockSpec(memory_space=VMEM)


def in_smem():
    return pl.BlockSpec(memory_space=SMEM)


def in_any():
    return pl.BlockSpec(memory_space=pl.ANY)


def on_chip(*values):
    return [pltpu.with_memory_space_constraint(value, VMEM) for value in values]


def mm(a, b):
    return jnp.dot(a, b, preferred_element_type=jnp.float32)


def fold_rows(operator, carry, piece, start):
    return jnp.einsum("wnm,wme->wne", operator, piece, preferred_element_type=jnp.float32)


def general_device(walkers, inv_intersection, trial, vectors, aux_field, log_weight, copy_list):
    green = jnp.einsum(
        "wne,wef->wnf", walkers, inv_intersection, preferred_element_type=jnp.float32
    ).astype(jnp.bfloat16)
    mixed = jnp.einsum("gnm,me->gne", vectors, trial, preferred_element_type=jnp.float32).astype(
        jnp.bfloat16
    )
    partial_bias = jnp.einsum("wne,gne->wg", green, mixed, preferred_element_type=jnp.float32)
    bias = lax.psum(partial_bias, "orb")
    shift = -step_root * bias
    field = aux_field - shift
    own_factor = jnp.sum(aux_field * shift - 0.5 * shift * shift, axis=1)
    new_log = log_weight + lax.psum(own_factor, "vec")
    weighted = (field * step_root).astype(jnp.bfloat16)
    local_operator = jnp.einsum(
        "wg,gnm->wnm", weighted, vectors, preferred_element_type=jnp.float32
    )
    operator = lax.psum(local_operator, "vec").astype(jnp.bfloat16)
    running = walkers.astype(jnp.float32)
    folder = partial(fold_rows, operator)
    operand = walkers
    for degree in range(1, ORDER + 1):
        initial = jnp.zeros(running.shape, jnp.float32)
        summed = folder(initial, lax.all_gather(operand, "orb", axis=1, tiled=True), jnp.int32(0))
        new_term = (summed / degree).astype(jnp.bfloat16)
        running = running + new_term.astype(jnp.float32)
        if degree < ORDER:
            operand = new_term
    propagated = running.astype(jnp.bfloat16)
    every_walker = lax.all_gather(propagated, "walk", axis=0, tiled=True)
    every_log = lax.all_gather(new_log, "walk", axis=0, tiled=True)
    return (every_walker[copy_list], every_log[copy_list])


def bias_kernel(aux_ref, log_ref, copy_ref, walkers_hbm, inv_hbm, trial_hbm, vec_hbm, out_ref,
                walkers_ref, inv_ref, trial_ref, vec_ref, green_ref, sems):
    n_walk = walkers_hbm.shape[0]
    n_vec = vec_hbm.shape[0]
    copies = [
        pltpu.make_async_copy(walkers_hbm, walkers_ref, sems.at[0]),
        pltpu.make_async_copy(inv_hbm, inv_ref, sems.at[1]),
        pltpu.make_async_copy(trial_hbm, trial_ref, sems.at[2]),
    ]
    vec_copies = [
        pltpu.make_async_copy(vec_hbm.at[g], vec_ref.at[g], sems.at[3 + g]) for g in range(n_vec)
    ]
    for copy in copies + vec_copies:
        copy.start()
    out_ref[...] = jnp.zeros_like(out_ref)
    out_ref[pl.ds(n_walk, n_walk), :] = aux_ref[...]
    out_ref[pl.ds(2 * n_walk, 1), :] = log_ref[...]
    out_ref[pl.ds(2 * n_walk + 1, 1), :] = copy_ref[...].astype(jnp.float32)
    copies[0].wait()
    copies[1].wait()
    for w in range(n_walk):
        green_ref[w] = mm(walkers_ref[w], inv_ref[w]).astype(jnp.bfloat16).astype(jnp.float32)
    copies[2].wait()
    trial = trial_ref[...]
    lane = lax.broadcasted_iota(jnp.int32, (n_walk, n_vec), 1)
    total = jnp.zeros((n_walk, n_vec), jnp.float32)
    for g in range(n_vec):
        vec_copies[g].wait()
        mixed = mm(vec_ref[g], trial).astype(jnp.bfloat16).astype(jnp.float32)
        rows = [jnp.sum(green_ref[w] * mixed, axis=0, keepdims=True) for w in range(n_walk)]
        column = jnp.sum(jnp.concatenate(rows, axis=0), axis=1, keepdims=True)
        total = total + jnp.where(lane == g, column, 0.0)
    out_ref[pl.ds(0, n_walk), :] = total


def partial_bias_of(aux, log_weight, copy_list, walkers, inv, trial, vectors):
    n_walk, n_vec = aux.shape
    return pl.pallas_call(
        bias_kernel,
        out_shape=VMEM((3 * n_walk, n_vec), jnp.float32),
        in_specs=[in_vmem()] * 3 + [in_any()] * 4,
        out_specs=in_vmem(),
        scratch_shapes=[
            VMEM(walkers.shape, walkers.dtype),
            VMEM(inv.shape, inv.dtype),
            VMEM(trial.shape, trial.dtype),
            VMEM(vectors.shape, vectors.dtype),
            VMEM(walkers.shape, jnp.float32),
            pltpu.SemaphoreType.DMA((3 + n_vec,)),
        ],
        name="bias",
    )(aux, log_weight[None, :], copy_list[None, :], walkers, inv, trial, vectors)


def operator_kernel(n_z, n_o, group, copy_ref, own_ref, orb_ref, walk_ref, far_ref, here_hbm, mate_hbm,
                    walkers_hbm, log_ref, *rest):
    piece_refs, source_refs = rest[:n_z], rest[n_z : n_z + 4]
    vec_ref, field_ref, weight_ref, sems = rest[n_z + 4 :]
    n_walk = own_ref.shape[0] // 3
    n_vec = own_ref.shape[1]
    size = here_hbm.shape[2]
    n_rows = here_hbm.shape[1]
    n_block = size // LANE
    z, x, o = lax.axis_index("vec"), lax.axis_index("walk"), lax.axis_index("orb")

    def block_copy(b, source):
        rows = pl.ds(b * LANE % n_rows, LANE)
        cols = pl.ds(b * LANE, size - b * LANE)
        return pltpu.make_async_copy(
            source.at[:, rows, cols], vec_ref.at[:, pl.ds(b * LANE, LANE), cols], sems.at[b]
        )

    for b in range(n_block):
        mine = o == b * LANE // n_rows

        @pl.when(mine)
        def _():
            block_copy(b, here_hbm).start()

        @pl.when(jnp.logical_not(mine))
        def _():
            block_copy(b, mate_hbm).start()

    slot, mate = z * n_o + o, z * n_o + (n_o - 1 - o)
    far_lane = lax.broadcasted_iota(jnp.int32, (1, n_walk), 1)
    far_list = walk_ref[pl.ds(2 * n_walk + 1, 1), :]

    def far_copy(at):
        return jnp.sum(jnp.where(far_lane == at, far_list, 0.0)).astype(jnp.int32)

    wanted = (copy_ref[slot], copy_ref[mate], far_copy(slot), far_copy(mate))
    source_copies = [
        pltpu.make_async_copy(walkers_hbm.at[lax.rem(at, n_walk)], out, sems.at[n_block + i])
        for i, (at, out) in enumerate(zip(wanted, source_refs))
    ]
    for copy in source_copies:
        copy.start()

    bias = jnp.concatenate(
        [own_ref[pl.ds(0, n_walk), :] + orb_ref[pl.ds(0, n_walk), :],
         walk_ref[pl.ds(0, n_walk), :] + far_ref[pl.ds(0, n_walk), :]], axis=0
    )
    aux = jnp.concatenate([own_ref[pl.ds(n_walk, n_walk), :], walk_ref[pl.ds(n_walk, n_walk), :]], axis=0)
    shift = -step_root * bias
    field_ref[...] = (aux - shift) * step_root
    factor = jnp.sum(aux * shift - 0.5 * shift * shift, axis=1, keepdims=True)
    for side, ref in enumerate((own_ref, walk_ref)):
        square = (n_walk, n_walk)
        eye = lax.broadcasted_iota(jnp.int32, square, 0) == lax.broadcasted_iota(jnp.int32, square, 1)
        log_ref[pl.ds(side * n_walk, n_walk), :] = jnp.sum(
            jnp.where(eye, ref[pl.ds(2 * n_walk, 1), :], 0.0), axis=1, keepdims=True
        )
    for k in range(n_z):
        source = copy_ref[jnp.bitwise_xor(z, k) * n_o + o]
        row = lax.rem(source, n_walk) + n_walk * (lax.div(source, n_walk) != x).astype(jnp.int32)
        weight_ref[pl.ds(k, 1), :] = field_ref[pl.ds(row, 1), :]
    weighted = weight_ref[...].astype(jnp.bfloat16)
    tall_shape = (n_z * group, n_z)
    pick = lax.broadcasted_iota(jnp.int32, tall_shape, 0) // group == lax.broadcasted_iota(
        jnp.int32, tall_shape, 1
    )
    tall = mm(pick.astype(jnp.float32).astype(jnp.bfloat16), weighted).astype(jnp.bfloat16)
    wide_shape = (n_vec, n_vec * group)
    spread = lax.broadcasted_iota(jnp.int32, wide_shape, 1) // group == lax.broadcasted_iota(
        jnp.int32, wide_shape, 0
    )
    wide = mm(tall, spread.astype(jnp.float32).astype(jnp.bfloat16))
    row_in = lax.rem(lax.broadcasted_iota(jnp.int32, wide.shape, 0), group)
    col_in = lax.rem(lax.broadcasted_iota(jnp.int32, wide.shape, 1), group)
    spreader = jnp.where(row_in == col_in, wide, 0.0).astype(jnp.bfloat16)

    half = n_block // 2
    offsets, at = {}, half * LANE
    for i in range(n_block):
        for j in range(i + 1, n_block):
            offsets[(i, j)] = at
            at += LANE
    lane = lax.broadcasted_iota(jnp.int32, (group, LANE), 1)
    line = lax.broadcasted_iota(jnp.int32, (group, LANE), 0)
    kept = {}
    for i in range(n_block):
        if i < n_block:
            block_copy(i, here_hbm).wait()
        diagonal = [jnp.zeros((1, LANE), jnp.float32) for _ in range(n_z)]
        for step in range(LANE // group):
            low = i * LANE + step * group
            stack = vec_ref[:, pl.ds(low, group), pl.ds(i * LANE, size - i * LANE)]
            value = mm(spreader, stack.reshape(n_vec * group, size - i * LANE))
            value = value.reshape(n_z, group, size - i * LANE)
            row_at = line + step * group
            for k in range(n_z):
                first = value[k, :, :LANE]
                spot = pl.ds((i // 2) * LANE + step * group, group)
                if i % 2 == 0:
                    kept[(k, step)] = first
                else:
                    merged = jnp.where(row_at <= lane, kept[(k, step)], first)
                    piece_refs[k][spot, :] = merged.astype(jnp.bfloat16)
                    diagonal[k] = diagonal[k] + jnp.sum(
                        jnp.where(row_at == lane, first, 0.0), axis=0, keepdims=True
                    )
                for j in range(i + 1, n_block):
                    spot = pl.ds(offsets[(i, j)] + step * group, group)
                    part = value[k, :, (j - i) * LANE : (j - i + 1) * LANE]
                    piece_refs[k][spot, :] = part.astype(jnp.bfloat16)
        if i % 2 == 1:
            for k in range(n_z):
                piece_refs[k][pl.ds(at + (i // 2) * 16, 16), :] = jnp.broadcast_to(
                    diagonal[k], (16, LANE)
                ).astype(jnp.bfloat16)
    at += half * 16
    lane = lax.broadcasted_iota(jnp.int32, (2 * n_walk, LANE), 1)
    split = jnp.zeros(lane.shape, jnp.float32)
    for i in range(3):
        part = factor.astype(jnp.bfloat16).astype(jnp.float32)
        split = jnp.where(lane == i, jnp.broadcast_to(part, lane.shape), split)
        factor = factor - part
    for k in range(n_z):
        piece_refs[k][pl.ds(at, 2 * n_walk), :] = split.astype(jnp.bfloat16)
    for copy in source_copies:
        copy.wait()


def piece_rows(size, n_both):
    n_block = size // LANE
    return (n_block // 2 + n_block * (n_block - 1) // 2) * LANE + n_block // 2 * 16 + n_both


def partial_operators(copy_list, packs, vectors, mate_vectors, walkers, n_z, n_o):
    n_walk, n_vec = packs[0].shape[0] // 3, packs[0].shape[1]
    size = vectors.shape[2]
    group = 2 * LANE // n_vec
    piece = VMEM((piece_rows(size, 2 * n_walk), LANE), jnp.bfloat16)
    source = VMEM(walkers.shape[1:], walkers.dtype)
    return pl.pallas_call(
        partial(operator_kernel, n_z, n_o, group),
        out_shape=[VMEM((2 * n_walk, 1), jnp.float32)] + [piece] * n_z + [source] * 4,
        in_specs=[in_smem()] + [in_vmem()] * 4 + [in_any()] * 3,
        out_specs=[in_vmem()] * (1 + n_z + 4),
        scratch_shapes=[
            VMEM((n_vec, size, size), vectors.dtype),
            VMEM((2 * n_walk, n_vec), jnp.float32),
            VMEM((n_z, n_vec), jnp.float32),
            pltpu.SemaphoreType.DMA((size // LANE + 4,)),
        ],
        name="operators",
    )(copy_list, *on_chip(*packs), vectors, mate_vectors, walkers)


def log_weights(copy_row, log_column, parts, x):
    n_walk = log_column.shape[0] // 2
    while len(parts) > 1:
        parts = [parts[i] + parts[i + 1] for i in range(0, len(parts), 2)]
    new_log = log_column + parts[0]
    row = lax.rem(copy_row, n_walk) + n_walk * (lax.div(copy_row, n_walk) != x).astype(jnp.int32)
    shape = (2 * n_walk, copy_row.shape[1])
    at = lax.broadcasted_iota(jnp.int32, shape, 0)
    chosen = jnp.where(at == jnp.broadcast_to(row, shape), jnp.broadcast_to(new_log, shape), 0.0)
    return jnp.sum(chosen, axis=0, keepdims=True)


def taylor_kernel(n_z, n_o, copy_ref, row_ref, log_ref, *refs):
    pieces = refs[:n_z]
    (own_ref, orb_ref, walk_ref, far_ref, mine_ref, other_ref, weights_ref,
     op_ref, term_ref, sum_ref) = refs[n_z:]
    z, x, o = lax.axis_index("vec"), lax.axis_index("walk"), lax.axis_index("orb")
    n_walk = copy_ref.shape[0]
    n_block = op_ref.shape[0] // LANE
    i_at = lax.broadcasted_iota(jnp.int32, (LANE, LANE), 0)
    j_at = lax.broadcasted_iota(jnp.int32, (LANE, LANE), 1)

    def total(start, count):
        result = pieces[0][pl.ds(start, count), :].astype(jnp.float32)
        for piece in pieces[1:]:
            result = result + piece[pl.ds(start, count), :].astype(jnp.float32)
        return result

    def put(i, j, value):
        op_ref[pl.ds(i * LANE, LANE), pl.ds(j * LANE, LANE)] = value.astype(jnp.bfloat16)

    at = n_block // 2 * LANE
    for i in range(n_block):
        for j in range(i + 1, n_block):
            value = total(at, LANE)
            put(i, j, value)
            put(j, i, value.T)
            at += LANE
    for pair in range(n_block // 2):
        merged = total(pair * LANE, LANE)
        diagonal = total(at + pair * 16, 16)[:1]
        turned = merged.T
        put(2 * pair, 2 * pair, jnp.where(i_at <= j_at, merged, turned))
        second = jnp.where(i_at > j_at, merged, turned)
        put(2 * pair + 1, 2 * pair + 1, jnp.where(i_at == j_at, diagonal, second))

    at += n_block // 2 * 16
    factors = [
        jnp.sum(piece[pl.ds(at, 2 * n_walk), :].astype(jnp.float32), axis=1, keepdims=True)
        for piece in pieces
    ]
    weights_ref[...] = log_weights(row_ref[...], log_ref[...], factors, x)

    here = lax.div(copy_ref[z * n_o + o], n_walk) == x
    rows = own_ref.shape[0]
    top = pl.ds(pl.multiple_of(o * rows, rows), rows)
    bottom = pl.ds(pl.multiple_of((1 - o) * rows, rows), rows)
    term_ref[top, :] = jnp.where(here, own_ref[...], walk_ref[...])
    term_ref[bottom, :] = jnp.where(here, orb_ref[...], far_ref[...])
    sum_ref[...] = term_ref[...].astype(jnp.float32)
    for degree in range(1, ORDER + 1):
        product = mm(op_ref[...], term_ref[...])
        term = (product / degree).astype(jnp.bfloat16)
        sum_ref[...] += term.astype(jnp.float32)
        if degree < ORDER:
            term_ref[...] = term
    mine_ref[...] = sum_ref[top, :].astype(jnp.bfloat16)
    other_ref[...] = sum_ref[bottom, :].astype(jnp.bfloat16)


def taylor(copy_list, log_column, pieces, candidates, n_o):
    rows, width = candidates[0].shape
    size = n_o * rows
    out = VMEM((rows, width), jnp.bfloat16)
    return pl.pallas_call(
        partial(taylor_kernel, len(pieces), n_o),
        out_shape=[out, out, jax.ShapeDtypeStruct((1,) + copy_list.shape, jnp.float32)],
        in_specs=[in_smem()] + [in_vmem()] * (2 + len(pieces) + 4),
        out_specs=[in_vmem()] * 3,
        scratch_shapes=[
            VMEM((size, size), jnp.bfloat16),
            VMEM((size, width), jnp.bfloat16),
            VMEM((size, width), jnp.float32),
        ],
        name="taylor",
    )(copy_list, copy_list[None, :], *on_chip(log_column, *pieces, *candidates))


def place_kernel(steps, n_o, *refs):
    n_line = len(steps)
    pieces, out_ref, sems = refs[:n_line], refs[n_line], refs[n_line + 1]
    z, o = lax.axis_index("vec"), lax.axis_index("orb")
    copies = [
        pltpu.make_async_copy(
            pieces[k],
            out_ref.at[jnp.bitwise_xor(z, dz) * n_o + jnp.bitwise_xor(o, flip)],
            sems.at[k],
        )
        for k, (dz, flip) in enumerate(steps)
    ]
    for copy in copies:
        copy.start()
    for copy in copies:
        copy.wait()


def put_in_place(steps, pieces, n_o):
    n_line = len(pieces)
    return pl.pallas_call(
        partial(place_kernel, steps, n_o),
        out_shape=jax.ShapeDtypeStruct((n_line,) + pieces[0].shape, pieces[0].dtype),
        in_specs=[in_vmem()] * n_line,
        out_specs=in_any(),
        scratch_shapes=[pltpu.SemaphoreType.DMA((n_line,))],
        name="place",
    )(*on_chip(*pieces))


def swapped(value, axes, sizes, masks):
    perm = []
    for a in range(sizes[0]):
        for b in range(sizes[1]):
            perm.append((a * sizes[1] + b, (a ^ masks[0]) * sizes[1] + (b ^ masks[1])))
    return lax.ppermute(value, axes, perm)


def slot_device(n_z, n_x, n_o, walkers, inv_intersection, trial, vectors, aux_field, log_weight, copy_list):
    line = partial(swapped, axes=("vec", "orb"), sizes=(n_z, n_o))
    near = partial(swapped, axes=("walk", "orb"), sizes=(n_x, n_o))

    mate_vectors = near(vectors, masks=(0, 1))
    own_pack = partial_bias_of(aux_field, log_weight, copy_list, walkers, inv_intersection, trial, vectors)
    others = ((0, 1), (1, 0), (1, 1))
    packs = [own_pack] + [near(own_pack, masks=m) for m in others]
    log_column, *made = partial_operators(copy_list, packs, vectors, mate_vectors, walkers, n_z, n_o)
    pieces, sources = made[:n_z], made[n_z:]
    arrived = [pieces[0]] + [line(pieces[k], masks=(k, 0)) for k in range(1, n_z)]
    candidates = [sources[0]] + [near(value, masks=m) for value, m in zip(sources[1:], others)]
    mine, other, weights_out = taylor(copy_list, log_column, arrived, candidates, n_o)
    steps = [(k, flip) for k in range(n_z) for flip in range(n_o)]
    landed = []
    for dz, flip in steps:
        half = mine if flip == 0 else other
        landed.append(half if (dz, flip) == (0, 0) else line(half, masks=(dz, flip)))
    return put_in_place(steps, landed, n_o), weights_out[0]


def suits(mesh, walkers, trial, vectors):
    n_z, n_x, n_o = mesh.shape["vec"], mesh.shape["walk"], mesh.shape["orb"]
    per_device = walkers.shape[0] // (mesh.shape["grp"] * n_x)
    local_vectors = vectors.shape[0] // n_z
    return (
        n_o == 2
        and n_x == 2
        and n_z == 4
        and per_device == n_z * n_o
        and local_vectors == per_device
        and vectors.shape[1] == 4 * LANE
        and trial.shape[1] == LANE
    )


def solution(mesh):
    def step(walkers, inv_intersection, trial, vectors, aux_field, log_weight, copy_list):
        if suits(mesh, walkers, trial, vectors):
            body = partial(slot_device, mesh.shape["vec"], mesh.shape["walk"], mesh.shape["orb"])
        else:
            body = general_device
        return jax.shard_map(
            body,
            mesh=mesh,
            in_specs=(
                P(("grp", "walk"), "orb", None),
                P(("grp", "walk"), None, None),
                P(),
                P("vec", "orb", None),
                P(("grp", "walk"), "vec"),
                P(("grp", "walk")),
                P(("grp", "walk")),
            ),
            out_specs=(P(("grp", "walk"), "orb", None), P(("grp", "walk"))),
            check_vma=False,
        )(walkers, inv_intersection, trial, vectors, aux_field, log_weight, copy_list)

    return step
```

```python
from functools import partial
import math

import jax
import jax.numpy as jnp
from jax import lax
from jax.experimental import pallas as pl
from jax.experimental.pallas import tpu as pltpu
from jax.sharding import PartitionSpec as P


ORDER = 6
LANE = 128
VMEM_LIMIT = 24 * 1024 * 1024

step_root = math.sqrt(0.08)

VMEM = pltpu.VMEM


def in_vmem():
    return pl.BlockSpec(memory_space=VMEM)


def in_hbm():
    return pl.BlockSpec(memory_space=pltpu.HBM)


def on_chip(*values):
    return [pltpu.with_memory_space_constraint(value, VMEM) for value in values]


def in_place(*values):
    return [pltpu.with_memory_space_constraint(value, pltpu.HBM) for value in values]


def mm(a, b):
    return jnp.dot(a, b, preferred_element_type=jnp.float32)


def fold_rows(operator, carry, piece, start):
    return jnp.einsum("wnm,wme->wne", operator, piece, preferred_element_type=jnp.float32)


def general_device(walkers, inv_intersection, trial, vectors, aux_field, log_weight, copy_list):
    green = jnp.einsum(
        "wne,wef->wnf", walkers, inv_intersection, preferred_element_type=jnp.float32
    ).astype(jnp.bfloat16)
    mixed = jnp.einsum("gnm,me->gne", vectors, trial, preferred_element_type=jnp.float32).astype(
        jnp.bfloat16
    )
    partial_bias = jnp.einsum("wne,gne->wg", green, mixed, preferred_element_type=jnp.float32)
    bias = lax.psum(partial_bias, "orb")
    shift = -step_root * bias
    field = aux_field - shift
    own_factor = jnp.sum(aux_field * shift - 0.5 * shift * shift, axis=1)
    new_log = log_weight + lax.psum(own_factor, "vec")
    weighted = (field * step_root).astype(jnp.bfloat16)
    local_operator = jnp.einsum(
        "wg,gnm->wnm", weighted, vectors, preferred_element_type=jnp.float32
    )
    operator = lax.psum(local_operator, "vec").astype(jnp.bfloat16)
    running = walkers.astype(jnp.float32)
    folder = partial(fold_rows, operator)
    operand = walkers
    for degree in range(1, ORDER + 1):
        initial = jnp.zeros(running.shape, jnp.float32)
        summed = folder(initial, lax.all_gather(operand, "orb", axis=1, tiled=True), jnp.int32(0))
        new_term = (summed / degree).astype(jnp.bfloat16)
        running = running + new_term.astype(jnp.float32)
        if degree < ORDER:
            operand = new_term
    propagated = running.astype(jnp.bfloat16)
    every_walker = lax.all_gather(propagated, "walk", axis=0, tiled=True)
    every_log = lax.all_gather(new_log, "walk", axis=0, tiled=True)
    return (every_walker[copy_list], every_log[copy_list])


def bias_kernel(aux_hbm, log_hbm, copy_hbm, walkers_hbm, inv_hbm, trial_hbm, vec_hbm, out_ref, vec_ref,
                aux_ref, log_ref, copy_ref, walkers_ref, inv_ref, trial_ref, green_ref, sems):
    n_walk = walkers_hbm.shape[0]
    n_vec = vec_hbm.shape[0]
    copies = [
        pltpu.make_async_copy(source, target, sems.at[i])
        for i, (source, target) in enumerate((
            (walkers_hbm, walkers_ref), (inv_hbm, inv_ref), (trial_hbm, trial_ref),
            (aux_hbm, aux_ref), (log_hbm, log_ref), (copy_hbm, copy_ref),
        ))
    ]
    vec_copies = [
        pltpu.make_async_copy(vec_hbm.at[g], vec_ref.at[g], sems.at[len(copies) + g]) for g in range(n_vec)
    ]
    for copy in copies[:3] + vec_copies + copies[3:]:
        copy.start()
    copies[0].wait()
    copies[1].wait()
    for w in range(n_walk):
        green_ref[w] = mm(walkers_ref[w], inv_ref[w]).astype(jnp.bfloat16).astype(jnp.float32)
    copies[2].wait()
    trial = trial_ref[...]
    lane = lax.broadcasted_iota(jnp.int32, (n_walk, n_vec), 1)
    total = jnp.zeros((n_walk, n_vec), jnp.float32)
    for g in range(n_vec):
        vec_copies[g].wait()
        mixed = mm(vec_ref[g], trial).astype(jnp.bfloat16).astype(jnp.float32)
        rows = [jnp.sum(green_ref[w] * mixed, axis=0, keepdims=True) for w in range(n_walk)]
        column = jnp.sum(jnp.concatenate(rows, axis=0), axis=1, keepdims=True)
        total = total + jnp.where(lane == g, column, 0.0)
    for copy in copies[3:]:
        copy.wait()
    out_ref[pl.ds(0, n_walk), :] = total
    out_ref[pl.ds(n_walk, n_walk), :] = aux_ref[...]
    out_ref[pl.ds(2 * n_walk, n_walk), :] = jnp.zeros((n_walk, n_vec), jnp.float32)
    out_ref[pl.ds(2 * n_walk, 1), :] = log_ref[...]
    out_ref[pl.ds(2 * n_walk + 1, 1), :] = copy_ref[...].astype(jnp.float32)


def partial_bias_of(aux, log_weight, copy_list, walkers, inv, trial, vectors):
    n_walk, n_vec = aux.shape
    log_row, copy_row = log_weight[None, :], copy_list[None, :]
    return pl.pallas_call(
        bias_kernel,
        out_shape=[VMEM((3 * n_walk, n_vec), jnp.float32), VMEM(vectors.shape, vectors.dtype)],
        in_specs=[in_hbm()] * 7,
        out_specs=[in_vmem()] * 2,
        scratch_shapes=[
            VMEM(aux.shape, aux.dtype),
            VMEM(log_row.shape, log_row.dtype),
            VMEM(copy_row.shape, copy_row.dtype),
            VMEM(walkers.shape, walkers.dtype),
            VMEM(inv.shape, inv.dtype),
            VMEM(trial.shape, trial.dtype),
            VMEM(walkers.shape, jnp.float32),
            pltpu.SemaphoreType.DMA((6 + n_vec,)),
        ],
        compiler_params=pltpu.CompilerParams(vmem_limit_bytes=VMEM_LIMIT),
        name="bias",
    )(*in_place(aux, log_row, copy_row, walkers, inv, trial, vectors))


def copies_of(pack_ref):
    n_walk = pack_ref.shape[0] // 3
    return pack_ref[pl.ds(2 * n_walk + 1, 1), :]


def entry(row, at):
    lane = lax.broadcasted_iota(jnp.int32, row.shape, 1)
    return jnp.sum(jnp.where(lane == at, row, 0.0)).astype(jnp.int32)


def layout(n_block):
    at = n_block // 2 * LANE
    offsets = {}
    for i in range(n_block):
        for j in range(i + 1, n_block):
            offsets[(i, j)] = at
            at += LANE
    return offsets, at


def piece_rows(size, n_both):
    n_block = size // LANE
    return layout(n_block)[1] + n_block // 2 * 16 + n_both


def fill_pieces(weights, here_ref, mate_ref, piece_refs, split, o):
    n_vec, n_rows, size = here_ref.shape
    n_block = size // LANE
    in_half = n_rows // LANE
    offsets, at = layout(n_block)
    count = len(piece_refs)
    tall = LANE // 2
    splats = [
        [jnp.broadcast_to(weights[k : k + 1, g : g + 1], (tall, LANE)) for g in range(n_vec)]
        for k in range(count)
    ]

    def sums(i, j, step):
        source = here_ref if i < in_half else mate_ref
        rows = pl.ds(i % in_half * LANE + step * tall, tall)
        column = lax.rem(j + o * in_half, n_block) * LANE
        columns = pl.ds(pl.multiple_of(column, LANE), LANE)
        result = [None] * count
        for g in range(n_vec):
            value = source[g, rows, columns].astype(jnp.float32)
            for k in range(count):
                part = splats[k][g] * value
                result[k] = part if g == 0 else result[k] + part
        return result

    line = lax.broadcasted_iota(jnp.int32, (tall, LANE), 0)
    lane = lax.broadcasted_iota(jnp.int32, (tall, LANE), 1)
    for step in range(LANE // tall):
        row_at = line + step * tall
        for (i, j), offset in offsets.items():
            for k, value in enumerate(sums(i, j, step)):
                piece_refs[k][pl.ds(offset + step * tall, tall), :] = value.astype(jnp.bfloat16)
        for pair in range(n_block // 2):
            upper = sums(2 * pair, 2 * pair, step)
            lower = sums(2 * pair + 1, 2 * pair + 1, step)
            for k in range(count):
                merged = jnp.where(row_at <= lane, upper[k], lower[k])
                piece_refs[k][pl.ds(pair * LANE + step * tall, tall), :] = merged.astype(jnp.bfloat16)
                found = jnp.sum(jnp.where(row_at == lane, lower[k], 0.0), axis=0, keepdims=True)
                spot = pl.ds(at + pair * 16, 16)
                row = jnp.broadcast_to(found, (16, LANE)).astype(jnp.bfloat16)
                if step == 0:
                    piece_refs[k][spot, :] = row
                else:
                    held = piece_refs[k][spot, :]
                    seen = lax.broadcasted_iota(jnp.int32, (16, LANE), 1) < step * tall
                    piece_refs[k][spot, :] = jnp.where(seen, held, row)
    at += n_block // 2 * 16
    for k in range(count):
        piece_refs[k][pl.ds(at, split.shape[0]), :] = split


def split_column(column):
    lane = lax.broadcasted_iota(jnp.int32, (column.shape[0], LANE), 1)
    split = jnp.zeros(lane.shape, jnp.float32)
    for i in range(3):
        part = column.astype(jnp.bfloat16).astype(jnp.float32)
        split = jnp.where(lane == i, jnp.broadcast_to(part, lane.shape), split)
        column = column - part
    return split.astype(jnp.bfloat16)


def joined(split):
    wide = split.astype(jnp.float32)
    return (wide[:, 0:1] + wide[:, 1:2]) + wide[:, 2:3]


def routes(z):
    inner = jnp.logical_or(z == 1, z == 2)
    first = jnp.where(lax.rem(z, 2) == 0, 3, 0)
    crossing = jnp.where(z == 0, 2, jnp.where(z == 3, 1, jnp.where(z == 1, 3, 0)))
    nearby = jnp.where(lax.rem(z, 2) == 0, 1, 2)
    return inner, first, crossing, nearby


def first_kernel(n_o, own_ref, orb_ref, walk_ref, far_ref, here_ref, mate_ref,
                 piece_ref, weight_ref, split_ref, log_ref):
    n_walk = own_ref.shape[0] // 3
    z, x, o = lax.axis_index("vec"), lax.axis_index("walk"), lax.axis_index("orb")
    bias = jnp.concatenate(
        [own_ref[pl.ds(0, n_walk), :] + orb_ref[pl.ds(0, n_walk), :],
         walk_ref[pl.ds(0, n_walk), :] + far_ref[pl.ds(0, n_walk), :]], axis=0
    )
    aux = jnp.concatenate([own_ref[pl.ds(n_walk, n_walk), :], walk_ref[pl.ds(n_walk, n_walk), :]], axis=0)
    shift = -step_root * bias
    weighted = ((aux - shift) * step_root).astype(jnp.bfloat16)
    split = split_column(jnp.sum(aux * shift - 0.5 * shift * shift, axis=1, keepdims=True))
    split_ref[...] = split
    _, first, crossing, nearby = routes(z)
    k_at = lax.broadcasted_iota(jnp.int32, (8, n_walk), 0)
    lane = lax.broadcasted_iota(jnp.int32, (8, n_walk), 1)
    to_z = jnp.where(k_at == 0, first, jnp.where(k_at == 1, crossing, jnp.where(k_at == 2, nearby, z)))
    sources = jnp.sum(
        jnp.where(lane == to_z * n_o + o, jnp.broadcast_to(copies_of(own_ref), lane.shape), 0.0),
        axis=1, keepdims=True,
    ).astype(jnp.int32)
    row = lax.rem(sources, n_walk) + n_walk * (lax.div(sources, n_walk) != x).astype(jnp.int32)
    pick = lax.broadcasted_iota(jnp.int32, (8, 2 * n_walk), 1) == row
    weights = mm(pick.astype(jnp.float32).astype(jnp.bfloat16), weighted)
    weight_ref[...] = weights
    fill_pieces(weights, here_ref, mate_ref, [piece_ref], split, o)
    square = (n_walk, n_walk)
    eye = lax.broadcasted_iota(jnp.int32, square, 0) == lax.broadcasted_iota(jnp.int32, square, 1)
    for side, ref in enumerate((own_ref, walk_ref)):
        log_ref[pl.ds(side * n_walk, n_walk), :] = jnp.sum(
            jnp.where(eye, ref[pl.ds(2 * n_walk, 1), :], 0.0), axis=1, keepdims=True
        )


def first_piece(packs, here, mate, n_o):
    n_walk, n_vec = packs[0].shape[0] // 3, packs[0].shape[1]
    return pl.pallas_call(
        partial(first_kernel, n_o),
        out_shape=[
            VMEM((piece_rows(here.shape[2], 2 * n_walk), LANE), jnp.bfloat16),
            VMEM((8, n_vec), jnp.float32),
            VMEM((2 * n_walk, LANE), jnp.bfloat16),
            VMEM((2 * n_walk, 1), jnp.float32),
        ],
        in_specs=[in_vmem()] * 6,
        out_specs=[in_vmem()] * 4,
        compiler_params=pltpu.CompilerParams(vmem_limit_bytes=VMEM_LIMIT),
        name="first_piece",
    )(*on_chip(*packs, here, mate))


def other_kernel(n_o, own_ref, walk_ref, weight_ref, split_ref, here_ref, mate_ref, walkers_hbm, *refs):
    pieces, sources, sems = refs[:3], refs[3:7], refs[7]
    n_walk = walkers_hbm.shape[0]
    z, o = lax.axis_index("vec"), lax.axis_index("orb")
    slot, mate = z * n_o + o, z * n_o + (n_o - 1 - o)
    own_list, far_list = copies_of(own_ref), copies_of(walk_ref)
    wanted = ((own_list, slot), (own_list, mate), (far_list, slot), (far_list, mate))
    copies = [
        pltpu.make_async_copy(walkers_hbm.at[lax.rem(entry(row, at), n_walk)], out, sems.at[i])
        for i, ((row, at), out) in enumerate(zip(wanted, sources))
    ]
    for copy in copies:
        copy.start()
    fill_pieces(weight_ref[...][1:4], here_ref, mate_ref, pieces, split_ref[...], o)
    for copy in copies:
        copy.wait()


def other_pieces(own_pack, walk_pack, weights, split, here, mate, walkers, n_o):
    piece = VMEM((piece_rows(here.shape[2], split.shape[0]), LANE), jnp.bfloat16)
    source = VMEM(walkers.shape[1:], walkers.dtype)
    return pl.pallas_call(
        partial(other_kernel, n_o),
        out_shape=[piece] * 3 + [source] * 4,
        in_specs=[in_vmem()] * 6 + [in_hbm()],
        out_specs=[in_vmem()] * 7,
        scratch_shapes=[pltpu.SemaphoreType.DMA((4,))],
        compiler_params=pltpu.CompilerParams(vmem_limit_bytes=VMEM_LIMIT),
        name="other_pieces",
    )(*on_chip(own_pack, walk_pack, weights, split, here, mate), *in_place(walkers))


def combine_kernel(n_both, mine_ref, came_ref, out_ref):
    inner = routes(lax.axis_index("vec"))[0]
    body = mine_ref.shape[0] - n_both

    @pl.when(inner)
    def _():
        for low in range(0, body, LANE):
            rows = pl.ds(low, min(LANE, body - low))
            value = mine_ref[rows, :].astype(jnp.float32) + came_ref[rows, :].astype(jnp.float32)
            out_ref[rows, :] = value.astype(jnp.bfloat16)
        tail = pl.ds(body, n_both)
        out_ref[tail, :] = split_column(joined(mine_ref[tail, :]) + joined(came_ref[tail, :]))

    @pl.when(jnp.logical_not(inner))
    def _():
        out_ref[...] = mine_ref[...]


def combined(mine, came, n_both):
    return pl.pallas_call(
        partial(combine_kernel, n_both),
        out_shape=VMEM(mine.shape, mine.dtype),
        in_specs=[in_vmem()] * 2,
        out_specs=in_vmem(),
        compiler_params=pltpu.CompilerParams(vmem_limit_bytes=VMEM_LIMIT),
        name="combine",
    )(*on_chip(mine, came))


def log_weights(copy_row, log_column, total, x):
    n_walk = log_column.shape[0] // 2
    new_log = log_column + total
    source = copy_row.astype(jnp.int32)
    row = lax.rem(source, n_walk) + n_walk * (lax.div(source, n_walk) != x).astype(jnp.int32)
    shape = (2 * n_walk, copy_row.shape[1])
    at = lax.broadcasted_iota(jnp.int32, shape, 0)
    chosen = jnp.where(at == jnp.broadcast_to(row, shape), jnp.broadcast_to(new_log, shape), 0.0)
    return jnp.sum(chosen, axis=0, keepdims=True)


def taylor_kernel(n_o, pack_ref, log_ref, kept_ref, first_ref, cross_ref, inside_ref, inward_ref,
                  own_ref, orb_ref, walk_ref, far_ref, mine_ref, other_ref, weights_ref,
                  op_ref, term_ref, sum_ref):
    z, x, o = lax.axis_index("vec"), lax.axis_index("walk"), lax.axis_index("orb")
    inner = routes(z)[0]
    n_both = log_ref.shape[0]
    n_walk = n_both // 2
    n_block = op_ref.shape[0] // LANE
    offsets, at = layout(n_block)
    i_at = lax.broadcasted_iota(jnp.int32, (LANE, LANE), 0)
    j_at = lax.broadcasted_iota(jnp.int32, (LANE, LANE), 1)

    def total(start, count):
        rows = pl.ds(start, count)
        first, cross, inside, inward, kept = (
            ref[rows, :].astype(jnp.float32)
            for ref in (first_ref, cross_ref, inside_ref, inward_ref, kept_ref)
        )
        return (kept + cross) + jnp.where(inner, inside + inward, first)

    def put(i, j, value):
        op_ref[pl.ds(i * LANE, LANE), pl.ds(j * LANE, LANE)] = value.astype(jnp.bfloat16)

    for (i, j), offset in offsets.items():
        value = total(offset, LANE)
        put(i, j, value)
        put(j, i, value.T)
    for pair in range(n_block // 2):
        merged = total(pair * LANE, LANE)
        diagonal = total(at + pair * 16, 16)[:1]
        turned = merged.T
        put(2 * pair, 2 * pair, jnp.where(i_at <= j_at, merged, turned))
        second = jnp.where(i_at > j_at, merged, turned)
        put(2 * pair + 1, 2 * pair + 1, jnp.where(i_at == j_at, diagonal, second))
    at += n_block // 2 * 16

    copy_row = copies_of(pack_ref)
    here = lax.div(entry(copy_row, z * n_o + o), n_walk) == x
    rows = own_ref.shape[0]
    top, bottom = pl.ds(0, rows), pl.ds(rows, rows)
    term_ref[top, :] = jnp.where(here, own_ref[...], walk_ref[...])
    term_ref[bottom, :] = jnp.where(here, orb_ref[...], far_ref[...])
    sum_ref[...] = term_ref[...].astype(jnp.float32)
    for degree in range(1, ORDER + 1):
        product = mm(op_ref[...], term_ref[...])
        term = (product / degree).astype(jnp.bfloat16)
        sum_ref[...] += term.astype(jnp.float32)
        if degree < ORDER:
            term_ref[...] = term
    mine_ref[...] = sum_ref[top, :].astype(jnp.bfloat16)
    other_ref[...] = sum_ref[bottom, :].astype(jnp.bfloat16)

    tail = pl.ds(at, n_both)
    first, cross, inside, inward, kept = (
        joined(ref[tail, :]) for ref in (first_ref, cross_ref, inside_ref, inward_ref, kept_ref)
    )
    factor = (kept + jnp.where(inner, inward, first)) + jnp.where(inner, inside + cross, cross)
    weights_ref[...] = log_weights(copy_row, log_ref[...], factor, x)


def taylor(pack, log_column, arrived, candidates, n_o):
    rows, width = candidates[0].shape
    size = n_o * rows
    out = VMEM((rows, width), jnp.bfloat16)
    return pl.pallas_call(
        partial(taylor_kernel, n_o),
        out_shape=[out, out, VMEM((1, log_column.shape[0] // 2), jnp.float32)],
        in_specs=[in_vmem()] * (2 + len(arrived) + 4),
        out_specs=[in_vmem()] * 3,
        scratch_shapes=[
            VMEM((size, size), jnp.bfloat16),
            VMEM((size, width), jnp.bfloat16),
            VMEM((size, width), jnp.float32),
        ],
        compiler_params=pltpu.CompilerParams(vmem_limit_bytes=VMEM_LIMIT),
        name="taylor",
    )(*on_chip(pack, log_column, *arrived, *candidates))


def place_kernel(steps, n_o, *refs):
    n_line = len(steps)
    pieces, weights_ref = refs[:n_line], refs[n_line]
    out_ref, weights_out, sems = refs[n_line + 1 :]
    z, o = lax.axis_index("vec"), lax.axis_index("orb")
    copies = [
        pltpu.make_async_copy(
            pieces[k],
            out_ref.at[jnp.bitwise_xor(z, dz) * n_o + jnp.bitwise_xor(o, flip)],
            sems.at[k],
        )
        for k, (dz, flip) in enumerate(steps)
    ]
    copies.append(pltpu.make_async_copy(weights_ref, weights_out, sems.at[n_line]))
    for copy in copies:
        copy.start()
    for copy in copies:
        copy.wait()


def put_in_place(steps, pieces, weights, n_o):
    n_line = len(pieces)
    return pl.pallas_call(
        partial(place_kernel, steps, n_o),
        out_shape=[
            jax.ShapeDtypeStruct((n_line,) + pieces[0].shape, pieces[0].dtype),
            jax.ShapeDtypeStruct(weights.shape, weights.dtype),
        ],
        in_specs=[in_vmem()] * (n_line + 1),
        out_specs=[in_hbm()] * 2,
        scratch_shapes=[pltpu.SemaphoreType.DMA((n_line + 1,))],
        compiler_params=pltpu.CompilerParams(vmem_limit_bytes=VMEM_LIMIT),
        name="place",
    )(*on_chip(*pieces, weights))


def swapped(value, axes, sizes, masks):
    perm = []
    for a in range(sizes[0]):
        for b in range(sizes[1]):
            perm.append((a * sizes[1] + b, (a ^ masks[0]) * sizes[1] + (b ^ masks[1])))
    return lax.ppermute(value, axes, perm)


def slot_device(n_z, n_x, n_o, walkers, inv_intersection, trial, vectors, aux_field, log_weight, copy_list):
    line = partial(swapped, axes=("vec", "orb"), sizes=(n_z, n_o))
    near = partial(swapped, axes=("walk", "orb"), sizes=(n_x, n_o))

    others = ((0, 1), (1, 0), (1, 1))
    outer_pairs = [(0, 1), (3, 2)]
    mate = near(vectors, masks=(0, 1))
    own_pack, here = partial_bias_of(
        aux_field, log_weight, copy_list, walkers, inv_intersection, trial, vectors
    )
    packs = [own_pack]
    for m in others:
        packs.append(near(own_pack, masks=m))
    piece, weights, split, log_column = first_piece(packs, here, mate, n_o)
    came = line(piece, masks=(1, 0))
    crossing, nearby, kept, *sources = other_pieces(
        own_pack, packs[2], weights, split, here, mate, walkers, n_o
    )
    inside = lax.ppermute(nearby, "vec", [(1, 2), (2, 1)])
    inward = lax.ppermute(nearby, "vec", outer_pairs)
    across = combined(crossing, came, split.shape[0])
    crossed = line(across, masks=(2, 0))
    candidates = [sources[0]]
    for value, m in zip(sources[1:], others):
        candidates.append(near(value, masks=m))
    mine, other, slot_weights = taylor(
        own_pack, log_column, [kept, came, crossed, inside, inward], candidates, n_o
    )
    steps = [(k, flip) for k in range(n_z) for flip in range(n_o)]
    landed = []
    for dz, flip in steps:
        half = mine if flip == 0 else other
        landed.append(half if (dz, flip) == (0, 0) else line(half, masks=(dz, flip)))
    walkers_out, weights_out = put_in_place(steps, landed, slot_weights, n_o)
    return walkers_out, weights_out[0]


def suits(mesh, walkers, trial, vectors):
    n_z, n_x, n_o = mesh.shape["vec"], mesh.shape["walk"], mesh.shape["orb"]
    per_device = walkers.shape[0] // (mesh.shape["grp"] * n_x)
    local_vectors = vectors.shape[0] // n_z
    return (
        n_o == 2
        and n_x == 2
        and n_z == 4
        and per_device == n_z * n_o
        and local_vectors == per_device
        and vectors.shape[1] == 4 * LANE
        and trial.shape[1] == LANE
    )


def solution(mesh):
    def step(walkers, inv_intersection, trial, vectors, aux_field, log_weight, copy_list):
        if suits(mesh, walkers, trial, vectors):
            body = partial(slot_device, mesh.shape["vec"], mesh.shape["walk"], mesh.shape["orb"])
        else:
            body = general_device
        return jax.shard_map(
            body,
            mesh=mesh,
            in_specs=(
                P(("grp", "walk"), "orb", None),
                P(("grp", "walk"), None, None),
                P(),
                P("vec", "orb", None),
                P(("grp", "walk"), "vec"),
                P(("grp", "walk")),
                P(("grp", "walk")),
            ),
            out_specs=(P(("grp", "walk"), "orb", None), P(("grp", "walk"))),
            check_vma=False,
        )(walkers, inv_intersection, trial, vectors, aux_field, log_weight, copy_list)

    return step
```

```python
from functools import partial
import math

import jax
import jax.numpy as jnp
from jax import lax
from jax.experimental import pallas as pl
from jax.experimental.pallas import tpu as pltpu
from jax.sharding import PartitionSpec as P


ORDER = 6
LANE = 128
VMEM_LIMIT = 24 * 1024 * 1024

step_root = math.sqrt(0.08)

VMEM = pltpu.VMEM


def in_vmem():
    return pl.BlockSpec(memory_space=VMEM)


def in_hbm():
    return pl.BlockSpec(memory_space=pltpu.HBM)


def on_chip(*values):
    return [pltpu.with_memory_space_constraint(value, VMEM) for value in values]


def in_place(*values):
    return [pltpu.with_memory_space_constraint(value, pltpu.HBM) for value in values]


def mm(a, b):
    return jnp.dot(a, b, preferred_element_type=jnp.float32)


def fold_rows(operator, carry, piece, start):
    return jnp.einsum("wnm,wme->wne", operator, piece, preferred_element_type=jnp.float32)


def general_device(walkers, inv_intersection, trial, vectors, aux_field, log_weight, copy_list):
    green = jnp.einsum(
        "wne,wef->wnf", walkers, inv_intersection, preferred_element_type=jnp.float32
    ).astype(jnp.bfloat16)
    mixed = jnp.einsum("gnm,me->gne", vectors, trial, preferred_element_type=jnp.float32).astype(
        jnp.bfloat16
    )
    partial_bias = jnp.einsum("wne,gne->wg", green, mixed, preferred_element_type=jnp.float32)
    bias = lax.psum(partial_bias, "orb")
    shift = -step_root * bias
    field = aux_field - shift
    own_factor = jnp.sum(aux_field * shift - 0.5 * shift * shift, axis=1)
    new_log = log_weight + lax.psum(own_factor, "vec")
    weighted = (field * step_root).astype(jnp.bfloat16)
    local_operator = jnp.einsum(
        "wg,gnm->wnm", weighted, vectors, preferred_element_type=jnp.float32
    )
    operator = lax.psum(local_operator, "vec").astype(jnp.bfloat16)
    running = walkers.astype(jnp.float32)
    folder = partial(fold_rows, operator)
    operand = walkers
    for degree in range(1, ORDER + 1):
        initial = jnp.zeros(running.shape, jnp.float32)
        summed = folder(initial, lax.all_gather(operand, "orb", axis=1, tiled=True), jnp.int32(0))
        new_term = (summed / degree).astype(jnp.bfloat16)
        running = running + new_term.astype(jnp.float32)
        if degree < ORDER:
            operand = new_term
    propagated = running.astype(jnp.bfloat16)
    every_walker = lax.all_gather(propagated, "walk", axis=0, tiled=True)
    every_log = lax.all_gather(new_log, "walk", axis=0, tiled=True)
    return (every_walker[copy_list], every_log[copy_list])


def bias_kernel(aux_hbm, log_hbm, copy_hbm, walkers_hbm, inv_hbm, trial_hbm, vec_hbm, out_ref, vec_ref, quad_ref,
                aux_ref, log_ref, copy_ref, walkers_ref, inv_ref, trial_ref, green_ref, sems):
    n_walk = walkers_hbm.shape[0]
    n_vec = vec_hbm.shape[0]
    copies = [
        pltpu.make_async_copy(source, target, sems.at[i])
        for i, (source, target) in enumerate((
            (walkers_hbm, walkers_ref), (inv_hbm, inv_ref), (trial_hbm, trial_ref),
            (aux_hbm, aux_ref), (log_hbm, log_ref), (copy_hbm, copy_ref),
        ))
    ]
    vec_copies = [
        pltpu.make_async_copy(vec_hbm.at[g], vec_ref.at[g], sems.at[len(copies) + g]) for g in range(n_vec)
    ]
    for copy in copies[:3] + vec_copies + copies[3:]:
        copy.start()
    copies[0].wait()
    copies[1].wait()
    for w in range(n_walk):
        green_ref[w] = mm(walkers_ref[w], inv_ref[w]).astype(jnp.bfloat16).astype(jnp.float32)
    copies[2].wait()
    trial = trial_ref[...]
    n_rows = vec_hbm.shape[1]
    columns = pl.ds(pl.multiple_of(lax.axis_index("orb") * n_rows, n_rows), n_rows)
    lane = lax.broadcasted_iota(jnp.int32, (n_walk, n_vec), 1)
    total = jnp.zeros((n_walk, n_vec), jnp.float32)
    for g in range(n_vec):
        vec_copies[g].wait()
        quad_ref[g] = vec_ref[g, :, columns]
        mixed = mm(vec_ref[g], trial).astype(jnp.bfloat16).astype(jnp.float32)
        rows = [jnp.sum(green_ref[w] * mixed, axis=0, keepdims=True) for w in range(n_walk)]
        column = jnp.sum(jnp.concatenate(rows, axis=0), axis=1, keepdims=True)
        total = total + jnp.where(lane == g, column, 0.0)
    for copy in copies[3:]:
        copy.wait()
    out_ref[pl.ds(0, n_walk), :] = total
    out_ref[pl.ds(n_walk, n_walk), :] = aux_ref[...]
    out_ref[pl.ds(2 * n_walk, n_walk), :] = jnp.zeros((n_walk, n_vec), jnp.float32)
    out_ref[pl.ds(2 * n_walk, 1), :] = log_ref[...]
    out_ref[pl.ds(2 * n_walk + 1, 1), :] = copy_ref[...].astype(jnp.float32)


def partial_bias_of(aux, log_weight, copy_list, walkers, inv, trial, vectors):
    n_walk, n_vec = aux.shape
    log_row, copy_row = log_weight[None, :], copy_list[None, :]
    return pl.pallas_call(
        bias_kernel,
        out_shape=[
            VMEM((3 * n_walk, n_vec), jnp.float32),
            VMEM(vectors.shape, vectors.dtype),
            VMEM((n_vec, vectors.shape[1], vectors.shape[1]), vectors.dtype),
        ],
        in_specs=[in_hbm()] * 7,
        out_specs=[in_vmem()] * 3,
        scratch_shapes=[
            VMEM(aux.shape, aux.dtype),
            VMEM(log_row.shape, log_row.dtype),
            VMEM(copy_row.shape, copy_row.dtype),
            VMEM(walkers.shape, walkers.dtype),
            VMEM(inv.shape, inv.dtype),
            VMEM(trial.shape, trial.dtype),
            VMEM(walkers.shape, jnp.float32),
            pltpu.SemaphoreType.DMA((6 + n_vec,)),
        ],
        compiler_params=pltpu.CompilerParams(vmem_limit_bytes=VMEM_LIMIT),
        name="bias",
    )(*in_place(aux, log_row, copy_row, walkers, inv, trial, vectors))


def copies_of(pack_ref):
    n_walk = pack_ref.shape[0] // 3
    return pack_ref[pl.ds(2 * n_walk + 1, 1), :]


def entry(row, at):
    lane = lax.broadcasted_iota(jnp.int32, row.shape, 1)
    return jnp.sum(jnp.where(lane == at, row, 0.0)).astype(jnp.int32)


def layout(n_block, n_both):
    offsets, at = {}, 0
    for i in range(n_block):
        for j in range(i + 1, n_block):
            offsets[(i, j)] = at
            at += LANE
    for i in range(0, n_block, 2):
        offsets[(i, i)] = at
        at += LANE
    for i in range(1, n_block, 2):
        offsets[(i, i)] = at
        at += 16
    offsets["factor"] = at
    offsets["end"] = at + n_both
    return offsets


def fill_pieces(weights, here_ref, mate_ref, targets, split, o):
    n_vec, n_rows, size = here_ref.shape
    n_block = size // LANE
    in_half = n_rows // LANE
    offsets = layout(n_block, split.shape[0])
    count = len(targets)
    tall = LANE // 2
    splats = [
        [jnp.broadcast_to(weights[k : k + 1, g : g + 1], (tall, LANE)) for g in range(n_vec)]
        for k in range(count)
    ]

    def sums(i, j, step):
        rows = pl.ds(i % in_half * LANE + step * tall, tall)
        if i < in_half:
            column = lax.rem(j + o * in_half, n_block) * LANE
            source, columns = here_ref, pl.ds(pl.multiple_of(column, LANE), LANE)
        else:
            source, columns = mate_ref, pl.ds((j - in_half) * LANE, LANE)
        result = [None] * count
        for g in range(n_vec):
            value = source[g, rows, columns].astype(jnp.float32)
            for k in range(count):
                product = splats[k][g] * value
                result[k] = product if g == 0 else result[k] + product
        return result

    def put(k, offset, count_rows, value):
        targets[k][pl.ds(offset, count_rows), :] = value

    line = lax.broadcasted_iota(jnp.int32, (tall, LANE), 0)
    lane = lax.broadcasted_iota(jnp.int32, (tall, LANE), 1)
    seen = lax.broadcasted_iota(jnp.int32, (16, LANE), 1)
    for pair, offset in offsets.items():
        if isinstance(pair, str):
            continue
        i, j = pair
        if i == j and i % 2 == 1:
            continue
        diagonals = [None] * count
        for step in range(LANE // tall):
            at = offset + step * tall
            upper = sums(i, j, step)
            if i == j:
                row_at = line + step * tall
                lower = sums(i + 1, i + 1, step)
                for k in range(count):
                    found = jnp.sum(jnp.where(row_at == lane, lower[k], 0.0), axis=0, keepdims=True)
                    diagonals[k] = found if step == 0 else diagonals[k] + found
                upper = [jnp.where(row_at <= lane, u, v) for u, v in zip(upper, lower)]
            for k in range(count):
                put(k, at, tall, upper[k].astype(jnp.bfloat16))
        if i == j:
            for k in range(count):
                row = jnp.broadcast_to(diagonals[k], (16, LANE)).astype(jnp.bfloat16)
                put(k, offsets[(i + 1, i + 1)], 16, row)
    for k in range(count):
        put(k, offsets["factor"], split.shape[0], split)


def split_column(column):
    lane = lax.broadcasted_iota(jnp.int32, (column.shape[0], LANE), 1)
    split = jnp.zeros(lane.shape, jnp.float32)
    for i in range(3):
        part = column.astype(jnp.bfloat16).astype(jnp.float32)
        split = jnp.where(lane == i, jnp.broadcast_to(part, lane.shape), split)
        column = column - part
    return split.astype(jnp.bfloat16)


def joined(split):
    wide = split.astype(jnp.float32)
    return (wide[:, 0:1] + wide[:, 1:2]) + wide[:, 2:3]


def routes(z):
    inner = jnp.logical_or(z == 1, z == 2)
    first = jnp.where(lax.rem(z, 2) == 0, 3, 0)
    crossing = jnp.where(z == 0, 2, jnp.where(z == 3, 1, jnp.where(z == 1, 3, 0)))
    nearby = jnp.where(lax.rem(z, 2) == 0, 1, 2)
    return inner, first, crossing, nearby


def first_kernel(n_o, own_ref, orb_ref, walk_ref, far_ref, here_ref, mate_ref,
                 piece_ref, weight_ref, split_ref, log_ref):
    n_walk = own_ref.shape[0] // 3
    z, x, o = lax.axis_index("vec"), lax.axis_index("walk"), lax.axis_index("orb")
    bias = jnp.concatenate(
        [own_ref[pl.ds(0, n_walk), :] + orb_ref[pl.ds(0, n_walk), :],
         walk_ref[pl.ds(0, n_walk), :] + far_ref[pl.ds(0, n_walk), :]], axis=0
    )
    aux = jnp.concatenate([own_ref[pl.ds(n_walk, n_walk), :], walk_ref[pl.ds(n_walk, n_walk), :]], axis=0)
    shift = -step_root * bias
    weighted = ((aux - shift) * step_root).astype(jnp.bfloat16)
    split = split_column(jnp.sum(aux * shift - 0.5 * shift * shift, axis=1, keepdims=True))
    split_ref[...] = split
    _, first, crossing, nearby = routes(z)
    k_at = lax.broadcasted_iota(jnp.int32, (8, n_walk), 0)
    lane = lax.broadcasted_iota(jnp.int32, (8, n_walk), 1)
    to_z = jnp.where(k_at == 0, first, jnp.where(k_at == 1, crossing, jnp.where(k_at == 2, nearby, z)))
    sources = jnp.sum(
        jnp.where(lane == to_z * n_o + o, jnp.broadcast_to(copies_of(own_ref), lane.shape), 0.0),
        axis=1, keepdims=True,
    ).astype(jnp.int32)
    row = lax.rem(sources, n_walk) + n_walk * (lax.div(sources, n_walk) != x).astype(jnp.int32)
    pick = lax.broadcasted_iota(jnp.int32, (8, 2 * n_walk), 1) == row
    weights = mm(pick.astype(jnp.float32).astype(jnp.bfloat16), weighted)
    weight_ref[...] = weights
    fill_pieces(weights, here_ref, mate_ref, [piece_ref], split, o)
    square = (n_walk, n_walk)
    eye = lax.broadcasted_iota(jnp.int32, square, 0) == lax.broadcasted_iota(jnp.int32, square, 1)
    for side, ref in enumerate((own_ref, walk_ref)):
        log_ref[pl.ds(side * n_walk, n_walk), :] = jnp.sum(
            jnp.where(eye, ref[pl.ds(2 * n_walk, 1), :], 0.0), axis=1, keepdims=True
        )


def first_piece(packs, here, mate, n_o):
    n_walk, n_vec = packs[0].shape[0] // 3, packs[0].shape[1]
    return pl.pallas_call(
        partial(first_kernel, n_o),
        out_shape=[
            VMEM((layout(here.shape[2] // LANE, 2 * n_walk)["end"], LANE), jnp.bfloat16),
            VMEM((8, n_vec), jnp.float32),
            VMEM((2 * n_walk, LANE), jnp.bfloat16),
            VMEM((2 * n_walk, 1), jnp.float32),
        ],
        in_specs=[in_vmem()] * 6,
        out_specs=[in_vmem()] * 4,
        compiler_params=pltpu.CompilerParams(vmem_limit_bytes=VMEM_LIMIT),
        name="first_piece",
    )(*on_chip(*packs, here, mate))


def other_kernel(n_o, own_ref, walk_ref, weight_ref, split_ref, here_ref, mate_ref, walkers_hbm, *refs):
    pieces, sources, sems = refs[:3], refs[3:7], refs[7]
    n_walk = walkers_hbm.shape[0]
    z, o = lax.axis_index("vec"), lax.axis_index("orb")
    slot, mate = z * n_o + o, z * n_o + (n_o - 1 - o)
    own_list, far_list = copies_of(own_ref), copies_of(walk_ref)
    wanted = ((own_list, slot), (own_list, mate), (far_list, slot), (far_list, mate))
    copies = [
        pltpu.make_async_copy(walkers_hbm.at[lax.rem(entry(row, at), n_walk)], out, sems.at[i])
        for i, ((row, at), out) in enumerate(zip(wanted, sources))
    ]
    for copy in copies:
        copy.start()
    fill_pieces(weight_ref[...][1:4], here_ref, mate_ref, pieces, split_ref[...], o)
    for copy in copies:
        copy.wait()


def other_pieces(own_pack, walk_pack, weights, split, here, mate, walkers, n_o):
    offsets = layout(here.shape[2] // LANE, split.shape[0])
    piece = VMEM((offsets["end"], LANE), jnp.bfloat16)
    source = VMEM(walkers.shape[1:], walkers.dtype)
    return pl.pallas_call(
        partial(other_kernel, n_o),
        out_shape=[piece] * 3 + [source] * 4,
        in_specs=[in_vmem()] * 6 + [in_hbm()],
        out_specs=[in_vmem()] * 7,
        scratch_shapes=[pltpu.SemaphoreType.DMA((4,))],
        compiler_params=pltpu.CompilerParams(vmem_limit_bytes=VMEM_LIMIT),
        name="other_pieces",
    )(*on_chip(own_pack, walk_pack, weights, split, here, mate), *in_place(walkers))


def combine_kernel(body, far_ref, near_ref, came_ref, out_ref):
    inner = routes(lax.axis_index("vec"))[0]

    @pl.when(inner)
    def _():
        for low in range(0, body, LANE):
            rows = pl.ds(low, min(LANE, body - low))
            value = far_ref[rows, :].astype(jnp.float32) + came_ref[rows, :].astype(jnp.float32)
            out_ref[rows, :] = value.astype(jnp.bfloat16)
        tail = pl.ds(body, out_ref.shape[0] - body)
        out_ref[tail, :] = split_column(joined(far_ref[tail, :]) + joined(came_ref[tail, :]))

    @pl.when(jnp.logical_not(inner))
    def _():
        out_ref[...] = near_ref[...]


def combined(far, nearby, came, n_both):
    return pl.pallas_call(
        partial(combine_kernel, came.shape[0] - n_both),
        out_shape=VMEM(came.shape, came.dtype),
        in_specs=[in_vmem()] * 3,
        out_specs=in_vmem(),
        compiler_params=pltpu.CompilerParams(vmem_limit_bytes=VMEM_LIMIT),
        name="combine",
    )(*on_chip(far, nearby, came))


def log_weights(copy_row, log_column, total, x):
    n_walk = log_column.shape[0] // 2
    new_log = log_column + total
    source = copy_row.astype(jnp.int32)
    row = lax.rem(source, n_walk) + n_walk * (lax.div(source, n_walk) != x).astype(jnp.int32)
    shape = (2 * n_walk, copy_row.shape[1])
    at = lax.broadcasted_iota(jnp.int32, shape, 0)
    chosen = jnp.where(at == jnp.broadcast_to(row, shape), jnp.broadcast_to(new_log, shape), 0.0)
    return jnp.sum(chosen, axis=0, keepdims=True)


def taylor_kernel(n_o, pack_ref, log_ref, kept_ref, first_ref, inside_ref, cross_ref, last_ref, own_ref, orb_ref, walk_ref, far_ref,
                  mine_ref, other_ref, weights_ref, op_ref, term_ref, sum_ref):
    z, x, o = lax.axis_index("vec"), lax.axis_index("walk"), lax.axis_index("orb")
    inner = routes(z)[0]
    n_both = log_ref.shape[0]
    n_walk = n_both // 2
    n_block = op_ref.shape[0] // LANE
    offsets = layout(n_block, n_both)
    i_at = lax.broadcasted_iota(jnp.int32, (LANE, LANE), 0)
    j_at = lax.broadcasted_iota(jnp.int32, (LANE, LANE), 1)

    def terms(offset, count):
        rows = pl.ds(offset, count)
        return (ref[rows, :] for ref in (kept_ref, first_ref, inside_ref, cross_ref, last_ref))

    def total(offset, count):
        kept, first, inside, cross, last = (value.astype(jnp.float32) for value in terms(offset, count))
        return (kept + last) + jnp.where(inner, inside + cross, first)

    def put(i, j, value):
        op_ref[pl.ds(i * LANE, LANE), pl.ds(j * LANE, LANE)] = value.astype(jnp.bfloat16)

    for i in range(n_block):
        for j in range(i + 1, n_block):
            value = total(offsets[(i, j)], LANE)
            put(i, j, value)
            put(j, i, value.T)
    for i in range(0, n_block, 2):
        merged = total(offsets[(i, i)], LANE)
        diagonal = total(offsets[(i + 1, i + 1)], 16)[:1]
        turned = merged.T
        put(i, i, jnp.where(i_at <= j_at, merged, turned))
        second = jnp.where(i_at > j_at, merged, turned)
        put(i + 1, i + 1, jnp.where(i_at == j_at, diagonal, second))

    copy_row = copies_of(pack_ref)
    here = lax.div(entry(copy_row, z * n_o + o), n_walk) == x
    rows = own_ref.shape[0]
    top, bottom = pl.ds(0, rows), pl.ds(rows, rows)
    term_ref[top, :] = jnp.where(here, own_ref[...], walk_ref[...])
    term_ref[bottom, :] = jnp.where(here, orb_ref[...], far_ref[...])
    sum_ref[...] = term_ref[...].astype(jnp.float32)
    for degree in range(1, ORDER + 1):
        product = mm(op_ref[...], term_ref[...])
        term = (product / degree).astype(jnp.bfloat16)
        sum_ref[...] += term.astype(jnp.float32)
        if degree < ORDER:
            term_ref[...] = term
    mine_ref[...] = sum_ref[top, :].astype(jnp.bfloat16)
    other_ref[...] = sum_ref[bottom, :].astype(jnp.bfloat16)

    kept, first, inside, cross, last = (joined(value) for value in terms(offsets["factor"], n_both))
    factor = (kept + jnp.where(inner, last, first)) + jnp.where(inner, inside + cross, last)
    weights_ref[...] = log_weights(copy_row, log_ref[...], factor, x)


def taylor(pack, log_column, arrived, candidates, n_o):
    rows, width = candidates[0].shape
    size = n_o * rows
    out = VMEM((rows, width), jnp.bfloat16)
    return pl.pallas_call(
        partial(taylor_kernel, n_o),
        out_shape=[out, out, VMEM((1, log_column.shape[0] // 2), jnp.float32)],
        in_specs=[in_vmem()] * (2 + len(arrived) + 4),
        out_specs=[in_vmem()] * 3,
        scratch_shapes=[
            VMEM((size, size), jnp.bfloat16),
            VMEM((size, width), jnp.bfloat16),
            VMEM((size, width), jnp.float32),
        ],
        compiler_params=pltpu.CompilerParams(vmem_limit_bytes=VMEM_LIMIT),
        name="taylor",
    )(*on_chip(pack, log_column, *arrived, *candidates))


def place_kernel(steps, n_o, *refs):
    n_line = len(steps)
    pieces, weights_ref = refs[:n_line], refs[n_line]
    out_ref, weights_out, sems = refs[n_line + 1 :]
    z, o = lax.axis_index("vec"), lax.axis_index("orb")
    copies = [
        pltpu.make_async_copy(
            pieces[k],
            out_ref.at[jnp.bitwise_xor(z, dz) * n_o + jnp.bitwise_xor(o, flip)],
            sems.at[k],
        )
        for k, (dz, flip) in enumerate(steps)
    ]
    copies.append(pltpu.make_async_copy(weights_ref, weights_out, sems.at[n_line]))
    for copy in copies:
        copy.start()
    for copy in copies:
        copy.wait()


def put_in_place(steps, pieces, weights, n_o):
    n_line = len(pieces)
    return pl.pallas_call(
        partial(place_kernel, steps, n_o),
        out_shape=[
            jax.ShapeDtypeStruct((n_line,) + pieces[0].shape, pieces[0].dtype),
            jax.ShapeDtypeStruct(weights.shape, weights.dtype),
        ],
        in_specs=[in_vmem()] * (n_line + 1),
        out_specs=[in_hbm()] * 2,
        scratch_shapes=[pltpu.SemaphoreType.DMA((n_line + 1,))],
        compiler_params=pltpu.CompilerParams(vmem_limit_bytes=VMEM_LIMIT),
        name="place",
    )(*on_chip(*pieces, weights))


def swapped(value, axes, sizes, masks):
    perm = []
    for a in range(sizes[0]):
        for b in range(sizes[1]):
            perm.append((a * sizes[1] + b, (a ^ masks[0]) * sizes[1] + (b ^ masks[1])))
    return lax.ppermute(value, axes, perm)


def slot_device(n_z, n_x, n_o, walkers, inv_intersection, trial, vectors, aux_field, log_weight, copy_list):
    line = partial(swapped, axes=("vec", "orb"), sizes=(n_z, n_o))
    near = partial(swapped, axes=("walk", "orb"), sizes=(n_x, n_o))

    others = ((0, 1), (1, 0), (1, 1))
    own_pack, here, quadrant = partial_bias_of(
        aux_field, log_weight, copy_list, walkers, inv_intersection, trial, vectors
    )
    packs = [own_pack]
    for m in others:
        packs.append(near(own_pack, masks=m))
    mate = near(quadrant, masks=(0, 1))
    piece, weights, split, log_column = first_piece(packs, here, mate, n_o)
    came = line(piece, masks=(1, 0))
    crossing, nearby, kept, *sources = other_pieces(
        own_pack, packs[2], weights, split, here, mate, walkers, n_o
    )
    inside = lax.ppermute(nearby, "vec", [(0, 0), (1, 2), (2, 1), (3, 3)])
    crossed = lax.ppermute(crossing, "vec", [(0, 2), (3, 1), (1, 0), (2, 3)])
    passed = combined(crossing, nearby, came, split.shape[0])
    last = lax.ppermute(passed, "vec", [(0, 1), (1, 3), (2, 0), (3, 2)])
    candidates = [sources[0]]
    for value, m in zip(sources[1:], others):
        candidates.append(near(value, masks=m))
    mine, other, slot_weights = taylor(
        own_pack, log_column, [kept, came, inside, crossed, last], candidates, n_o
    )
    steps = [(k, flip) for k in range(n_z) for flip in range(n_o)]
    landed = []
    for dz, flip in steps:
        half = mine if flip == 0 else other
        landed.append(half if (dz, flip) == (0, 0) else line(half, masks=(dz, flip)))
    walkers_out, weights_out = put_in_place(steps, landed, slot_weights, n_o)
    return walkers_out, weights_out[0]


def suits(mesh, walkers, trial, vectors):
    n_z, n_x, n_o = mesh.shape["vec"], mesh.shape["walk"], mesh.shape["orb"]
    per_device = walkers.shape[0] // (mesh.shape["grp"] * n_x)
    local_vectors = vectors.shape[0] // n_z
    return (
        n_o == 2
        and n_x == 2
        and n_z == 4
        and per_device == n_z * n_o
        and local_vectors == per_device
        and vectors.shape[1] == 4 * LANE
        and trial.shape[1] == LANE
    )


def solution(mesh):
    def step(walkers, inv_intersection, trial, vectors, aux_field, log_weight, copy_list):
        if suits(mesh, walkers, trial, vectors):
            body = partial(slot_device, mesh.shape["vec"], mesh.shape["walk"], mesh.shape["orb"])
        else:
            body = general_device
        return jax.shard_map(
            body,
            mesh=mesh,
            in_specs=(
                P(("grp", "walk"), "orb", None),
                P(("grp", "walk"), None, None),
                P(),
                P("vec", "orb", None),
                P(("grp", "walk"), "vec"),
                P(("grp", "walk")),
                P(("grp", "walk")),
            ),
            out_specs=(P(("grp", "walk"), "orb", None), P(("grp", "walk"))),
            check_vma=False,
        )(walkers, inv_intersection, trial, vectors, aux_field, log_weight, copy_list)

    return step
```

```python
from functools import partial
import math

import jax
import jax.numpy as jnp
from jax import lax
from jax.experimental import pallas as pl
from jax.experimental.pallas import tpu as pltpu
from jax.sharding import PartitionSpec as P


ORDER = 6
LANE = 128
VMEM_LIMIT = 24 * 1024 * 1024

step_root = math.sqrt(0.08)

VMEM = pltpu.VMEM


def in_vmem():
    return pl.BlockSpec(memory_space=VMEM)


def in_hbm():
    return pl.BlockSpec(memory_space=pltpu.HBM)


def on_chip(*values):
    return [pltpu.with_memory_space_constraint(value, VMEM) for value in values]


def in_place(*values):
    return [pltpu.with_memory_space_constraint(value, pltpu.HBM) for value in values]


def mm(a, b):
    return jnp.dot(a, b, preferred_element_type=jnp.float32)


def fold_rows(operator, carry, piece, start):
    return jnp.einsum("wnm,wme->wne", operator, piece, preferred_element_type=jnp.float32)


def general_device(walkers, inv_intersection, trial, vectors, aux_field, log_weight, copy_list):
    green = jnp.einsum(
        "wne,wef->wnf", walkers, inv_intersection, preferred_element_type=jnp.float32
    ).astype(jnp.bfloat16)
    mixed = jnp.einsum("gnm,me->gne", vectors, trial, preferred_element_type=jnp.float32).astype(
        jnp.bfloat16
    )
    partial_bias = jnp.einsum("wne,gne->wg", green, mixed, preferred_element_type=jnp.float32)
    bias = lax.psum(partial_bias, "orb")
    shift = -step_root * bias
    field = aux_field - shift
    own_factor = jnp.sum(aux_field * shift - 0.5 * shift * shift, axis=1)
    new_log = log_weight + lax.psum(own_factor, "vec")
    weighted = (field * step_root).astype(jnp.bfloat16)
    local_operator = jnp.einsum(
        "wg,gnm->wnm", weighted, vectors, preferred_element_type=jnp.float32
    )
    operator = lax.psum(local_operator, "vec").astype(jnp.bfloat16)
    running = walkers.astype(jnp.float32)
    folder = partial(fold_rows, operator)
    operand = walkers
    for degree in range(1, ORDER + 1):
        initial = jnp.zeros(running.shape, jnp.float32)
        summed = folder(initial, lax.all_gather(operand, "orb", axis=1, tiled=True), jnp.int32(0))
        new_term = (summed / degree).astype(jnp.bfloat16)
        running = running + new_term.astype(jnp.float32)
        if degree < ORDER:
            operand = new_term
    propagated = running.astype(jnp.bfloat16)
    every_walker = lax.all_gather(propagated, "walk", axis=0, tiled=True)
    every_log = lax.all_gather(new_log, "walk", axis=0, tiled=True)
    return (every_walker[copy_list], every_log[copy_list])


def bias_kernel(aux_hbm, log_hbm, copy_hbm, walkers_hbm, inv_hbm, trial_hbm, vec_hbm, out_ref, vec_ref, quad_ref,
                aux_ref, log_ref, copy_ref, walkers_ref, inv_ref, trial_ref, green_ref, sems):
    n_walk = walkers_hbm.shape[0]
    n_vec = vec_hbm.shape[0]
    copies = [
        pltpu.make_async_copy(source, target, sems.at[i])
        for i, (source, target) in enumerate((
            (walkers_hbm, walkers_ref), (inv_hbm, inv_ref), (trial_hbm, trial_ref),
            (aux_hbm, aux_ref), (log_hbm, log_ref), (copy_hbm, copy_ref),
        ))
    ]
    vec_copies = [
        pltpu.make_async_copy(vec_hbm.at[g], vec_ref.at[g], sems.at[len(copies) + g]) for g in range(n_vec)
    ]
    for copy in copies[:3] + vec_copies + copies[3:]:
        copy.start()
    copies[0].wait()
    copies[1].wait()
    for w in range(n_walk):
        green_ref[w] = mm(walkers_ref[w], inv_ref[w]).astype(jnp.bfloat16).astype(jnp.float32)
    copies[2].wait()
    trial = trial_ref[...]
    n_rows = vec_hbm.shape[1]
    columns = pl.ds(pl.multiple_of(lax.axis_index("orb") * n_rows, n_rows), n_rows)
    lane = lax.broadcasted_iota(jnp.int32, (n_walk, n_vec), 1)
    total = jnp.zeros((n_walk, n_vec), jnp.float32)
    vec_copies[0].wait()
    ahead = mm(vec_ref[0], trial)
    for g in range(n_vec):
        mixed = ahead.astype(jnp.bfloat16).astype(jnp.float32)
        if g + 1 < n_vec:
            vec_copies[g + 1].wait()
            ahead = mm(vec_ref[g + 1], trial)
        quad_ref[g] = vec_ref[g, :, columns]
        rows = [jnp.sum(green_ref[w] * mixed, axis=0, keepdims=True) for w in range(n_walk)]
        column = jnp.sum(jnp.concatenate(rows, axis=0), axis=1, keepdims=True)
        total = total + jnp.where(lane == g, column, 0.0)
    for copy in copies[3:]:
        copy.wait()
    out_ref[pl.ds(0, n_walk), :] = total
    out_ref[pl.ds(n_walk, n_walk), :] = aux_ref[...]
    out_ref[pl.ds(2 * n_walk, n_walk), :] = jnp.zeros((n_walk, n_vec), jnp.float32)
    out_ref[pl.ds(2 * n_walk, 1), :] = log_ref[...]
    out_ref[pl.ds(2 * n_walk + 1, 1), :] = copy_ref[...].astype(jnp.float32)


def partial_bias_of(aux, log_weight, copy_list, walkers, inv, trial, vectors):
    n_walk, n_vec = aux.shape
    log_row, copy_row = log_weight[None, :], copy_list[None, :]
    return pl.pallas_call(
        bias_kernel,
        out_shape=[
            VMEM((3 * n_walk, n_vec), jnp.float32),
            VMEM(vectors.shape, vectors.dtype),
            VMEM((n_vec, vectors.shape[1], vectors.shape[1]), vectors.dtype),
        ],
        in_specs=[in_hbm()] * 7,
        out_specs=[in_vmem()] * 3,
        scratch_shapes=[
            VMEM(aux.shape, aux.dtype),
            VMEM(log_row.shape, log_row.dtype),
            VMEM(copy_row.shape, copy_row.dtype),
            VMEM(walkers.shape, walkers.dtype),
            VMEM(inv.shape, inv.dtype),
            VMEM(trial.shape, trial.dtype),
            VMEM(walkers.shape, jnp.float32),
            pltpu.SemaphoreType.DMA((6 + n_vec,)),
        ],
        compiler_params=pltpu.CompilerParams(vmem_limit_bytes=VMEM_LIMIT),
        name="bias",
    )(*in_place(aux, log_row, copy_row, walkers, inv, trial, vectors))


def copies_of(pack_ref):
    n_walk = pack_ref.shape[0] // 3
    return pack_ref[pl.ds(2 * n_walk + 1, 1), :]


def entry(row, at):
    lane = lax.broadcasted_iota(jnp.int32, row.shape, 1)
    return jnp.sum(jnp.where(lane == at, row, 0.0)).astype(jnp.int32)


def layout(n_block, n_both):
    offsets, at = {}, 0
    for i in range(n_block):
        for j in range(i + 1, n_block):
            offsets[(i, j)] = at
            at += LANE
    for i in range(0, n_block, 2):
        offsets[(i, i)] = at
        at += LANE
    for i in range(1, n_block, 2):
        offsets[(i, i)] = at
        at += 16
    offsets["factor"] = at
    offsets["end"] = at + n_both
    return offsets


def fill_pieces(weights, here_ref, mate_ref, targets, split, o):
    n_vec, n_rows, size = here_ref.shape
    n_block = size // LANE
    in_half = n_rows // LANE
    offsets = layout(n_block, split.shape[0])
    count = len(targets)
    tall = LANE // 2
    splats = [
        [jnp.broadcast_to(weights[k : k + 1, g : g + 1], (tall, LANE)) for g in range(n_vec)]
        for k in range(count)
    ]

    def sums(i, j, step):
        rows = pl.ds(i % in_half * LANE + step * tall, tall)
        if i < in_half:
            column = lax.rem(j + o * in_half, n_block) * LANE
            source, columns = here_ref, pl.ds(pl.multiple_of(column, LANE), LANE)
        else:
            source, columns = mate_ref, pl.ds((j - in_half) * LANE, LANE)
        result = [None] * count
        for g in range(n_vec):
            value = source[g, rows, columns].astype(jnp.float32)
            for k in range(count):
                product = splats[k][g] * value
                result[k] = product if g == 0 else result[k] + product
        return result

    def put(k, offset, count_rows, value):
        targets[k][pl.ds(offset, count_rows), :] = value

    line = lax.broadcasted_iota(jnp.int32, (tall, LANE), 0)
    lane = lax.broadcasted_iota(jnp.int32, (tall, LANE), 1)
    seen = lax.broadcasted_iota(jnp.int32, (16, LANE), 1)
    for pair, offset in offsets.items():
        if isinstance(pair, str):
            continue
        i, j = pair
        if i == j and i % 2 == 1:
            continue
        diagonals = [None] * count
        for step in range(LANE // tall):
            at = offset + step * tall
            upper = sums(i, j, step)
            if i == j:
                row_at = line + step * tall
                lower = sums(i + 1, i + 1, step)
                for k in range(count):
                    found = jnp.sum(jnp.where(row_at == lane, lower[k], 0.0), axis=0, keepdims=True)
                    diagonals[k] = found if step == 0 else diagonals[k] + found
                upper = [jnp.where(row_at <= lane, u, v) for u, v in zip(upper, lower)]
            for k in range(count):
                put(k, at, tall, upper[k].astype(jnp.bfloat16))
        if i == j:
            for k in range(count):
                row = jnp.broadcast_to(diagonals[k], (16, LANE)).astype(jnp.bfloat16)
                put(k, offsets[(i + 1, i + 1)], 16, row)
    for k in range(count):
        put(k, offsets["factor"], split.shape[0], split)


def split_column(column):
    lane = lax.broadcasted_iota(jnp.int32, (column.shape[0], LANE), 1)
    split = jnp.zeros(lane.shape, jnp.float32)
    for i in range(3):
        part = column.astype(jnp.bfloat16).astype(jnp.float32)
        split = jnp.where(lane == i, jnp.broadcast_to(part, lane.shape), split)
        column = column - part
    return split.astype(jnp.bfloat16)


def joined(split):
    wide = split.astype(jnp.float32)
    return (wide[:, 0:1] + wide[:, 1:2]) + wide[:, 2:3]


def routes(z):
    inner = jnp.logical_or(z == 1, z == 2)
    first = jnp.where(lax.rem(z, 2) == 0, 3, 0)
    crossing = jnp.where(z == 0, 2, jnp.where(z == 3, 1, jnp.where(z == 1, 3, 0)))
    nearby = jnp.where(lax.rem(z, 2) == 0, 1, 2)
    return inner, first, crossing, nearby


def first_kernel(n_o, own_ref, walk_ref, here_ref, mate_ref,
                 first_ref, near_ref, weight_ref, split_ref, log_ref):
    n_walk = own_ref.shape[0] // 3
    z, x, o = lax.axis_index("vec"), lax.axis_index("walk"), lax.axis_index("orb")
    bias = jnp.concatenate(
        [own_ref[pl.ds(0, n_walk), :], walk_ref[pl.ds(0, n_walk), :]], axis=0
    )
    aux = jnp.concatenate([own_ref[pl.ds(n_walk, n_walk), :], walk_ref[pl.ds(n_walk, n_walk), :]], axis=0)
    shift = -step_root * bias
    weighted = ((aux - shift) * step_root).astype(jnp.bfloat16)
    split = split_column(jnp.sum(aux * shift - 0.5 * shift * shift, axis=1, keepdims=True))
    split_ref[...] = split
    _, first, crossing, nearby = routes(z)
    k_at = lax.broadcasted_iota(jnp.int32, (8, n_walk), 0)
    lane = lax.broadcasted_iota(jnp.int32, (8, n_walk), 1)
    to_z = jnp.where(k_at == 0, first, jnp.where(k_at == 1, nearby, jnp.where(k_at == 2, crossing, z)))
    sources = jnp.sum(
        jnp.where(lane == to_z * n_o + o, jnp.broadcast_to(copies_of(own_ref), lane.shape), 0.0),
        axis=1, keepdims=True,
    ).astype(jnp.int32)
    row = lax.rem(sources, n_walk) + n_walk * (lax.div(sources, n_walk) != x).astype(jnp.int32)
    pick = lax.broadcasted_iota(jnp.int32, (8, 2 * n_walk), 1) == row
    weights = mm(pick.astype(jnp.float32).astype(jnp.bfloat16), weighted)
    weight_ref[...] = weights
    fill_pieces(weights, here_ref, mate_ref, [first_ref, near_ref], split, o)
    square = (n_walk, n_walk)
    eye = lax.broadcasted_iota(jnp.int32, square, 0) == lax.broadcasted_iota(jnp.int32, square, 1)
    for side, ref in enumerate((own_ref, walk_ref)):
        log_ref[pl.ds(side * n_walk, n_walk), :] = jnp.sum(
            jnp.where(eye, ref[pl.ds(2 * n_walk, 1), :], 0.0), axis=1, keepdims=True
        )


def sum_kernel(own_ref, orb_ref, out_ref):
    n_walk = own_ref.shape[0] // 3
    out_ref[...] = own_ref[...]
    out_ref[pl.ds(0, n_walk), :] = own_ref[pl.ds(0, n_walk), :] + orb_ref[pl.ds(0, n_walk), :]


def summed_pack(own, orb):
    return pl.pallas_call(
        sum_kernel,
        out_shape=VMEM(own.shape, own.dtype),
        in_specs=[in_vmem()] * 2,
        out_specs=in_vmem(),
        compiler_params=pltpu.CompilerParams(vmem_limit_bytes=VMEM_LIMIT),
        name="summed_pack",
    )(*on_chip(own, orb))


def first_pieces(packs, here, mate, n_o):
    n_walk, n_vec = packs[0].shape[0] // 3, packs[0].shape[1]
    return pl.pallas_call(
        partial(first_kernel, n_o),
        out_shape=[VMEM((layout(here.shape[2] // LANE, 2 * n_walk)["end"], LANE), jnp.bfloat16)] * 2 + [
            VMEM((8, n_vec), jnp.float32),
            VMEM((2 * n_walk, LANE), jnp.bfloat16),
            VMEM((2 * n_walk, 1), jnp.float32),
        ],
        in_specs=[in_vmem()] * 4,
        out_specs=[in_vmem()] * 5,
        compiler_params=pltpu.CompilerParams(vmem_limit_bytes=VMEM_LIMIT),
        name="first_piece",
    )(*on_chip(*packs, here, mate))


def other_kernel(n_o, own_ref, walk_ref, weight_ref, split_ref, here_ref, mate_ref, walkers_hbm, *refs):
    pieces, sources, sems = refs[:2], refs[2:6], refs[6]
    n_walk = walkers_hbm.shape[0]
    z, o = lax.axis_index("vec"), lax.axis_index("orb")
    slot, mate = z * n_o + o, z * n_o + (n_o - 1 - o)
    own_list, far_list = copies_of(own_ref), copies_of(walk_ref)
    wanted = ((own_list, slot), (own_list, mate), (far_list, slot), (far_list, mate))
    copies = [
        pltpu.make_async_copy(walkers_hbm.at[lax.rem(entry(row, at), n_walk)], out, sems.at[i])
        for i, ((row, at), out) in enumerate(zip(wanted, sources))
    ]
    for copy in copies:
        copy.start()
    fill_pieces(weight_ref[...][2:4], here_ref, mate_ref, pieces, split_ref[...], o)
    for copy in copies:
        copy.wait()


def other_pieces(own_pack, walk_pack, weights, split, here, mate, walkers, n_o):
    offsets = layout(here.shape[2] // LANE, split.shape[0])
    piece = VMEM((offsets["end"], LANE), jnp.bfloat16)
    source = VMEM(walkers.shape[1:], walkers.dtype)
    return pl.pallas_call(
        partial(other_kernel, n_o),
        out_shape=[piece] * 2 + [source] * 4,
        in_specs=[in_vmem()] * 6 + [in_hbm()],
        out_specs=[in_vmem()] * 6,
        scratch_shapes=[pltpu.SemaphoreType.DMA((4,))],
        compiler_params=pltpu.CompilerParams(vmem_limit_bytes=VMEM_LIMIT),
        name="other_pieces",
    )(*on_chip(own_pack, walk_pack, weights, split, here, mate), *in_place(walkers))


def combine_kernel(body, far_ref, near_ref, came_ref, out_ref):
    inner = routes(lax.axis_index("vec"))[0]

    @pl.when(inner)
    def _():
        for low in range(0, body, LANE):
            rows = pl.ds(low, min(LANE, body - low))
            value = far_ref[rows, :].astype(jnp.float32) + came_ref[rows, :].astype(jnp.float32)
            out_ref[rows, :] = value.astype(jnp.bfloat16)
        tail = pl.ds(body, out_ref.shape[0] - body)
        out_ref[tail, :] = split_column(joined(far_ref[tail, :]) + joined(came_ref[tail, :]))

    @pl.when(jnp.logical_not(inner))
    def _():
        out_ref[...] = near_ref[...]


def combined(far, nearby, came, n_both):
    return pl.pallas_call(
        partial(combine_kernel, came.shape[0] - n_both),
        out_shape=VMEM(came.shape, came.dtype),
        in_specs=[in_vmem()] * 3,
        out_specs=in_vmem(),
        compiler_params=pltpu.CompilerParams(vmem_limit_bytes=VMEM_LIMIT),
        name="combine",
    )(*on_chip(far, nearby, came))


def log_weights(copy_row, log_column, total, x):
    n_walk = log_column.shape[0] // 2
    new_log = log_column + total
    source = copy_row.astype(jnp.int32)
    row = lax.rem(source, n_walk) + n_walk * (lax.div(source, n_walk) != x).astype(jnp.int32)
    shape = (2 * n_walk, copy_row.shape[1])
    at = lax.broadcasted_iota(jnp.int32, shape, 0)
    chosen = jnp.where(at == jnp.broadcast_to(row, shape), jnp.broadcast_to(new_log, shape), 0.0)
    return jnp.sum(chosen, axis=0, keepdims=True)


def taylor_kernel(n_o, pack_ref, log_ref, kept_ref, first_ref, inside_ref, cross_ref, last_ref, own_ref, orb_ref, walk_ref, far_ref,
                  mine_ref, other_ref, weights_ref, op_ref, term_ref, sum_ref):
    z, x, o = lax.axis_index("vec"), lax.axis_index("walk"), lax.axis_index("orb")
    inner = routes(z)[0]
    n_both = log_ref.shape[0]
    n_walk = n_both // 2
    n_block = op_ref.shape[0] // LANE
    offsets = layout(n_block, n_both)
    i_at = lax.broadcasted_iota(jnp.int32, (LANE, LANE), 0)
    j_at = lax.broadcasted_iota(jnp.int32, (LANE, LANE), 1)

    def terms(offset, count):
        rows = pl.ds(offset, count)
        return (ref[rows, :] for ref in (kept_ref, first_ref, inside_ref, cross_ref, last_ref))

    def total(offset, count):
        kept, first, inside, cross, last = (value.astype(jnp.float32) for value in terms(offset, count))
        return (kept + last) + jnp.where(inner, inside + cross, first)

    def put(i, j, value):
        op_ref[pl.ds(i * LANE, LANE), pl.ds(j * LANE, LANE)] = value.astype(jnp.bfloat16)

    for i in range(n_block):
        for j in range(i + 1, n_block):
            value = total(offsets[(i, j)], LANE)
            put(i, j, value)
            put(j, i, value.T)
    for i in range(0, n_block, 2):
        merged = total(offsets[(i, i)], LANE)
        diagonal = total(offsets[(i + 1, i + 1)], 16)[:1]
        turned = merged.T
        put(i, i, jnp.where(i_at <= j_at, merged, turned))
        second = jnp.where(i_at > j_at, merged, turned)
        put(i + 1, i + 1, jnp.where(i_at == j_at, diagonal, second))

    copy_row = copies_of(pack_ref)
    here = lax.div(entry(copy_row, z * n_o + o), n_walk) == x
    rows = own_ref.shape[0]
    top, bottom = pl.ds(0, rows), pl.ds(rows, rows)
    term_ref[top, :] = jnp.where(here, own_ref[...], walk_ref[...])
    term_ref[bottom, :] = jnp.where(here, orb_ref[...], far_ref[...])
    sum_ref[...] = term_ref[...].astype(jnp.float32)
    for degree in range(1, ORDER + 1):
        product = mm(op_ref[...], term_ref[...])
        term = (product / degree).astype(jnp.bfloat16)
        sum_ref[...] += term.astype(jnp.float32)
        if degree < ORDER:
            term_ref[...] = term
    mine_ref[...] = sum_ref[top, :].astype(jnp.bfloat16)
    other_ref[...] = sum_ref[bottom, :].astype(jnp.bfloat16)

    kept, first, inside, cross, last = (joined(value) for value in terms(offsets["factor"], n_both))
    factor = (kept + jnp.where(inner, last, first)) + jnp.where(inner, inside + cross, last)
    weights_ref[...] = log_weights(copy_row, log_ref[...], factor, x)


def taylor(pack, log_column, arrived, candidates, n_o):
    rows, width = candidates[0].shape
    size = n_o * rows
    out = VMEM((rows, width), jnp.bfloat16)
    return pl.pallas_call(
        partial(taylor_kernel, n_o),
        out_shape=[out, out, VMEM((1, log_column.shape[0] // 2), jnp.float32)],
        in_specs=[in_vmem()] * (2 + len(arrived) + 4),
        out_specs=[in_vmem()] * 3,
        scratch_shapes=[
            VMEM((size, size), jnp.bfloat16),
            VMEM((size, width), jnp.bfloat16),
            VMEM((size, width), jnp.float32),
        ],
        compiler_params=pltpu.CompilerParams(vmem_limit_bytes=VMEM_LIMIT),
        name="taylor",
    )(*on_chip(pack, log_column, *arrived, *candidates))


def place_kernel(steps, n_o, *refs):
    n_line = len(steps)
    pieces, weights_ref = refs[:n_line], refs[n_line]
    out_ref, weights_out, sems = refs[n_line + 1 :]
    z, o = lax.axis_index("vec"), lax.axis_index("orb")
    copies = [
        pltpu.make_async_copy(
            pieces[k],
            out_ref.at[jnp.bitwise_xor(z, dz) * n_o + jnp.bitwise_xor(o, flip)],
            sems.at[k],
        )
        for k, (dz, flip) in enumerate(steps)
    ]
    copies.append(pltpu.make_async_copy(weights_ref, weights_out, sems.at[n_line]))
    for copy in copies:
        copy.start()
    for copy in copies:
        copy.wait()


def put_in_place(steps, pieces, weights, n_o):
    n_line = len(pieces)
    return pl.pallas_call(
        partial(place_kernel, steps, n_o),
        out_shape=[
            jax.ShapeDtypeStruct((n_line,) + pieces[0].shape, pieces[0].dtype),
            jax.ShapeDtypeStruct(weights.shape, weights.dtype),
        ],
        in_specs=[in_vmem()] * (n_line + 1),
        out_specs=[in_hbm()] * 2,
        scratch_shapes=[pltpu.SemaphoreType.DMA((n_line + 1,))],
        compiler_params=pltpu.CompilerParams(vmem_limit_bytes=VMEM_LIMIT),
        name="place",
    )(*on_chip(*pieces, weights))


def swapped(value, axes, sizes, masks):
    perm = []
    for a in range(sizes[0]):
        for b in range(sizes[1]):
            perm.append((a * sizes[1] + b, (a ^ masks[0]) * sizes[1] + (b ^ masks[1])))
    return lax.ppermute(value, axes, perm)


def slot_device(n_z, n_x, n_o, walkers, inv_intersection, trial, vectors, aux_field, log_weight, copy_list):
    line = partial(swapped, axes=("vec", "orb"), sizes=(n_z, n_o))
    near = partial(swapped, axes=("walk", "orb"), sizes=(n_x, n_o))

    others = ((0, 1), (1, 0), (1, 1))
    own_pack, here, quadrant = partial_bias_of(
        aux_field, log_weight, copy_list, walkers, inv_intersection, trial, vectors
    )
    orb_pack = near(own_pack, masks=(0, 1))
    own_pack = summed_pack(own_pack, orb_pack)
    walk_pack = near(own_pack, masks=(1, 0))
    packs = [own_pack, walk_pack]
    mate = near(quadrant, masks=(0, 1))
    piece, nearby, weights, split, log_column = first_pieces(packs, here, mate, n_o)
    came = line(piece, masks=(1, 0))
    inside = lax.ppermute(nearby, "vec", [(0, 0), (1, 2), (2, 1), (3, 3)])
    crossing, kept, *sources = other_pieces(
        own_pack, walk_pack, weights, split, here, mate, walkers, n_o
    )
    crossed = lax.ppermute(crossing, "vec", [(0, 2), (3, 1), (1, 0), (2, 3)])
    passed = combined(crossing, nearby, came, split.shape[0])
    last = lax.ppermute(passed, "vec", [(0, 1), (1, 3), (2, 0), (3, 2)])
    candidates = [sources[0]]
    for value, m in zip(sources[1:], others):
        candidates.append(near(value, masks=m))
    mine, other, slot_weights = taylor(
        own_pack, log_column, [kept, came, inside, crossed, last], candidates, n_o
    )
    steps = [(k, flip) for k in range(n_z) for flip in range(n_o)]
    landed = []
    for dz, flip in steps:
        half = mine if flip == 0 else other
        landed.append(half if (dz, flip) == (0, 0) else line(half, masks=(dz, flip)))
    walkers_out, weights_out = put_in_place(steps, landed, slot_weights, n_o)
    return walkers_out, weights_out[0]


def suits(mesh, walkers, trial, vectors):
    n_z, n_x, n_o = mesh.shape["vec"], mesh.shape["walk"], mesh.shape["orb"]
    per_device = walkers.shape[0] // (mesh.shape["grp"] * n_x)
    local_vectors = vectors.shape[0] // n_z
    return (
        n_o == 2
        and n_x == 2
        and n_z == 4
        and per_device == n_z * n_o
        and local_vectors == per_device
        and vectors.shape[1] == 4 * LANE
        and trial.shape[1] == LANE
    )


def solution(mesh):
    def step(walkers, inv_intersection, trial, vectors, aux_field, log_weight, copy_list):
        if suits(mesh, walkers, trial, vectors):
            body = partial(slot_device, mesh.shape["vec"], mesh.shape["walk"], mesh.shape["orb"])
        else:
            body = general_device
        return jax.shard_map(
            body,
            mesh=mesh,
            in_specs=(
                P(("grp", "walk"), "orb", None),
                P(("grp", "walk"), None, None),
                P(),
                P("vec", "orb", None),
                P(("grp", "walk"), "vec"),
                P(("grp", "walk")),
                P(("grp", "walk")),
            ),
            out_specs=(P(("grp", "walk"), "orb", None), P(("grp", "walk"))),
            check_vma=False,
        )(walkers, inv_intersection, trial, vectors, aux_field, log_weight, copy_list)

    return step
```

```python
from functools import partial
import math

import jax
import jax.numpy as jnp
from jax import lax
from jax.experimental import pallas as pl
from jax.experimental.pallas import tpu as pltpu
from jax.sharding import PartitionSpec as P


ORDER = 6
LANE = 128
VMEM_LIMIT = 24 * 1024 * 1024
CHUNK = 64

step_root = math.sqrt(0.08)

VMEM = pltpu.VMEM


def in_vmem():
    return pl.BlockSpec(memory_space=VMEM)


def in_hbm():
    return pl.BlockSpec(memory_space=pltpu.HBM)


def on_chip(*values):
    return [pltpu.with_memory_space_constraint(value, VMEM) for value in values]


def in_place(*values):
    return [pltpu.with_memory_space_constraint(value, pltpu.HBM) for value in values]


def mm(a, b):
    return jnp.dot(a, b, preferred_element_type=jnp.float32)


def fold_rows(operator, carry, piece, start):
    return jnp.einsum("wnm,wme->wne", operator, piece, preferred_element_type=jnp.float32)


def general_device(walkers, inv_intersection, trial, vectors, aux_field, log_weight, copy_list):
    green = jnp.einsum(
        "wne,wef->wnf", walkers, inv_intersection, preferred_element_type=jnp.float32
    ).astype(jnp.bfloat16)
    mixed = jnp.einsum("gnm,me->gne", vectors, trial, preferred_element_type=jnp.float32).astype(
        jnp.bfloat16
    )
    partial_bias = jnp.einsum("wne,gne->wg", green, mixed, preferred_element_type=jnp.float32)
    bias = lax.psum(partial_bias, "orb")
    shift = -step_root * bias
    field = aux_field - shift
    own_factor = jnp.sum(aux_field * shift - 0.5 * shift * shift, axis=1)
    new_log = log_weight + lax.psum(own_factor, "vec")
    weighted = (field * step_root).astype(jnp.bfloat16)
    local_operator = jnp.einsum(
        "wg,gnm->wnm", weighted, vectors, preferred_element_type=jnp.float32
    )
    operator = lax.psum(local_operator, "vec").astype(jnp.bfloat16)
    running = walkers.astype(jnp.float32)
    folder = partial(fold_rows, operator)
    operand = walkers
    for degree in range(1, ORDER + 1):
        initial = jnp.zeros(running.shape, jnp.float32)
        summed = folder(initial, lax.all_gather(operand, "orb", axis=1, tiled=True), jnp.int32(0))
        new_term = (summed / degree).astype(jnp.bfloat16)
        running = running + new_term.astype(jnp.float32)
        if degree < ORDER:
            operand = new_term
    propagated = running.astype(jnp.bfloat16)
    every_walker = lax.all_gather(propagated, "walk", axis=0, tiled=True)
    every_log = lax.all_gather(new_log, "walk", axis=0, tiled=True)
    return (every_walker[copy_list], every_log[copy_list])


def bias_kernel(aux_hbm, log_hbm, copy_hbm, walkers_hbm, inv_hbm, trial_hbm, vec_hbm, out_ref, vec_ref, quad_ref,
                aux_ref, log_ref, copy_ref, walkers_ref, inv_ref, trial_ref, green_ref, sems):
    n_walk = walkers_hbm.shape[0]
    n_vec = vec_hbm.shape[0]
    copies = [
        pltpu.make_async_copy(source, target, sems.at[i])
        for i, (source, target) in enumerate((
            (walkers_hbm, walkers_ref), (inv_hbm, inv_ref), (trial_hbm, trial_ref),
            (aux_hbm, aux_ref), (log_hbm, log_ref), (copy_hbm, copy_ref),
        ))
    ]
    vec_copies = [
        pltpu.make_async_copy(vec_hbm.at[g], vec_ref.at[g], sems.at[len(copies) + g]) for g in range(n_vec)
    ]
    for copy in copies[:3] + vec_copies + copies[3:]:
        copy.start()
    copies[0].wait()
    copies[1].wait()
    for w in range(n_walk):
        green_ref[w] = mm(walkers_ref[w], inv_ref[w]).astype(jnp.bfloat16).astype(jnp.float32)
    copies[2].wait()
    trial = trial_ref[...]
    n_rows = vec_hbm.shape[1]
    columns = pl.ds(pl.multiple_of(lax.axis_index("orb") * n_rows, n_rows), n_rows)
    lane = lax.broadcasted_iota(jnp.int32, (n_walk, n_vec), 1)
    total = jnp.zeros((n_walk, n_vec), jnp.float32)
    vec_copies[0].wait()
    ahead = mm(vec_ref[0], trial)
    for g in range(n_vec):
        mixed = ahead.astype(jnp.bfloat16).astype(jnp.float32)
        if g + 1 < n_vec:
            vec_copies[g + 1].wait()
            ahead = mm(vec_ref[g + 1], trial)
        quad_ref[g] = vec_ref[g, :, columns]
        held = [None] * n_walk
        for low in range(0, n_rows, CHUNK):
            part = mixed[low : low + CHUNK]
            for w in range(n_walk):
                product = (green_ref[w, pl.ds(low, CHUNK), :] * part).reshape(CHUNK // 8, 8, -1)
                found = jnp.sum(product, axis=0)
                held[w] = found if low == 0 else held[w] + found
        rows = [jnp.sum(value, axis=0, keepdims=True) for value in held]
        column = jnp.sum(jnp.concatenate(rows, axis=0), axis=1, keepdims=True)
        total = total + jnp.where(lane == g, column, 0.0)
    for copy in copies[3:]:
        copy.wait()
    out_ref[pl.ds(0, n_walk), :] = total
    out_ref[pl.ds(n_walk, n_walk), :] = aux_ref[...]
    out_ref[pl.ds(2 * n_walk, n_walk), :] = jnp.zeros((n_walk, n_vec), jnp.float32)
    out_ref[pl.ds(2 * n_walk, 1), :] = log_ref[...]
    out_ref[pl.ds(2 * n_walk + 1, 1), :] = copy_ref[...].astype(jnp.float32)


def partial_bias_of(aux, log_weight, copy_list, walkers, inv, trial, vectors):
    n_walk, n_vec = aux.shape
    log_row, copy_row = log_weight[None, :], copy_list[None, :]
    return pl.pallas_call(
        bias_kernel,
        out_shape=[
            VMEM((3 * n_walk, n_vec), jnp.float32),
            VMEM(vectors.shape, vectors.dtype),
            VMEM((n_vec, vectors.shape[1], vectors.shape[1]), vectors.dtype),
        ],
        in_specs=[in_hbm()] * 7,
        out_specs=[in_vmem()] * 3,
        scratch_shapes=[
            VMEM(aux.shape, aux.dtype),
            VMEM(log_row.shape, log_row.dtype),
            VMEM(copy_row.shape, copy_row.dtype),
            VMEM(walkers.shape, walkers.dtype),
            VMEM(inv.shape, inv.dtype),
            VMEM(trial.shape, trial.dtype),
            VMEM(walkers.shape, jnp.float32),
            pltpu.SemaphoreType.DMA((6 + n_vec,)),
        ],
        compiler_params=pltpu.CompilerParams(vmem_limit_bytes=VMEM_LIMIT),
        name="bias",
    )(*in_place(aux, log_row, copy_row, walkers, inv, trial, vectors))


def copies_of(pack_ref):
    n_walk = pack_ref.shape[0] // 3
    return pack_ref[pl.ds(2 * n_walk + 1, 1), :]


def entry(row, at):
    lane = lax.broadcasted_iota(jnp.int32, row.shape, 1)
    return jnp.sum(jnp.where(lane == at, row, 0.0)).astype(jnp.int32)


def layout(n_block, n_both):
    offsets, at = {}, 0
    for i in range(n_block):
        for j in range(i + 1, n_block):
            offsets[(i, j)] = at
            at += LANE
    for i in range(0, n_block, 2):
        offsets[(i, i)] = at
        at += LANE
    for i in range(1, n_block, 2):
        offsets[(i, i)] = at
        at += 16
    offsets["factor"] = at
    offsets["end"] = at + n_both
    return offsets


def fill_pieces(weights, here_ref, mate_ref, targets, split, o):
    n_vec, n_rows, size = here_ref.shape
    n_block = size // LANE
    in_half = n_rows // LANE
    offsets = layout(n_block, split.shape[0])
    count = len(targets)
    tall = LANE // 2
    splats = [
        [jnp.broadcast_to(weights[k : k + 1, g : g + 1], (tall, LANE)) for g in range(n_vec)]
        for k in range(count)
    ]

    def sums(i, j, step):
        rows = pl.ds(i % in_half * LANE + step * tall, tall)
        if i < in_half:
            column = lax.rem(j + o * in_half, n_block) * LANE
            source, columns = here_ref, pl.ds(pl.multiple_of(column, LANE), LANE)
        else:
            source, columns = mate_ref, pl.ds((j - in_half) * LANE, LANE)
        result = [None] * count
        for g in range(n_vec):
            value = source[g, rows, columns].astype(jnp.float32)
            for k in range(count):
                product = splats[k][g] * value
                result[k] = product if g == 0 else result[k] + product
        return result

    def put(k, offset, count_rows, value):
        targets[k][pl.ds(offset, count_rows), :] = value

    line = lax.broadcasted_iota(jnp.int32, (tall, LANE), 0)
    lane = lax.broadcasted_iota(jnp.int32, (tall, LANE), 1)
    seen = lax.broadcasted_iota(jnp.int32, (16, LANE), 1)
    for pair, offset in offsets.items():
        if isinstance(pair, str):
            continue
        i, j = pair
        if i == j and i % 2 == 1:
            continue
        diagonals = [None] * count
        for step in range(LANE // tall):
            at = offset + step * tall
            upper = sums(i, j, step)
            if i == j:
                row_at = line + step * tall
                lower = sums(i + 1, i + 1, step)
                for k in range(count):
                    found = jnp.sum(jnp.where(row_at == lane, lower[k], 0.0), axis=0, keepdims=True)
                    diagonals[k] = found if step == 0 else diagonals[k] + found
                upper = [jnp.where(row_at <= lane, u, v) for u, v in zip(upper, lower)]
            for k in range(count):
                put(k, at, tall, upper[k].astype(jnp.bfloat16))
        if i == j:
            for k in range(count):
                row = jnp.broadcast_to(diagonals[k], (16, LANE)).astype(jnp.bfloat16)
                put(k, offsets[(i + 1, i + 1)], 16, row)
    for k in range(count):
        put(k, offsets["factor"], split.shape[0], split)


def split_column(column):
    lane = lax.broadcasted_iota(jnp.int32, (column.shape[0], LANE), 1)
    split = jnp.zeros(lane.shape, jnp.float32)
    for i in range(3):
        part = column.astype(jnp.bfloat16).astype(jnp.float32)
        split = jnp.where(lane == i, jnp.broadcast_to(part, lane.shape), split)
        column = column - part
    return split.astype(jnp.bfloat16)


def joined(split):
    wide = split.astype(jnp.float32)
    return (wide[:, 0:1] + wide[:, 1:2]) + wide[:, 2:3]


def routes(z):
    inner = jnp.logical_or(z == 1, z == 2)
    first = jnp.where(lax.rem(z, 2) == 0, 3, 0)
    crossing = jnp.where(z == 0, 2, jnp.where(z == 3, 1, jnp.where(z == 1, 3, 0)))
    nearby = jnp.where(lax.rem(z, 2) == 0, 1, 2)
    return inner, first, crossing, nearby


def first_kernel(n_o, own_ref, walk_ref, here_ref, mate_ref,
                 first_ref, near_ref, weight_ref, split_ref, log_ref):
    n_walk = own_ref.shape[0] // 3
    z, x, o = lax.axis_index("vec"), lax.axis_index("walk"), lax.axis_index("orb")
    bias = jnp.concatenate(
        [own_ref[pl.ds(0, n_walk), :], walk_ref[pl.ds(0, n_walk), :]], axis=0
    )
    aux = jnp.concatenate([own_ref[pl.ds(n_walk, n_walk), :], walk_ref[pl.ds(n_walk, n_walk), :]], axis=0)
    shift = -step_root * bias
    weighted = ((aux - shift) * step_root).astype(jnp.bfloat16)
    split = split_column(jnp.sum(aux * shift - 0.5 * shift * shift, axis=1, keepdims=True))
    split_ref[...] = split
    _, first, crossing, nearby = routes(z)
    k_at = lax.broadcasted_iota(jnp.int32, (8, n_walk), 0)
    lane = lax.broadcasted_iota(jnp.int32, (8, n_walk), 1)
    to_z = jnp.where(k_at == 0, first, jnp.where(k_at == 1, nearby, jnp.where(k_at == 2, crossing, z)))
    sources = jnp.sum(
        jnp.where(lane == to_z * n_o + o, jnp.broadcast_to(copies_of(own_ref), lane.shape), 0.0),
        axis=1, keepdims=True,
    ).astype(jnp.int32)
    row = lax.rem(sources, n_walk) + n_walk * (lax.div(sources, n_walk) != x).astype(jnp.int32)
    pick = lax.broadcasted_iota(jnp.int32, (8, 2 * n_walk), 1) == row
    weights = mm(pick.astype(jnp.float32).astype(jnp.bfloat16), weighted)
    weight_ref[...] = weights
    fill_pieces(weights, here_ref, mate_ref, [first_ref, near_ref], split, o)
    square = (n_walk, n_walk)
    eye = lax.broadcasted_iota(jnp.int32, square, 0) == lax.broadcasted_iota(jnp.int32, square, 1)
    for side, ref in enumerate((own_ref, walk_ref)):
        log_ref[pl.ds(side * n_walk, n_walk), :] = jnp.sum(
            jnp.where(eye, ref[pl.ds(2 * n_walk, 1), :], 0.0), axis=1, keepdims=True
        )


def sum_kernel(own_ref, orb_ref, out_ref):
    n_walk = own_ref.shape[0] // 3
    out_ref[...] = own_ref[...]
    out_ref[pl.ds(0, n_walk), :] = own_ref[pl.ds(0, n_walk), :] + orb_ref[pl.ds(0, n_walk), :]


def summed_pack(own, orb):
    return pl.pallas_call(
        sum_kernel,
        out_shape=VMEM(own.shape, own.dtype),
        in_specs=[in_vmem()] * 2,
        out_specs=in_vmem(),
        compiler_params=pltpu.CompilerParams(vmem_limit_bytes=VMEM_LIMIT),
        name="summed_pack",
    )(*on_chip(own, orb))


def first_pieces(packs, here, mate, n_o):
    n_walk, n_vec = packs[0].shape[0] // 3, packs[0].shape[1]
    return pl.pallas_call(
        partial(first_kernel, n_o),
        out_shape=[VMEM((layout(here.shape[2] // LANE, 2 * n_walk)["end"], LANE), jnp.bfloat16)] * 2 + [
            VMEM((8, n_vec), jnp.float32),
            VMEM((2 * n_walk, LANE), jnp.bfloat16),
            VMEM((2 * n_walk, 1), jnp.float32),
        ],
        in_specs=[in_vmem()] * 4,
        out_specs=[in_vmem()] * 5,
        compiler_params=pltpu.CompilerParams(vmem_limit_bytes=VMEM_LIMIT),
        name="first_piece",
    )(*on_chip(*packs, here, mate))


def other_kernel(n_o, own_ref, walk_ref, weight_ref, split_ref, here_ref, mate_ref, walkers_hbm, *refs):
    pieces, sources, sems = refs[:2], refs[2:6], refs[6]
    n_walk = walkers_hbm.shape[0]
    z, o = lax.axis_index("vec"), lax.axis_index("orb")
    slot, mate = z * n_o + o, z * n_o + (n_o - 1 - o)
    own_list, far_list = copies_of(own_ref), copies_of(walk_ref)
    wanted = ((own_list, slot), (own_list, mate), (far_list, slot), (far_list, mate))
    copies = [
        pltpu.make_async_copy(walkers_hbm.at[lax.rem(entry(row, at), n_walk)], out, sems.at[i])
        for i, ((row, at), out) in enumerate(zip(wanted, sources))
    ]
    for copy in copies:
        copy.start()
    fill_pieces(weight_ref[...][2:4], here_ref, mate_ref, pieces, split_ref[...], o)
    for copy in copies:
        copy.wait()


def other_pieces(own_pack, walk_pack, weights, split, here, mate, walkers, n_o):
    offsets = layout(here.shape[2] // LANE, split.shape[0])
    piece = VMEM((offsets["end"], LANE), jnp.bfloat16)
    source = VMEM(walkers.shape[1:], walkers.dtype)
    return pl.pallas_call(
        partial(other_kernel, n_o),
        out_shape=[piece] * 2 + [source] * 4,
        in_specs=[in_vmem()] * 6 + [in_hbm()],
        out_specs=[in_vmem()] * 6,
        scratch_shapes=[pltpu.SemaphoreType.DMA((4,))],
        compiler_params=pltpu.CompilerParams(vmem_limit_bytes=VMEM_LIMIT),
        name="other_pieces",
    )(*on_chip(own_pack, walk_pack, weights, split, here, mate), *in_place(walkers))


def combine_kernel(body, far_ref, near_ref, came_ref, out_ref):
    inner = routes(lax.axis_index("vec"))[0]

    @pl.when(inner)
    def _():
        for low in range(0, body, LANE):
            rows = pl.ds(low, min(LANE, body - low))
            value = far_ref[rows, :].astype(jnp.float32) + came_ref[rows, :].astype(jnp.float32)
            out_ref[rows, :] = value.astype(jnp.bfloat16)
        tail = pl.ds(body, out_ref.shape[0] - body)
        out_ref[tail, :] = split_column(joined(far_ref[tail, :]) + joined(came_ref[tail, :]))

    @pl.when(jnp.logical_not(inner))
    def _():
        out_ref[...] = near_ref[...]


def combined(far, nearby, came, n_both):
    return pl.pallas_call(
        partial(combine_kernel, came.shape[0] - n_both),
        out_shape=VMEM(came.shape, came.dtype),
        in_specs=[in_vmem()] * 3,
        out_specs=in_vmem(),
        compiler_params=pltpu.CompilerParams(vmem_limit_bytes=VMEM_LIMIT),
        name="combine",
    )(*on_chip(far, nearby, came))


def log_weights(copy_row, log_column, total, x):
    n_walk = log_column.shape[0] // 2
    new_log = log_column + total
    source = copy_row.astype(jnp.int32)
    row = lax.rem(source, n_walk) + n_walk * (lax.div(source, n_walk) != x).astype(jnp.int32)
    shape = (2 * n_walk, copy_row.shape[1])
    at = lax.broadcasted_iota(jnp.int32, shape, 0)
    chosen = jnp.where(at == jnp.broadcast_to(row, shape), jnp.broadcast_to(new_log, shape), 0.0)
    return jnp.sum(chosen, axis=0, keepdims=True)


def taylor_kernel(n_o, pack_ref, log_ref, kept_ref, first_ref, inside_ref, cross_ref, last_ref, own_ref, orb_ref, walk_ref, far_ref,
                  mine_ref, other_ref, weights_ref, op_ref, term_ref, sum_ref):
    z, x, o = lax.axis_index("vec"), lax.axis_index("walk"), lax.axis_index("orb")
    inner = routes(z)[0]
    n_both = log_ref.shape[0]
    n_walk = n_both // 2
    n_block = op_ref.shape[0] // LANE
    offsets = layout(n_block, n_both)
    i_at = lax.broadcasted_iota(jnp.int32, (LANE, LANE), 0)
    j_at = lax.broadcasted_iota(jnp.int32, (LANE, LANE), 1)

    def terms(offset, count):
        rows = pl.ds(offset, count)
        return (ref[rows, :] for ref in (kept_ref, first_ref, inside_ref, cross_ref, last_ref))

    def total(offset, count):
        kept, first, inside, cross, last = (value.astype(jnp.float32) for value in terms(offset, count))
        return (kept + last) + jnp.where(inner, inside + cross, first)

    def put(i, j, value):
        op_ref[pl.ds(i * LANE, LANE), pl.ds(j * LANE, LANE)] = value.astype(jnp.bfloat16)

    for i in range(n_block):
        for j in range(i + 1, n_block):
            value = total(offsets[(i, j)], LANE)
            put(i, j, value)
            put(j, i, value.T)
    for i in range(0, n_block, 2):
        merged = total(offsets[(i, i)], LANE)
        diagonal = total(offsets[(i + 1, i + 1)], 16)[:1]
        turned = merged.T
        put(i, i, jnp.where(i_at <= j_at, merged, turned))
        second = jnp.where(i_at > j_at, merged, turned)
        put(i + 1, i + 1, jnp.where(i_at == j_at, diagonal, second))

    copy_row = copies_of(pack_ref)
    here = lax.div(entry(copy_row, z * n_o + o), n_walk) == x
    rows = own_ref.shape[0]
    top, bottom = pl.ds(0, rows), pl.ds(rows, rows)
    term_ref[top, :] = jnp.where(here, own_ref[...], walk_ref[...])
    term_ref[bottom, :] = jnp.where(here, orb_ref[...], far_ref[...])
    sum_ref[...] = term_ref[...].astype(jnp.float32)
    for degree in range(1, ORDER + 1):
        halves = [mm(op_ref[half, :], term_ref[...]) for half in (top, bottom)]
        for half, product in zip((top, bottom), halves):
            term = (product * (1.0 / degree)).astype(jnp.bfloat16)
            sum_ref[half, :] += term.astype(jnp.float32)
            if degree < ORDER:
                term_ref[half, :] = term
    mine_ref[...] = sum_ref[top, :].astype(jnp.bfloat16)
    other_ref[...] = sum_ref[bottom, :].astype(jnp.bfloat16)

    kept, first, inside, cross, last = (joined(value) for value in terms(offsets["factor"], n_both))
    factor = (kept + jnp.where(inner, last, first)) + jnp.where(inner, inside + cross, last)
    weights_ref[...] = log_weights(copy_row, log_ref[...], factor, x)


def taylor(pack, log_column, arrived, candidates, n_o):
    rows, width = candidates[0].shape
    size = n_o * rows
    out = VMEM((rows, width), jnp.bfloat16)
    return pl.pallas_call(
        partial(taylor_kernel, n_o),
        out_shape=[out, out, VMEM((1, log_column.shape[0] // 2), jnp.float32)],
        in_specs=[in_vmem()] * (2 + len(arrived) + 4),
        out_specs=[in_vmem()] * 3,
        scratch_shapes=[
            VMEM((size, size), jnp.bfloat16),
            VMEM((size, width), jnp.bfloat16),
            VMEM((size, width), jnp.float32),
        ],
        compiler_params=pltpu.CompilerParams(vmem_limit_bytes=VMEM_LIMIT),
        name="taylor",
    )(*on_chip(pack, log_column, *arrived, *candidates))


def place_kernel(steps, n_o, *refs):
    n_line = len(steps)
    pieces, weights_ref = refs[:n_line], refs[n_line]
    out_ref, weights_out, sems = refs[n_line + 1 :]
    z, o = lax.axis_index("vec"), lax.axis_index("orb")
    copies = [
        pltpu.make_async_copy(
            pieces[k],
            out_ref.at[jnp.bitwise_xor(z, dz) * n_o + jnp.bitwise_xor(o, flip)],
            sems.at[k],
        )
        for k, (dz, flip) in enumerate(steps)
    ]
    copies.append(pltpu.make_async_copy(weights_ref, weights_out, sems.at[n_line]))
    for copy in copies:
        copy.start()
    for copy in copies:
        copy.wait()


def put_in_place(steps, pieces, weights, n_o):
    n_line = len(pieces)
    return pl.pallas_call(
        partial(place_kernel, steps, n_o),
        out_shape=[
            jax.ShapeDtypeStruct((n_line,) + pieces[0].shape, pieces[0].dtype),
            jax.ShapeDtypeStruct(weights.shape, weights.dtype),
        ],
        in_specs=[in_vmem()] * (n_line + 1),
        out_specs=[in_hbm()] * 2,
        scratch_shapes=[pltpu.SemaphoreType.DMA((n_line + 1,))],
        compiler_params=pltpu.CompilerParams(vmem_limit_bytes=VMEM_LIMIT),
        name="place",
    )(*on_chip(*pieces, weights))


def swapped(value, axes, sizes, masks):
    perm = []
    for a in range(sizes[0]):
        for b in range(sizes[1]):
            perm.append((a * sizes[1] + b, (a ^ masks[0]) * sizes[1] + (b ^ masks[1])))
    return lax.ppermute(value, axes, perm)


def slot_device(n_z, n_x, n_o, walkers, inv_intersection, trial, vectors, aux_field, log_weight, copy_list):
    line = partial(swapped, axes=("vec", "orb"), sizes=(n_z, n_o))
    near = partial(swapped, axes=("walk", "orb"), sizes=(n_x, n_o))

    others = ((0, 1), (1, 0), (1, 1))
    own_pack, here, quadrant = partial_bias_of(
        aux_field, log_weight, copy_list, walkers, inv_intersection, trial, vectors
    )
    orb_pack = near(own_pack, masks=(0, 1))
    own_pack = summed_pack(own_pack, orb_pack)
    walk_pack = near(own_pack, masks=(1, 0))
    packs = [own_pack, walk_pack]
    mate = near(quadrant, masks=(0, 1))
    piece, nearby, weights, split, log_column = first_pieces(packs, here, mate, n_o)
    came = line(piece, masks=(1, 0))
    inside = lax.ppermute(nearby, "vec", [(0, 0), (1, 2), (2, 1), (3, 3)])
    crossing, kept, *sources = other_pieces(
        own_pack, walk_pack, weights, split, here, mate, walkers, n_o
    )
    crossed = lax.ppermute(crossing, "vec", [(0, 2), (3, 1), (1, 0), (2, 3)])
    passed = combined(crossing, nearby, came, split.shape[0])
    last = lax.ppermute(passed, "vec", [(0, 1), (1, 3), (2, 0), (3, 2)])
    candidates = [sources[0]]
    for value, m in zip(sources[1:], others):
        candidates.append(near(value, masks=m))
    mine, other, slot_weights = taylor(
        own_pack, log_column, [kept, came, inside, crossed, last], candidates, n_o
    )
    steps = [(k, flip) for k in range(n_z) for flip in range(n_o)]
    landed = []
    for dz, flip in steps:
        half = mine if flip == 0 else other
        landed.append(half if (dz, flip) == (0, 0) else line(half, masks=(dz, flip)))
    walkers_out, weights_out = put_in_place(steps, landed, slot_weights, n_o)
    return walkers_out, weights_out[0]


def suits(mesh, walkers, trial, vectors):
    n_z, n_x, n_o = mesh.shape["vec"], mesh.shape["walk"], mesh.shape["orb"]
    per_device = walkers.shape[0] // (mesh.shape["grp"] * n_x)
    local_vectors = vectors.shape[0] // n_z
    return (
        n_o == 2
        and n_x == 2
        and n_z == 4
        and per_device == n_z * n_o
        and local_vectors == per_device
        and vectors.shape[1] == 4 * LANE
        and trial.shape[1] == LANE
    )


def solution(mesh):
    def step(walkers, inv_intersection, trial, vectors, aux_field, log_weight, copy_list):
        if suits(mesh, walkers, trial, vectors):
            body = partial(slot_device, mesh.shape["vec"], mesh.shape["walk"], mesh.shape["orb"])
        else:
            body = general_device
        return jax.shard_map(
            body,
            mesh=mesh,
            in_specs=(
                P(("grp", "walk"), "orb", None),
                P(("grp", "walk"), None, None),
                P(),
                P("vec", "orb", None),
                P(("grp", "walk"), "vec"),
                P(("grp", "walk")),
                P(("grp", "walk")),
            ),
            out_specs=(P(("grp", "walk"), "orb", None), P(("grp", "walk"))),
            check_vma=False,
        )(walkers, inv_intersection, trial, vectors, aux_field, log_weight, copy_list)

    return step
```

```python
from functools import partial
import math

import jax
import jax.numpy as jnp
from jax import lax
from jax.experimental import pallas as pl
from jax.experimental.pallas import tpu as pltpu
from jax.sharding import PartitionSpec as P


ORDER = 6
LANE = 128
VMEM_LIMIT = 24 * 1024 * 1024
CHUNK = 64

step_root = math.sqrt(0.08)

VMEM = pltpu.VMEM


def in_vmem():
    return pl.BlockSpec(memory_space=VMEM)


def in_hbm():
    return pl.BlockSpec(memory_space=pltpu.HBM)


def on_chip(*values):
    return [pltpu.with_memory_space_constraint(value, VMEM) for value in values]


def in_place(*values):
    return [pltpu.with_memory_space_constraint(value, pltpu.HBM) for value in values]


def mm(a, b):
    return jnp.dot(a, b, preferred_element_type=jnp.float32)


def fold_rows(operator, carry, piece, start):
    return jnp.einsum("wnm,wme->wne", operator, piece, preferred_element_type=jnp.float32)


def general_device(walkers, inv_intersection, trial, vectors, aux_field, log_weight, copy_list):
    green = jnp.einsum(
        "wne,wef->wnf", walkers, inv_intersection, preferred_element_type=jnp.float32
    ).astype(jnp.bfloat16)
    mixed = jnp.einsum("gnm,me->gne", vectors, trial, preferred_element_type=jnp.float32).astype(
        jnp.bfloat16
    )
    partial_bias = jnp.einsum("wne,gne->wg", green, mixed, preferred_element_type=jnp.float32)
    bias = lax.psum(partial_bias, "orb")
    shift = -step_root * bias
    field = aux_field - shift
    own_factor = jnp.sum(aux_field * shift - 0.5 * shift * shift, axis=1)
    new_log = log_weight + lax.psum(own_factor, "vec")
    weighted = (field * step_root).astype(jnp.bfloat16)
    local_operator = jnp.einsum(
        "wg,gnm->wnm", weighted, vectors, preferred_element_type=jnp.float32
    )
    operator = lax.psum(local_operator, "vec").astype(jnp.bfloat16)
    running = walkers.astype(jnp.float32)
    folder = partial(fold_rows, operator)
    operand = walkers
    for degree in range(1, ORDER + 1):
        initial = jnp.zeros(running.shape, jnp.float32)
        summed = folder(initial, lax.all_gather(operand, "orb", axis=1, tiled=True), jnp.int32(0))
        new_term = (summed / degree).astype(jnp.bfloat16)
        running = running + new_term.astype(jnp.float32)
        if degree < ORDER:
            operand = new_term
    propagated = running.astype(jnp.bfloat16)
    every_walker = lax.all_gather(propagated, "walk", axis=0, tiled=True)
    every_log = lax.all_gather(new_log, "walk", axis=0, tiled=True)
    return (every_walker[copy_list], every_log[copy_list])


def bias_kernel(aux_hbm, log_hbm, copy_hbm, walkers_hbm, inv_hbm, trial_hbm, vec_hbm, out_ref, vec_ref, quad_ref,
                aux_ref, log_ref, copy_ref, walkers_ref, inv_ref, trial_ref, green_ref, sems):
    n_walk = walkers_hbm.shape[0]
    n_vec = vec_hbm.shape[0]
    copies = [
        pltpu.make_async_copy(source, target, sems.at[i])
        for i, (source, target) in enumerate((
            (walkers_hbm, walkers_ref), (inv_hbm, inv_ref), (trial_hbm, trial_ref),
            (aux_hbm, aux_ref), (log_hbm, log_ref), (copy_hbm, copy_ref),
        ))
    ]
    vec_copies = [
        pltpu.make_async_copy(vec_hbm.at[g], vec_ref.at[g], sems.at[len(copies) + g]) for g in range(n_vec)
    ]
    for copy in copies[:3] + vec_copies + copies[3:]:
        copy.start()
    copies[0].wait()
    copies[1].wait()
    for w in range(n_walk):
        green_ref[w] = mm(walkers_ref[w], inv_ref[w]).astype(jnp.bfloat16).astype(jnp.float32)
    copies[2].wait()
    trial = trial_ref[...]
    n_rows = vec_hbm.shape[1]
    columns = pl.ds(pl.multiple_of(lax.axis_index("orb") * n_rows, n_rows), n_rows)
    lane = lax.broadcasted_iota(jnp.int32, (n_walk, n_vec), 1)
    total = jnp.zeros((n_walk, n_vec), jnp.float32)
    vec_copies[0].wait()
    ahead = mm(vec_ref[0], trial)
    for g in range(n_vec):
        mixed = ahead.astype(jnp.bfloat16).astype(jnp.float32)
        if g + 1 < n_vec:
            vec_copies[g + 1].wait()
            ahead = mm(vec_ref[g + 1], trial)
        quad_ref[g] = vec_ref[g, :, columns]
        held = [None] * n_walk
        for low in range(0, n_rows, CHUNK):
            part = mixed[low : low + CHUNK]
            for w in range(n_walk):
                product = (green_ref[w, pl.ds(low, CHUNK), :] * part).reshape(CHUNK // 8, 8, -1)
                found = jnp.sum(product, axis=0)
                held[w] = found if low == 0 else held[w] + found
        rows = [jnp.sum(value, axis=0, keepdims=True) for value in held]
        column = jnp.sum(jnp.concatenate(rows, axis=0), axis=1, keepdims=True)
        total = total + jnp.where(lane == g, column, 0.0)
    for copy in copies[3:]:
        copy.wait()
    out_ref[pl.ds(0, n_walk), :] = total
    out_ref[pl.ds(n_walk, n_walk), :] = aux_ref[...]
    out_ref[pl.ds(2 * n_walk, n_walk), :] = jnp.zeros((n_walk, n_vec), jnp.float32)
    out_ref[pl.ds(2 * n_walk, 1), :] = log_ref[...]
    out_ref[pl.ds(2 * n_walk + 1, 1), :] = copy_ref[...].astype(jnp.float32)


def partial_bias_of(aux, log_weight, copy_list, walkers, inv, trial, vectors):
    n_walk, n_vec = aux.shape
    log_row, copy_row = log_weight[None, :], copy_list[None, :]
    return pl.pallas_call(
        bias_kernel,
        out_shape=[
            VMEM((3 * n_walk, n_vec), jnp.float32),
            VMEM(vectors.shape, vectors.dtype),
            VMEM((n_vec, vectors.shape[1], vectors.shape[1]), vectors.dtype),
        ],
        in_specs=[in_hbm()] * 7,
        out_specs=[in_vmem()] * 3,
        scratch_shapes=[
            VMEM(aux.shape, aux.dtype),
            VMEM(log_row.shape, log_row.dtype),
            VMEM(copy_row.shape, copy_row.dtype),
            VMEM(walkers.shape, walkers.dtype),
            VMEM(inv.shape, inv.dtype),
            VMEM(trial.shape, trial.dtype),
            VMEM(walkers.shape, jnp.float32),
            pltpu.SemaphoreType.DMA((6 + n_vec,)),
        ],
        compiler_params=pltpu.CompilerParams(vmem_limit_bytes=VMEM_LIMIT),
        name="bias",
    )(*in_place(aux, log_row, copy_row, walkers, inv, trial, vectors))


def copies_of(pack_ref):
    n_walk = pack_ref.shape[0] // 3
    return pack_ref[pl.ds(2 * n_walk + 1, 1), :]


def entry(row, at):
    lane = lax.broadcasted_iota(jnp.int32, row.shape, 1)
    return jnp.sum(jnp.where(lane == at, row, 0.0)).astype(jnp.int32)


def layout(n_block, n_both):
    offsets, at = {}, 0
    for i in range(n_block):
        for j in range(i + 1, n_block):
            offsets[(i, j)] = at
            at += LANE
    for i in range(0, n_block, 2):
        offsets[(i, i)] = at
        at += LANE
    for i in range(1, n_block, 2):
        offsets[(i, i)] = at
        at += 16
    offsets["factor"] = at
    offsets["end"] = at + n_both
    return offsets


def fill_pieces(weights, here_ref, mate_ref, targets, split, o):
    n_vec, n_rows, size = here_ref.shape
    n_block = size // LANE
    in_half = n_rows // LANE
    offsets = layout(n_block, split.shape[0])
    count = len(targets)
    tall = LANE // 2
    splats = [
        [jnp.broadcast_to(weights[k : k + 1, g : g + 1], (tall, LANE)) for g in range(n_vec)]
        for k in range(count)
    ]

    def sums(i, j, step):
        rows = pl.ds(i % in_half * LANE + step * tall, tall)
        if i < in_half:
            column = lax.rem(j + o * in_half, n_block) * LANE
            source, columns = here_ref, pl.ds(pl.multiple_of(column, LANE), LANE)
        else:
            source, columns = mate_ref, pl.ds((j - in_half) * LANE, LANE)
        result = [None] * count
        for g in range(n_vec):
            value = source[g, rows, columns].astype(jnp.float32)
            for k in range(count):
                product = splats[k][g] * value
                result[k] = product if g == 0 else result[k] + product
        return result

    def put(k, offset, count_rows, value):
        targets[k][pl.ds(offset, count_rows), :] = value

    line = lax.broadcasted_iota(jnp.int32, (tall, LANE), 0)
    lane = lax.broadcasted_iota(jnp.int32, (tall, LANE), 1)
    seen = lax.broadcasted_iota(jnp.int32, (16, LANE), 1)
    for pair, offset in offsets.items():
        if isinstance(pair, str):
            continue
        i, j = pair
        if i == j and i % 2 == 1:
            continue
        diagonals = [None] * count
        for step in range(LANE // tall):
            at = offset + step * tall
            upper = sums(i, j, step)
            if i == j:
                row_at = line + step * tall
                lower = sums(i + 1, i + 1, step)
                for k in range(count):
                    found = jnp.sum(jnp.where(row_at == lane, lower[k], 0.0), axis=0, keepdims=True)
                    diagonals[k] = found if step == 0 else diagonals[k] + found
                upper = [jnp.where(row_at <= lane, u, v) for u, v in zip(upper, lower)]
            for k in range(count):
                put(k, at, tall, upper[k].astype(jnp.bfloat16))
        if i == j:
            for k in range(count):
                row = jnp.broadcast_to(diagonals[k], (16, LANE)).astype(jnp.bfloat16)
                put(k, offsets[(i + 1, i + 1)], 16, row)
    for k in range(count):
        put(k, offsets["factor"], split.shape[0], split)


def split_column(column):
    lane = lax.broadcasted_iota(jnp.int32, (column.shape[0], LANE), 1)
    split = jnp.zeros(lane.shape, jnp.float32)
    for i in range(3):
        part = column.astype(jnp.bfloat16).astype(jnp.float32)
        split = jnp.where(lane == i, jnp.broadcast_to(part, lane.shape), split)
        column = column - part
    return split.astype(jnp.bfloat16)


def joined(split):
    wide = split.astype(jnp.float32)
    return (wide[:, 0:1] + wide[:, 1:2]) + wide[:, 2:3]


def routes(z):
    inner = jnp.logical_or(z == 1, z == 2)
    first = jnp.where(lax.rem(z, 2) == 0, 3, 0)
    crossing = jnp.where(z == 0, 2, jnp.where(z == 3, 1, jnp.where(z == 1, 3, 0)))
    nearby = jnp.where(lax.rem(z, 2) == 0, 1, 2)
    return inner, first, crossing, nearby


def first_kernel(n_o, own_ref, walk_ref, here_ref, mate_ref,
                 first_ref, near_ref, weight_ref, split_ref, log_ref):
    n_walk = own_ref.shape[0] // 3
    z, x, o = lax.axis_index("vec"), lax.axis_index("walk"), lax.axis_index("orb")
    bias = jnp.concatenate(
        [own_ref[pl.ds(0, n_walk), :], walk_ref[pl.ds(0, n_walk), :]], axis=0
    )
    aux = jnp.concatenate([own_ref[pl.ds(n_walk, n_walk), :], walk_ref[pl.ds(n_walk, n_walk), :]], axis=0)
    shift = -step_root * bias
    weighted = ((aux - shift) * step_root).astype(jnp.bfloat16)
    split = split_column(jnp.sum(aux * shift - 0.5 * shift * shift, axis=1, keepdims=True))
    split_ref[...] = split
    _, first, crossing, nearby = routes(z)
    k_at = lax.broadcasted_iota(jnp.int32, (8, n_walk), 0)
    lane = lax.broadcasted_iota(jnp.int32, (8, n_walk), 1)
    to_z = jnp.where(k_at == 0, first, jnp.where(k_at == 1, nearby, jnp.where(k_at == 2, crossing, z)))
    sources = jnp.sum(
        jnp.where(lane == to_z * n_o + o, jnp.broadcast_to(copies_of(own_ref), lane.shape), 0.0),
        axis=1, keepdims=True,
    ).astype(jnp.int32)
    row = lax.rem(sources, n_walk) + n_walk * (lax.div(sources, n_walk) != x).astype(jnp.int32)
    pick = lax.broadcasted_iota(jnp.int32, (8, 2 * n_walk), 1) == row
    weights = mm(pick.astype(jnp.float32).astype(jnp.bfloat16), weighted)
    weight_ref[...] = weights
    fill_pieces(weights, here_ref, mate_ref, [first_ref, near_ref], split, o)
    square = (n_walk, n_walk)
    eye = lax.broadcasted_iota(jnp.int32, square, 0) == lax.broadcasted_iota(jnp.int32, square, 1)
    for side, ref in enumerate((own_ref, walk_ref)):
        log_ref[pl.ds(side * n_walk, n_walk), :] = jnp.sum(
            jnp.where(eye, ref[pl.ds(2 * n_walk, 1), :], 0.0), axis=1, keepdims=True
        )


def sum_kernel(own_ref, orb_ref, out_ref):
    n_walk = own_ref.shape[0] // 3
    out_ref[...] = own_ref[...]
    out_ref[pl.ds(0, n_walk), :] = own_ref[pl.ds(0, n_walk), :] + orb_ref[pl.ds(0, n_walk), :]


def summed_pack(own, orb):
    return pl.pallas_call(
        sum_kernel,
        out_shape=VMEM(own.shape, own.dtype),
        in_specs=[in_vmem()] * 2,
        out_specs=in_vmem(),
        compiler_params=pltpu.CompilerParams(vmem_limit_bytes=VMEM_LIMIT),
        name="summed_pack",
    )(*on_chip(own, orb))


def first_pieces(packs, here, mate, n_o):
    n_walk, n_vec = packs[0].shape[0] // 3, packs[0].shape[1]
    return pl.pallas_call(
        partial(first_kernel, n_o),
        out_shape=[VMEM((layout(here.shape[2] // LANE, 2 * n_walk)["end"], LANE), jnp.bfloat16)] * 2 + [
            VMEM((8, n_vec), jnp.float32),
            VMEM((2 * n_walk, LANE), jnp.bfloat16),
            VMEM((2 * n_walk, 1), jnp.float32),
        ],
        in_specs=[in_vmem()] * 4,
        out_specs=[in_vmem()] * 5,
        compiler_params=pltpu.CompilerParams(vmem_limit_bytes=VMEM_LIMIT),
        name="first_piece",
    )(*on_chip(*packs, here, mate))


def other_kernel(n_o, own_ref, walk_ref, weight_ref, split_ref, here_ref, mate_ref, walkers_hbm, *refs):
    pieces, sources, sems = refs[:2], refs[2:6], refs[6]
    n_walk = walkers_hbm.shape[0]
    z, o = lax.axis_index("vec"), lax.axis_index("orb")
    slot, mate = z * n_o + o, z * n_o + (n_o - 1 - o)
    own_list, far_list = copies_of(own_ref), copies_of(walk_ref)
    wanted = ((own_list, slot), (own_list, mate), (far_list, slot), (far_list, mate))
    copies = [
        pltpu.make_async_copy(walkers_hbm.at[lax.rem(entry(row, at), n_walk)], out, sems.at[i])
        for i, ((row, at), out) in enumerate(zip(wanted, sources))
    ]
    for copy in copies:
        copy.start()
    fill_pieces(weight_ref[...][2:4], here_ref, mate_ref, pieces, split_ref[...], o)
    for copy in copies:
        copy.wait()


def other_pieces(own_pack, walk_pack, weights, split, here, mate, walkers, n_o):
    offsets = layout(here.shape[2] // LANE, split.shape[0])
    piece = VMEM((offsets["end"], LANE), jnp.bfloat16)
    source = VMEM(walkers.shape[1:], walkers.dtype)
    return pl.pallas_call(
        partial(other_kernel, n_o),
        out_shape=[piece] * 2 + [source] * 4,
        in_specs=[in_vmem()] * 6 + [in_hbm()],
        out_specs=[in_vmem()] * 6,
        scratch_shapes=[pltpu.SemaphoreType.DMA((4,))],
        compiler_params=pltpu.CompilerParams(vmem_limit_bytes=VMEM_LIMIT),
        name="other_pieces",
    )(*on_chip(own_pack, walk_pack, weights, split, here, mate), *in_place(walkers))


def combine_kernel(body, far_ref, near_ref, came_ref, out_ref):
    inner = routes(lax.axis_index("vec"))[0]

    @pl.when(inner)
    def _():
        for low in range(0, body, LANE):
            rows = pl.ds(low, min(LANE, body - low))
            value = far_ref[rows, :].astype(jnp.float32) + came_ref[rows, :].astype(jnp.float32)
            out_ref[rows, :] = value.astype(jnp.bfloat16)
        tail = pl.ds(body, out_ref.shape[0] - body)
        out_ref[tail, :] = split_column(joined(far_ref[tail, :]) + joined(came_ref[tail, :]))

    @pl.when(jnp.logical_not(inner))
    def _():
        out_ref[...] = near_ref[...]


def combined(far, nearby, came, n_both):
    return pl.pallas_call(
        partial(combine_kernel, came.shape[0] - n_both),
        out_shape=VMEM(came.shape, came.dtype),
        in_specs=[in_vmem()] * 3,
        out_specs=in_vmem(),
        compiler_params=pltpu.CompilerParams(vmem_limit_bytes=VMEM_LIMIT),
        name="combine",
    )(*on_chip(far, nearby, came))


def log_weights(copy_row, log_column, total, x):
    n_walk = log_column.shape[0] // 2
    new_log = log_column + total
    source = copy_row.astype(jnp.int32)
    row = lax.rem(source, n_walk) + n_walk * (lax.div(source, n_walk) != x).astype(jnp.int32)
    shape = (2 * n_walk, copy_row.shape[1])
    at = lax.broadcasted_iota(jnp.int32, shape, 0)
    chosen = jnp.where(at == jnp.broadcast_to(row, shape), jnp.broadcast_to(new_log, shape), 0.0)
    return jnp.sum(chosen, axis=0, keepdims=True)


def taylor_kernel(n_o, pack_ref, log_ref, kept_ref, first_ref, inside_ref, cross_ref, last_ref, own_ref, orb_ref, walk_ref, far_ref,
                  mine_ref, other_ref, weights_ref, op_ref, term_ref, sum_ref):
    z, x, o = lax.axis_index("vec"), lax.axis_index("walk"), lax.axis_index("orb")
    inner = routes(z)[0]
    n_both = log_ref.shape[0]
    n_walk = n_both // 2
    n_block = op_ref.shape[0] // LANE
    offsets = layout(n_block, n_both)
    i_at = lax.broadcasted_iota(jnp.int32, (LANE, LANE), 0)
    j_at = lax.broadcasted_iota(jnp.int32, (LANE, LANE), 1)

    def terms(offset, count):
        rows = pl.ds(offset, count)
        return (ref[rows, :] for ref in (kept_ref, first_ref, inside_ref, cross_ref, last_ref))

    def total(offset, count):
        kept, first, inside, cross, last = (value.astype(jnp.float32) for value in terms(offset, count))
        return (kept + last) + jnp.where(inner, inside + cross, first)

    def put(i, j, value):
        op_ref[pl.ds(i * LANE, LANE), pl.ds(j * LANE, LANE)] = value.astype(jnp.bfloat16)

    for i in range(n_block):
        for j in range(i + 1, n_block):
            value = total(offsets[(i, j)], LANE)
            put(i, j, value)
            put(j, i, value.T)
    for i in range(0, n_block, 2):
        merged = total(offsets[(i, i)], LANE)
        diagonal = total(offsets[(i + 1, i + 1)], 16)[:1]
        turned = merged.T
        put(i, i, jnp.where(i_at <= j_at, merged, turned))
        second = jnp.where(i_at > j_at, merged, turned)
        put(i + 1, i + 1, jnp.where(i_at == j_at, diagonal, second))

    copy_row = copies_of(pack_ref)
    here = lax.div(entry(copy_row, z * n_o + o), n_walk) == x
    rows = own_ref.shape[0]
    top, bottom = pl.ds(0, rows), pl.ds(rows, rows)
    term_ref[top, :] = jnp.where(here, own_ref[...], walk_ref[...])
    term_ref[bottom, :] = jnp.where(here, orb_ref[...], far_ref[...])
    sum_ref[...] = term_ref[...].astype(jnp.float32)
    for degree in range(1, ORDER + 1):
        halves = [mm(op_ref[half, :], term_ref[...]) for half in (top, bottom)]
        for half, product in zip((top, bottom), halves):
            term = (product * (1.0 / degree)).astype(jnp.bfloat16)
            sum_ref[half, :] += term.astype(jnp.float32)
            if degree < ORDER:
                term_ref[half, :] = term
    mine_ref[...] = sum_ref[top, :].astype(jnp.bfloat16)
    other_ref[...] = sum_ref[bottom, :].astype(jnp.bfloat16)

    kept, first, inside, cross, last = (joined(value) for value in terms(offsets["factor"], n_both))
    factor = (kept + jnp.where(inner, last, first)) + jnp.where(inner, inside + cross, last)
    weights_ref[...] = log_weights(copy_row, log_ref[...], factor, x)


def taylor(pack, log_column, arrived, candidates, n_o):
    rows, width = candidates[0].shape
    size = n_o * rows
    out = VMEM((rows, width), jnp.bfloat16)
    return pl.pallas_call(
        partial(taylor_kernel, n_o),
        out_shape=[out, out, VMEM((1, log_column.shape[0] // 2), jnp.float32)],
        in_specs=[in_vmem()] * (2 + len(arrived) + 4),
        out_specs=[in_vmem()] * 3,
        scratch_shapes=[
            VMEM((size, size), jnp.bfloat16),
            VMEM((size, width), jnp.bfloat16),
            VMEM((size, width), jnp.float32),
        ],
        compiler_params=pltpu.CompilerParams(vmem_limit_bytes=VMEM_LIMIT),
        name="taylor",
    )(*on_chip(pack, log_column, *arrived, *candidates))


def slot_copies(steps, n_o, pieces, out_ref, sems):
    z, o = lax.axis_index("vec"), lax.axis_index("orb")
    return [
        pltpu.make_async_copy(
            pieces[k],
            out_ref.at[jnp.bitwise_xor(z, dz) * n_o + jnp.bitwise_xor(o, flip)],
            sems.at[k],
        )
        for k, (dz, flip) in enumerate(steps)
    ]


def run_copies(copies):
    for copy in copies:
        copy.start()
    for copy in copies:
        copy.wait()


def early_place_kernel(steps, n_o, *refs):
    count = len(steps)
    weights_ref, out_ref, weights_out, sems = refs[count:]
    copies = slot_copies(steps, n_o, refs[:count], out_ref, sems)
    run_copies(copies + [pltpu.make_async_copy(weights_ref, weights_out, sems.at[count])])


def late_place_kernel(steps, n_o, *refs):
    count = len(steps)
    _, out_ref, sems = refs[count:]
    run_copies(slot_copies(steps, n_o, refs[:count], out_ref, sems))


def put_in_place(steps, pieces, late, weights, n_o):
    out = jax.ShapeDtypeStruct((len(pieces),) + pieces[0].shape, pieces[0].dtype)
    first = [k for k, step in enumerate(steps) if step not in late]
    last = [k for k, step in enumerate(steps) if step in late]
    limits = pltpu.CompilerParams(vmem_limit_bytes=VMEM_LIMIT)
    held, weights_out = pl.pallas_call(
        partial(early_place_kernel, [steps[k] for k in first], n_o),
        out_shape=[out, jax.ShapeDtypeStruct(weights.shape, weights.dtype)],
        in_specs=[in_vmem()] * (len(first) + 1),
        out_specs=[in_hbm()] * 2,
        scratch_shapes=[pltpu.SemaphoreType.DMA((len(first) + 1,))],
        compiler_params=limits,
        name="early_place",
    )(*on_chip(*[pieces[k] for k in first], weights))
    walkers_out = pl.pallas_call(
        partial(late_place_kernel, [steps[k] for k in last], n_o),
        out_shape=out,
        in_specs=[in_vmem()] * len(last) + [in_hbm()],
        out_specs=in_hbm(),
        scratch_shapes=[pltpu.SemaphoreType.DMA((len(last),))],
        input_output_aliases={len(last): 0},
        compiler_params=limits,
        name="late_place",
    )(*on_chip(*[pieces[k] for k in last]), held)
    return walkers_out, weights_out


def swapped(value, axes, sizes, masks):
    perm = []
    for a in range(sizes[0]):
        for b in range(sizes[1]):
            perm.append((a * sizes[1] + b, (a ^ masks[0]) * sizes[1] + (b ^ masks[1])))
    return lax.ppermute(value, axes, perm)


def slot_device(n_z, n_x, n_o, walkers, inv_intersection, trial, vectors, aux_field, log_weight, copy_list):
    line = partial(swapped, axes=("vec", "orb"), sizes=(n_z, n_o))
    near = partial(swapped, axes=("walk", "orb"), sizes=(n_x, n_o))

    others = ((0, 1), (1, 0), (1, 1))
    own_pack, here, quadrant = partial_bias_of(
        aux_field, log_weight, copy_list, walkers, inv_intersection, trial, vectors
    )
    orb_pack = near(own_pack, masks=(0, 1))
    own_pack = summed_pack(own_pack, orb_pack)
    walk_pack = near(own_pack, masks=(1, 0))
    packs = [own_pack, walk_pack]
    mate = near(quadrant, masks=(0, 1))
    piece, nearby, weights, split, log_column = first_pieces(packs, here, mate, n_o)
    came = line(piece, masks=(1, 0))
    inside = lax.ppermute(nearby, "vec", [(0, 0), (1, 2), (2, 1), (3, 3)])
    crossing, kept, *sources = other_pieces(
        own_pack, walk_pack, weights, split, here, mate, walkers, n_o
    )
    crossed = lax.ppermute(crossing, "vec", [(0, 2), (3, 1), (1, 0), (2, 3)])
    passed = combined(crossing, nearby, came, split.shape[0])
    last = lax.ppermute(passed, "vec", [(0, 1), (1, 3), (2, 0), (3, 2)])
    candidates = [sources[0]]
    for value, m in zip(sources[1:], others):
        candidates.append(near(value, masks=m))
    mine, other, slot_weights = taylor(
        own_pack, log_column, [kept, came, inside, crossed, last], candidates, n_o
    )
    steps = [(k, flip) for k in range(n_z) for flip in range(n_o)]
    landed = []
    for dz, flip in steps:
        half = mine if flip == 0 else other
        landed.append(half if (dz, flip) == (0, 0) else line(half, masks=(dz, flip)))
    walkers_out, weights_out = put_in_place(steps, landed, ((2, 0), (2, 1), (1, 0), (1, 1), (0, 1)), slot_weights, n_o)
    return walkers_out, weights_out[0]


def suits(mesh, walkers, trial, vectors):
    n_z, n_x, n_o = mesh.shape["vec"], mesh.shape["walk"], mesh.shape["orb"]
    per_device = walkers.shape[0] // (mesh.shape["grp"] * n_x)
    local_vectors = vectors.shape[0] // n_z
    return (
        n_o == 2
        and n_x == 2
        and n_z == 4
        and per_device == n_z * n_o
        and local_vectors == per_device
        and vectors.shape[1] == 4 * LANE
        and trial.shape[1] == LANE
    )


def solution(mesh):
    def step(walkers, inv_intersection, trial, vectors, aux_field, log_weight, copy_list):
        if suits(mesh, walkers, trial, vectors):
            body = partial(slot_device, mesh.shape["vec"], mesh.shape["walk"], mesh.shape["orb"])
        else:
            body = general_device
        return jax.shard_map(
            body,
            mesh=mesh,
            in_specs=(
                P(("grp", "walk"), "orb", None),
                P(("grp", "walk"), None, None),
                P(),
                P("vec", "orb", None),
                P(("grp", "walk"), "vec"),
                P(("grp", "walk")),
                P(("grp", "walk")),
            ),
            out_specs=(P(("grp", "walk"), "orb", None), P(("grp", "walk"))),
            check_vma=False,
        )(walkers, inv_intersection, trial, vectors, aux_field, log_weight, copy_list)

    return step
```
